32 devices in a mesh: ctx: 16 (over z, y, core), tp: 2 (over x).
Axes of the slice: x: 2, y: 2, z: 4, core: 2. Of those that a mesh axis runs over, the one named last changes fastest.
Arguments:
- tokens: bfloat16 [6144, 2048], P(('ctx', 'tp')), may hold values from -6 to 6
- attn_gain: float32 [2048], replicated, may hold values from 0.5 to 1.5
- ffn_gain: float32 [2048], replicated, may hold values from 0.5 to 1.5
- query_norm_gain: float32 [64], replicated, may hold values from 0.5 to 1.5
- k_gain: float32 [64], replicated, may hold values from 0.5 to 1.5
- w_query: bfloat16 [2048, 2048], P('ctx', 'tp'), may hold values from -0.125 to 0.125
- key_projection: bfloat16 [2048, 512], P('ctx', 'tp'), may hold values from -0.125 to 0.125
- value_projection: bfloat16 [2048, 512], P('ctx', 'tp'), may hold values from -0.125 to 0.125
- w_out: bfloat16 [2048, 2048], P('tp', 'ctx'), may hold values from -2 to 2
- w_gate: bfloat16 [2048, 8192], P('ctx', 'tp'), may hold values from -0.125 to 0.125
- w_up: bfloat16 [2048, 8192], P('ctx', 'tp'), may hold values from -0.125 to 0.125
- w_down: bfloat16 [8192, 2048], P('tp', 'ctx'), may hold values from -0.0625 to 0.0625
- doc_start: int32 [6144], P('ctx'), may hold values from 0 to 6143, as said below
- cotangent: bfloat16 [6144, 2048], P(('ctx', 'tp')), may hold values from -9 to 9
Outputs:
- out_tokens: bfloat16 [6144, 2048], P(('ctx', 'tp'))
- d_tokens: float32 [6144, 2048], P(('ctx', 'tp'))
- d_attn_gain: float32 [2048], replicated
- d_ffn_gain: float32 [2048], replicated
- d_q_gain: float32 [64], replicated
- d_k_gain: float32 [64], replicated
- d_query: float32 [2048, 2048], P('ctx', 'tp')
- d_key: float32 [2048, 512], P('ctx', 'tp')
- d_value: float32 [2048, 512], P('ctx', 'tp')
- d_out: float32 [2048, 2048], P('tp', 'ctx')
- d_gate: float32 [2048, 8192], P('ctx', 'tp')
- d_up: float32 [2048, 8192], P('ctx', 'tp')
- d_down: float32 [8192, 2048], P('tp', 'ctx')
The draws below stay inside these ranges and needn't reach their ends.
Inputs may be any that keep to these rules, and one draw needn't show every extreme that they name: `doc_start`: each token's value is the first position of its document; documents are runs of consecutive positions in order, of 144 to 2304 tokens (the last one may be cut shorter by the end), and one document holds exactly 2304 tokens.
All inputs are finite; a program needn't handle non-finite values.
Results may differ from the reference program's by a relative error of at most 0.022.
Values may be sent and summed in bfloat16 or wider, within the bound.
No kernel may reach another device: no remote copies, remote signals or barrier semaphores. Data moves between devices by JAX's collectives and lax.ppermute only.
A program may use at most 320 MiB of HBM per device.

```python
import jax
import jax.numpy as jnp
from jax import lax

MODEL_WIDTH = 2048
QUERY_HEADS = 32
KEY_VALUE_HEADS = 8
HEAD_WIDTH = 64
FF = 8192
CT = 384
WB = 6
DOC_MAX = 2304
TOKEN_COUNT = 6144
N_CTX = 16


def draw_doc_start(key, part):
    shortest = max(DOC_MAX // 16, 1)
    total_docs = TOKEN_COUNT // shortest + 2
    key_len, key_pick = jax.random.split(key)
    lengths = jax.random.randint(key_len, (total_docs,), shortest, DOC_MAX + 1)
    chosen = jax.random.randint(key_pick, (), 0, TOKEN_COUNT // DOC_MAX)
    lengths = jnp.where(jnp.arange(total_docs) == chosen, DOC_MAX, lengths)
    doc_ends = jnp.cumsum(lengths)
    begins = doc_ends - lengths
    owners = jnp.searchsorted(doc_ends, jnp.arange(TOKEN_COUNT), side='right')
    return begins[owners].astype(jnp.int32)


def draw_cotangent(key, part):
    positions = jnp.arange(TOKEN_COUNT, dtype=jnp.float32)
    ramp = 0.6 + 1.2 * positions / TOKEN_COUNT
    base = jnp.clip(jax.random.normal(key, (TOKEN_COUNT, MODEL_WIDTH), jnp.float32), -5.0, 5.0)
    return (base * ramp[:, None]).astype(jnp.bfloat16)


def block_levels(key, extent, cuts, smallest, top_value):
    gain = 1.0
    for axis_at, blocks in cuts:
        steps = jax.random.uniform(jax.random.fold_in(jax.random.fold_in(key, 6), axis_at), (blocks,), jnp.float32, smallest / len(cuts), top_value / len(cuts))
        gain = gain * jnp.repeat(jnp.exp(steps), extent[axis_at] // blocks).reshape((-1,) + (1,) * (len(extent) - 1 - axis_at))
    return gain


def normal_values(key, extent, deviation, bound, shards=(), held_as=jnp.bfloat16):
    entries = deviation * jax.random.normal(key, extent, jnp.float32)
    if shards:
        entries = entries * block_levels(key, extent, shards, -0.22, 0.18)
    return jnp.clip(entries, -bound, bound).astype(held_as)


def setup_inputs(seed: int = 0) -> dict:
    seeds = jax.random.split(jax.random.key(seed), 15)
    tokens = normal_values(seeds[0], (TOKEN_COUNT, MODEL_WIDTH), 1.0, 6.0, ((0, 32),))
    attn_gain = jnp.clip(1.0 + 0.1 * jax.random.normal(seeds[1], (MODEL_WIDTH,), jnp.float32), 0.5, 1.5)
    ffn_gain = jnp.clip(1.0 + 0.1 * jax.random.normal(seeds[2], (MODEL_WIDTH,), jnp.float32), 0.5, 1.5)
    query_norm_gain = jnp.clip(1.0 + 0.1 * jax.random.normal(seeds[3], (HEAD_WIDTH,), jnp.float32), 0.5, 1.5)
    k_gain = jnp.clip(1.0 + 0.1 * jax.random.normal(seeds[4], (HEAD_WIDTH,), jnp.float32), 0.5, 1.5)
    w_query = normal_values(seeds[5], (MODEL_WIDTH, QUERY_HEADS * HEAD_WIDTH), MODEL_WIDTH ** -0.5, 0.125, ((0, 16), (1, 2)))
    key_projection = normal_values(seeds[6], (MODEL_WIDTH, KEY_VALUE_HEADS * HEAD_WIDTH), MODEL_WIDTH ** -0.5, 0.125, ((0, 16), (1, 2)))
    value_projection = normal_values(seeds[7], (MODEL_WIDTH, KEY_VALUE_HEADS * HEAD_WIDTH), MODEL_WIDTH ** -0.5, 0.125, ((0, 16), (1, 2)))
    w_out = normal_values(seeds[8], (QUERY_HEADS * HEAD_WIDTH, MODEL_WIDTH), (max(QUERY_HEADS * HEAD_WIDTH // 256, 1)) ** -0.5, 2.0, ((0, 2), (1, 16)))
    w_gate = normal_values(seeds[9], (MODEL_WIDTH, FF), MODEL_WIDTH ** -0.5, 0.125, ((0, 16), (1, 2)))
    w_up = normal_values(seeds[10], (MODEL_WIDTH, FF), MODEL_WIDTH ** -0.5, 0.125, ((0, 16), (1, 2)))
    w_down = normal_values(seeds[11], (FF, MODEL_WIDTH), FF ** -0.5, 0.0625, ((0, 2), (1, 16)))
    doc_start = draw_doc_start(jax.random.fold_in(seeds[14], 71), 0)
    cotangent = draw_cotangent(jax.random.fold_in(seeds[14], 71), 0)
    return {"tokens": tokens, "attn_gain": attn_gain, "ffn_gain": ffn_gain, "query_norm_gain": query_norm_gain, "k_gain": k_gain, "w_query": w_query, "key_projection": key_projection, "value_projection": value_projection, "w_out": w_out, "w_gate": w_gate, "w_up": w_up, "w_down": w_down, "doc_start": doc_start, "cotangent": cotangent}


epsilon = 1e-05
rope_base = 1000000.0
neg_large = -1e+30

@jax.custom_vjp
def lowered_matmul(v):
    return lax.optimization_barrier(v.astype(jnp.bfloat16)).astype(jnp.float32)

@jax.custom_vjp
def lowered_backward(v):
    return v

def low_keep(v):
    return (lowered_matmul(v), None)

def low_pass(kept, grad):
    return (grad,)

def back_keep(v):
    return (v, None)

def back_low(kept, grad):
    return (lowered_matmul(grad),)
lowered_matmul.defvjp(low_keep, low_pass)
lowered_backward.defvjp(back_keep, back_low)

def rms_scale(values):
    return lax.rsqrt(lax.optimization_barrier(jnp.mean(values * values, axis=-1, keepdims=True)) + epsilon)

def feature_rms_norm(values, gain_vec):
    return values * rms_scale(values) * gain_vec

def rotary_embed_heads(values, cosine_table, sine_table):
    half_size = values.shape[-1] // 2
    first = values[..., :half_size]
    second = values[..., half_size:]
    return jnp.concatenate([first * cosine_table - second * sine_table, second * cosine_table + first * sine_table], axis=-1)

def rope_tables(relative, head_size):
    half_size = head_size // 2
    inv_freq = jnp.power(rope_base, -2.0 * jnp.arange(half_size, dtype=jnp.float32) / head_size)
    angles = relative.astype(jnp.float32)[:, None] * inv_freq[None, :]
    return (jnp.cos(angles), jnp.sin(angles))

def matrix_multiply(left, right):
    return jnp.dot(left, right, preferred_element_type=jnp.float32, precision=lax.Precision.HIGHEST)

def attend_blocks(query_rows, every_key_row, every_value_row, doc_start):
    padding_length = WB * CT
    span_len = (WB + 1) * CT
    key_padded = jnp.concatenate([jnp.zeros((padding_length, KEY_VALUE_HEADS, HEAD_WIDTH), every_key_row.dtype), every_key_row], axis=0)
    value_padded = jnp.concatenate([jnp.zeros((padding_length, KEY_VALUE_HEADS, HEAD_WIDTH), every_value_row.dtype), every_value_row], axis=0)
    scale_factor = HEAD_WIDTH ** (-0.5)

    def one_block(block_id):
        first_row = (block_id * CT).astype(jnp.int32)
        q_block = lax.dynamic_slice_in_dim(query_rows, first_row, CT, 0)
        k_block = lax.dynamic_slice_in_dim(key_padded, first_row, span_len, 0)
        v_block = lax.dynamic_slice_in_dim(value_padded, first_row, span_len, 0)
        starts = lax.dynamic_slice_in_dim(doc_start, first_row, CT, 0)
        q_pos = first_row + jnp.arange(CT, dtype=jnp.int32)
        k_pos = first_row - padding_length + jnp.arange(span_len, dtype=jnp.int32)
        allowed = (k_pos[None, :] >= starts[:, None]) & (k_pos[None, :] <= q_pos[:, None])
        raw_scores = jnp.einsum('qhgd,khd->qhgk', q_block, k_block, precision=lax.Precision.HIGHEST)
        scores = jnp.where(allowed[:, None, None, :], lowered_backward(raw_scores) * scale_factor, neg_large)
        probs = jax.nn.softmax(scores, axis=-1)
        return jnp.einsum('qhgk,khd->qhgd', lowered_matmul(probs), v_block, precision=lax.Precision.HIGHEST)
    blocks = lax.map(jax.checkpoint(one_block), jnp.arange(N_CTX, dtype=jnp.int32))
    return blocks.reshape(TOKEN_COUNT, QUERY_HEADS * HEAD_WIDTH)

def block_forward(x_in, attn_gain, ffn_gain, query_norm_gain, k_gain, w_query, key_projection, value_projection, w_out, w_gate, w_up, w_down, doc_start):
    first_operand = lowered_matmul(feature_rms_norm(x_in, attn_gain))
    query_unnormed = lowered_backward(matrix_multiply(first_operand, w_query)).reshape(TOKEN_COUNT, QUERY_HEADS, HEAD_WIDTH)
    key_unnormed = lowered_backward(matrix_multiply(first_operand, key_projection)).reshape(TOKEN_COUNT, KEY_VALUE_HEADS, HEAD_WIDTH)
    value_every_head = lowered_backward(lowered_matmul(matrix_multiply(first_operand, value_projection))).reshape(TOKEN_COUNT, KEY_VALUE_HEADS, HEAD_WIDTH)
    positions = jnp.arange(TOKEN_COUNT, dtype=jnp.int32)
    cosine_table, sine_table = rope_tables(positions - doc_start, HEAD_WIDTH)
    cosine_table = cosine_table[:, None, :]
    sine_table = sine_table[:, None, :]
    query_rows = lowered_matmul(rotary_embed_heads(feature_rms_norm(query_unnormed, query_norm_gain), cosine_table, sine_table)).reshape(TOKEN_COUNT, KEY_VALUE_HEADS, QUERY_HEADS // KEY_VALUE_HEADS, HEAD_WIDTH)
    every_key_row = lowered_matmul(rotary_embed_heads(feature_rms_norm(key_unnormed, k_gain), cosine_table, sine_table))
    attended = lowered_backward(lowered_matmul(attend_blocks(query_rows, every_key_row, value_every_head, doc_start)))
    resid = x_in + lowered_backward(matrix_multiply(attended, w_out))
    a_two = lowered_matmul(feature_rms_norm(resid, ffn_gain))
    gate = lowered_backward(matrix_multiply(a_two, w_gate))
    up_part = lowered_backward(matrix_multiply(a_two, w_up))
    hidden = lowered_matmul(jax.nn.silu(gate) * up_part)
    return resid + lowered_backward(matrix_multiply(hidden, w_down))

def reference(tokens, attn_gain, ffn_gain, query_norm_gain, k_gain, w_query, key_projection, value_projection, w_out, w_gate, w_up, w_down, doc_start, cotangent):

    def forward_of(x_in, gain_a, gain_f, gain_q, gain_k, mat_q, mat_k, mat_v, mat_o, mat_g, mat_u, mat_d):
        return block_forward(x_in, gain_a, gain_f, gain_q, gain_k, mat_q, mat_k, mat_v, mat_o, mat_g, mat_u, mat_d, doc_start)
    out_value, back_fn = jax.vjp(forward_of, tokens.astype(jnp.float32), attn_gain.astype(jnp.float32), ffn_gain.astype(jnp.float32), query_norm_gain.astype(jnp.float32), k_gain.astype(jnp.float32), w_query.astype(jnp.float32), key_projection.astype(jnp.float32), value_projection.astype(jnp.float32), w_out.astype(jnp.float32), w_gate.astype(jnp.float32), w_up.astype(jnp.float32), w_down.astype(jnp.float32))
    grads = back_fn(cotangent.astype(jnp.float32))
    return (out_value.astype(jnp.bfloat16), grads[0], grads[1], grads[2], grads[3], grads[4], grads[5], grads[6], grads[7], grads[8], grads[9], grads[10], grads[11])
```

```python
import functools
import math

import jax
import jax.numpy as jnp
from jax import lax
from jax.experimental import pallas as pl
from jax.experimental.pallas import tpu as pltpu
from jax.sharding import PartitionSpec as P

WB = 6
EPSILON = 1e-05
ROPE_BASE = 1000000.0
LOG2E = math.log2(math.e)

QUAD = 4
KEY_BLOCK = 256

F32 = jnp.float32
BF16 = jnp.bfloat16


def swap_ctx(value, bit):
    n = lax.axis_size("ctx")
    return lax.ppermute(value, "ctx", [(i, i ^ bit) for i in range(n)])


def swap_core(value):
    return swap_ctx(value, 1)


def swap_b(value):
    return swap_ctx(value, 2)


def swap_x(value):
    return lax.ppermute(value, "tp", [(0, 1), (1, 0)])


def line_move(value, by, sources):
    pairs = [(s * QUAD + q, (s + by) * QUAD + q) for s in sources for q in range(QUAD)]
    return lax.ppermute(value, "ctx", pairs)


def line_gather(own, line, n):
    up, down = [own], [own]
    for j in range(1, n):
        up.append(line_move(up[-1], 1, range(j - 1, n - 1)))
        down.append(line_move(down[-1], -1, range(1, n - j + 1)))
    slots = [own]
    for j in range(1, n):
        slots.append(jnp.where(line + j < n, down[j], up[n - j]))
    return slots


def add16(a, b):
    return (a.astype(F32) + b.astype(F32)).astype(BF16)


def line_scatter(slots, n):
    got_up = got_down = None
    for t in range(1, n):
        send_up, send_down = slots[n - t], slots[t]
        if got_up is not None:
            send_up, send_down = add16(send_up, got_up), add16(send_down, got_down)
        got_up = line_move(send_up, 1, range(0, t))
        got_down = line_move(send_down, -1, range(n - t, n))
    total = slots[0].astype(F32)
    if got_up is not None:
        total = total + got_up.astype(F32) + got_down.astype(F32)
    return total


def gather_rows(own):
    half = own.shape[0] // 2
    from_x, from_b = swap_x(own), swap_b(own)
    top, bottom = swap_x(from_b[:half]), swap_b(from_x[half:])
    near = [own, from_x, from_b, top, bottom]
    return jnp.concatenate(near + [swap_core(piece) for piece in near], axis=0)


def scatter_rows(near, far):
    r = near.shape[0] // 4
    half = r // 2

    def fold(block):
        rows = slice(block * r, (block + 1) * r)
        return add16(near[rows], swap_core(far[rows]))

    both, for_x, for_b, own = fold(3), fold(1), fold(2), fold(0)
    top, bottom = swap_x(both[:half]), swap_b(both[half:])
    x_top, b_bottom = swap_x(for_x[:half]), swap_b(for_b[half:])
    x_bottom = swap_x(add16(for_x[half:], bottom))
    b_top = swap_b(add16(for_b[:half], top))
    own = own.astype(F32)
    return jnp.concatenate(
        [
            own[:half] + x_top.astype(F32) + b_top.astype(F32),
            own[half:] + b_bottom.astype(F32) + x_bottom.astype(F32),
        ],
        axis=0,
    )


def spread(pieces):
    n = lax.axis_size("ctx")
    groups = [list(range(i, i + QUAD)) for i in range(0, n, QUAD)]
    return lax.all_to_all(pieces, "ctx", 0, 0, axis_index_groups=groups, tiled=True)


def sum_everywhere(value):
    bit = 1
    value = value + swap_x(value)
    while bit < lax.axis_size("ctx"):
        value = value + swap_ctx(value, bit)
        bit *= 2
    return value


def dot(a, b):
    return jnp.dot(a, b, preferred_element_type=F32)


def dot_nt(a, b):
    return lax.dot_general(a, b, (((1,), (1,)), ((), ())), preferred_element_type=F32)


def dot_tn(a, b):
    return lax.dot_general(a, b, (((0,), (0,)), ((), ())), preferred_element_type=F32)


def rms_scale(values):
    return lax.rsqrt(jnp.mean(values * values, axis=-1, keepdims=True) + EPSILON)


def norm_back(values, scale, gain, grad):
    unit = values * scale
    inner = grad * gain
    d_values = scale * (inner - unit * jnp.mean(inner * unit, axis=-1, keepdims=True))
    return d_values, jnp.sum(grad * unit, axis=0)


def swap_halves(u):
    h = u.shape[-1] // 2
    return jnp.concatenate([u[:, h:], u[:, :h]], axis=-1)


def prep_kernel(table, raw_ref, cos_ref, sin_ref, q_gain_ref, k_gain_ref, q_ref, kv_ref, *, heads, width):
    cos, sin = cos_ref[...], sin_ref[...]

    def ready(u, gain):
        u = u * rms_scale(u) * gain
        return (u * cos + swap_halves(u) * sin).astype(BF16)

    for h in range(heads):
        cols = slice(h * width, (h + 1) * width)
        q_ref[:, cols] = ready(raw_ref[:, cols], q_gain_ref[...])
    k0 = heads * width
    kv_ref[:, :width] = ready(raw_ref[:, k0 : k0 + width], k_gain_ref[...])
    kv_ref[:, width:] = raw_ref[:, k0 + width :].astype(BF16)


def prep_back_kernel(
    table, raw_ref, cos_ref, sin_ref, q_gain_ref, k_gain_ref, dq_ref, dkv_ref, out_ref, dg_ref, *, heads, width
):
    cos, sin = cos_ref[...], sin_ref[...]

    @pl.when(pl.program_id(0) == 0)
    def _():
        dg_ref[...] = jnp.zeros_like(dg_ref)

    def back(w, gain, grad):
        e = grad * cos - swap_halves(grad) * sin
        scale = rms_scale(w)
        unit = w * scale
        inner = e * gain
        dw = scale * (inner - unit * jnp.mean(inner * unit, axis=-1, keepdims=True))
        return dw.astype(BF16), jnp.sum(e * unit, axis=0, keepdims=True)

    total = jnp.zeros((1, width), F32)
    for h in range(heads):
        cols = slice(h * width, (h + 1) * width)
        dw, dg = back(raw_ref[:, cols], q_gain_ref[...], dq_ref[:, cols])
        out_ref[:, cols] = dw
        total = total + dg
    k0 = heads * width
    dw, dg = back(raw_ref[:, k0 : k0 + width], k_gain_ref[...], dkv_ref[:, :width])
    out_ref[:, k0 : k0 + width] = dw
    out_ref[:, k0 + width :] = dkv_ref[:, width:].astype(BF16)
    dg_ref[0:1, :] += total
    dg_ref[1:2, :] += dg


def stack_heads(block, heads, width):
    return jnp.concatenate([block[:, h * width : (h + 1) * width] for h in range(heads)], axis=0)


def attend_kernel(
    table, lo, hi, q_ref, start_ref, kv_ref, o_ref, of_ref, stat_ref, acc, total, *, heads, width, reach, bk
):
    t = pl.program_id(0)
    r = q_ref.shape[0]
    q = stack_heads(q_ref[...], heads, width)
    q = jnp.concatenate([q, jnp.zeros_like(q)], axis=-1)
    start = jnp.concatenate([start_ref[...]] * heads, axis=0)
    pos = reach + t * r + lax.broadcasted_iota(jnp.int32, (r, 1), 0)
    pos = jnp.concatenate([pos] * heads, axis=0)
    acc[...] = jnp.zeros_like(acc)
    total[...] = jnp.zeros_like(total)
    c = LOG2E / math.sqrt(width)

    def step(kb, carry):
        k0 = pl.multiple_of(kb * bk, bk)
        kv = kv_ref[pl.ds(k0, bk), :]
        s = dot_nt(q, kv)
        key = k0 + lax.broadcasted_iota(jnp.int32, (1, bk), 1)
        p = jnp.where((key >= start) & (key <= pos), jnp.exp2(s * c), 0.0)
        total[...] += jnp.sum(p, axis=-1, keepdims=True)
        acc[...] += dot(p.astype(BF16), kv)
        return carry

    lax.fori_loop(lo[t], hi[t], step, 0)
    o = acc[...][:, width:] / total[...]
    stat_ref[...] = jnp.log2(total[...])
    for h in range(heads):
        part = o[h * r : (h + 1) * r]
        of_ref[:, h * width : (h + 1) * width] = part
        o_ref[:, h * width : (h + 1) * width] = part.astype(BF16)


def attend_back_kernel(
    table, lo, hi, q_ref, do_ref, of_ref, stat_ref, start_ref, kv_ref, dq_ref, dkv_ref, acc, *, heads, width, reach, bk
):
    t = pl.program_id(0)
    r = q_ref.shape[0]

    @pl.when(t == 0)
    def _():
        dkv_ref[...] = jnp.zeros_like(dkv_ref)

    scale = 1.0 / math.sqrt(width)
    q = stack_heads(q_ref[...], heads, width)
    do = stack_heads(do_ref[...], heads, width)
    of = stack_heads(of_ref[...], heads, width)
    delta = jnp.sum(do.astype(F32) * of, axis=-1, keepdims=True)
    lane = lax.broadcasted_iota(jnp.int32, (heads * r, 2 * width), 1)
    rows = jnp.transpose(jnp.where(lane == 0, stat_ref[...], delta))
    stat, delta = rows[0:1, :], rows[1:2, :]
    q = jnp.concatenate([q, jnp.zeros_like(q)], axis=-1)
    q_scaled = (q.astype(F32) * scale).astype(BF16)
    do = jnp.concatenate([jnp.zeros_like(do), do], axis=-1)
    start = jnp.concatenate([start_ref[0]] * heads, axis=-1)
    pos = reach + t * r + lax.broadcasted_iota(jnp.int32, (1, r), 1)
    pos = jnp.concatenate([pos] * heads, axis=-1)
    acc[...] = jnp.zeros_like(acc)

    def step(kb, carry):
        k0 = pl.multiple_of(kb * bk, bk)
        kv = kv_ref[pl.ds(k0, bk), :]
        s = dot_nt(kv, q_scaled)
        dp = dot_nt(kv, do)
        key = k0 + lax.broadcasted_iota(jnp.int32, (bk, 1), 0)
        p = jnp.where((key >= start) & (key <= pos), jnp.exp2(s * LOG2E - stat), 0.0)
        ds = (p * (dp - delta)).astype(BF16)
        dkv_ref[pl.ds(k0, bk), :] += dot(ds, q_scaled) + dot(p.astype(BF16), do)
        acc[...] += dot_tn(ds, kv)
        return carry

    lax.fori_loop(lo[t], hi[t], step, 0)
    dq = acc[...][:, :width] * scale
    for h in range(heads):
        dq_ref[:, h * width : (h + 1) * width] = dq[h * r : (h + 1) * r]


def call(kernel, blocks, prefetch, ins, outs, scratch, args, flops, nbytes, transcendentals=0):
    return pl.pallas_call(
        kernel,
        out_shape=[jax.ShapeDtypeStruct(shape, dtype) for shape, dtype, _ in outs],
        grid_spec=pltpu.PrefetchScalarGridSpec(
            num_scalar_prefetch=prefetch,
            grid=(blocks,),
            in_specs=ins,
            out_specs=[spec for _, _, spec in outs],
            scratch_shapes=scratch,
        ),
        compiler_params=pltpu.CompilerParams(
            dimension_semantics=("arbitrary",), vmem_limit_bytes=48 * 1024 * 1024
        ),
        cost_estimate=pl.CostEstimate(
            flops=int(flops), bytes_accessed=int(nbytes), transcendentals=int(transcendentals)
        ),
    )(*args)


def on_device(
    tokens,
    attn_gain,
    ffn_gain,
    query_norm_gain,
    k_gain,
    w_query,
    key_projection,
    value_projection,
    w_out,
    w_gate,
    w_up,
    w_down,
    doc_start,
    cotangent,
):
    i, x = lax.axis_index("ctx"), lax.axis_index("tp")
    n = lax.axis_size("ctx") // QUAD
    line, b, core = i // QUAD, (i // 2) % 2, i % 2
    r, model = tokens.shape
    plane = 2 * QUAD * r
    width = query_norm_gain.shape[0]
    heads = w_query.shape[1] // QUAD // width
    qw = heads * width
    hidden = w_gate.shape[1] // QUAD
    step = model // n
    reach = WB * doc_start.shape[0]

    def rotated(v):
        return lax.dynamic_slice_in_dim(jnp.concatenate([v, v], axis=-1), line * step, model, v.ndim - 1)

    def unrotated(v):
        return lax.dynamic_slice_in_dim(jnp.concatenate([v, v], axis=-1), (n - line) * step, model, v.ndim - 1)

    def columns(j):
        return slice(j * step, (j + 1) * step)

    def by_quarter(w):
        return w.reshape(w.shape[0], QUAD, -1)

    qkv_shard = jnp.concatenate(
        [by_quarter(w_query), by_quarter(key_projection), by_quarter(value_projection)], axis=-1
    ).transpose(1, 0, 2)
    qkv_shard = spread(qkv_shard).reshape(step, -1)
    out_shard = spread(w_out.reshape(QUAD, qw, -1)).transpose(1, 0, 2).reshape(qw, step)
    gu_shard = jnp.concatenate([by_quarter(w_gate), by_quarter(w_up)], axis=-1).transpose(1, 0, 2)
    gu_shard = spread(gu_shard).reshape(step, -1)
    down_shard = spread(w_down.reshape(QUAD, hidden, -1)).transpose(1, 0, 2).reshape(hidden, step)
    w_qkv = jnp.concatenate(line_gather(qkv_shard, line, n), axis=0)
    w_o = jnp.concatenate(line_gather(out_shard, line, n), axis=1)
    w_gu = jnp.concatenate(line_gather(gu_shard, line, n), axis=0)
    w_d = jnp.concatenate(line_gather(down_shard, line, n), axis=1)

    near_core, near_b = swap_core(doc_start), swap_b(doc_start)
    far = swap_core(near_b)
    rows0 = [jnp.where(core == c, doc_start, near_core) for c in range(2)]
    rows1 = [jnp.where(core == c, near_b, far) for c in range(2)]
    starts = jnp.concatenate([jnp.where(b == y, rows0[c], rows1[c]) for y in range(2) for c in range(2)])
    first = line * plane
    relative = first + jnp.arange(plane, dtype=jnp.int32) - starts
    inv_freq = jnp.power(ROPE_BASE, -2.0 * jnp.arange(width // 2, dtype=F32) / width)
    angles = relative.astype(F32)[:, None] * inv_freq[None, :]
    cos, sin = jnp.cos(angles), jnp.sin(angles)
    cos = jnp.concatenate([cos, cos], axis=-1)
    sin = jnp.concatenate([-sin, sin], axis=-1)
    blocks = jnp.arange(2 * QUAD, dtype=jnp.int32)
    table = (
        ((((blocks >> 1) & 1) ^ core) << 2) | (((blocks >> 2) ^ b) << 1) | ((blocks & 1) ^ x)
    ).astype(jnp.int32)
    local_start = starts - (first - reach)
    lo = local_start[::r] // KEY_BLOCK
    hi = (reach + (blocks + 1) * r - 1) // KEY_BLOCK + 1
    nb = 2 * QUAD

    gain_1, gain_2 = rotated(attn_gain), rotated(ffn_gain)
    x_own = rotated(tokens).astype(F32)
    scale_1 = rms_scale(x_own)
    a_one = gather_rows((x_own * scale_1 * gain_1).astype(BF16))
    cot_own = rotated(cotangent)
    cot = gather_rows(cot_own)
    raw = dot(a_one, w_qkv)

    def here(cols):
        return pl.BlockSpec((r, cols), lambda t, *_: (t, 0))

    def moved(cols):
        return pl.BlockSpec((r, cols), lambda t, table, *_: (table[t], 0))

    def whole(shape):
        return pl.BlockSpec(shape, lambda t, *_: (0,) * len(shape))

    q_gain, key_gain = query_norm_gain[None, :], k_gain[None, :]
    q, kv = call(
        functools.partial(prep_kernel, heads=heads, width=width),
        nb,
        1,
        [moved(qw + 2 * width), here(width), here(width), whole((1, width)), whole((1, width))],
        [((plane, qw), BF16, here(qw)), ((plane, 2 * width), BF16, here(2 * width))],
        [],
        (table, raw, cos, sin, q_gain, key_gain),
        plane * (qw + width) * 10,
        plane * (qw + 2 * width) * 6,
    )
    spans = []
    left, distance = reach, 1
    while left > 0:
        spans.append((distance, min(left, plane)))
        left -= plane
        distance += 1
    halo = [line_move(kv[plane - rows :], d, range(0, max(n - d, 0))) for d, rows in spans]
    keys = jnp.concatenate(halo[::-1] + [kv], axis=0)
    nk = keys.shape[0]
    attn_flops = 2 * plane * heads * (plane // 2 + 2 * KEY_BLOCK) * width

    stacked = pl.BlockSpec((heads * r, 1), lambda t, *_: (t, 0))
    o, o_float, stat = call(
        functools.partial(attend_kernel, heads=heads, width=width, reach=reach, bk=KEY_BLOCK),
        nb,
        3,
        [here(qw), pl.BlockSpec((r, 1), lambda t, *_: (t, 0)), whole((nk, 2 * width))],
        [
            ((plane, qw), BF16, moved(qw)),
            ((plane, qw), F32, here(qw)),
            ((plane * heads, 1), F32, stacked),
        ],
        [pltpu.VMEM((heads * r, 2 * width), F32), pltpu.VMEM((heads * r, 1), F32)],
        (table, lo, hi, q, local_start[:, None], keys),
        8 * attn_flops,
        plane * qw * 8,
    )

    half = plane // 2
    attn_sum = scatter_rows(dot(o[:half], w_o).astype(BF16), dot(o[half:], w_o).astype(BF16))
    resid = x_own + attn_sum
    scale_2 = rms_scale(resid)
    a_two = gather_rows((resid * scale_2 * gain_2).astype(BF16))

    gate_up = dot(a_two, w_gu)
    gate, up = gate_up[:, :hidden], gate_up[:, hidden:]
    d_hid = dot_nt(cot, w_d)
    sig = jax.nn.sigmoid(gate)
    silu = gate * sig
    hid = (silu * up).astype(BF16)
    d_gate = (d_hid * up * sig * (1.0 + gate * (1.0 - sig))).astype(BF16)
    d_up = (d_hid * silu).astype(BF16)
    d_gu = jnp.concatenate([d_gate, d_up], axis=-1)
    d_two = scatter_rows(dot_nt(d_gu[:half], w_gu).astype(BF16), dot_nt(d_gu[half:], w_gu).astype(BF16))
    d_res, d_ffn_gain = norm_back(resid, scale_2, gain_2, d_two)
    d_h = cot_own.astype(F32) + d_res
    d_h_rows = gather_rows(d_h.astype(BF16))
    ffn_sum = scatter_rows(dot(hid[:half], w_d).astype(BF16), dot(hid[half:], w_d).astype(BF16))
    out_tokens = unrotated((resid + ffn_sum).astype(BF16))

    gu_grad = line_scatter([dot_tn(a_two[:, columns(j)], d_gu).astype(BF16) for j in range(n)], n)
    down_grad = line_scatter([dot_tn(hid, cot[:, columns(j)]).astype(BF16) for j in range(n)], n)

    d_o = dot_nt(d_h_rows, w_o).astype(BF16)
    dq, dkv = call(
        functools.partial(attend_back_kernel, heads=heads, width=width, reach=reach, bk=KEY_BLOCK),
        nb,
        3,
        [
            here(qw),
            moved(qw),
            here(qw),
            stacked,
            pl.BlockSpec((1, 1, r), lambda t, *_: (t, 0, 0)),
            whole((nk, 2 * width)),
        ],
        [((plane, qw), F32, here(qw)), ((nk, 2 * width), F32, whole((nk, 2 * width)))],
        [pltpu.VMEM((heads * r, 2 * width), F32)],
        (table, lo, hi, q, d_o, o_float, stat, local_start.reshape(nb, 1, r), keys),
        20 * attn_flops,
        plane * qw * 12,
    )
    dkv_own = dkv[nk - plane :]
    offset = nk - plane
    for d, rows in spans:
        back = line_move(dkv[offset - rows : offset].astype(BF16), -d, range(d, n)).astype(F32)
        offset -= rows
        dkv_own = dkv_own + jnp.concatenate([jnp.zeros((plane - rows, 2 * width), F32), back], axis=0)
    d_raw, d_head_gains = call(
        functools.partial(prep_back_kernel, heads=heads, width=width),
        nb,
        1,
        [
            moved(qw + 2 * width),
            here(width),
            here(width),
            whole((1, width)),
            whole((1, width)),
            here(qw),
            here(2 * width),
        ],
        [((plane, qw + 2 * width), BF16, moved(qw + 2 * width)), ((8, width), F32, whole((8, width)))],
        [],
        (table, raw, cos, sin, q_gain, key_gain, dq, dkv_own),
        plane * (qw + width) * 20,
        plane * (qw + 2 * width) * 10,
    )
    out_grad = line_scatter([dot_tn(o, d_h_rows[:, columns(j)]).astype(BF16) for j in range(n)], n)
    qkv_grad = line_scatter([dot_tn(a_one[:, columns(j)], d_raw).astype(BF16) for j in range(n)], n)
    d_one = scatter_rows(dot_nt(d_raw[:half], w_qkv).astype(BF16), dot_nt(d_raw[half:], w_qkv).astype(BF16))
    d_x, d_attn_gain = norm_back(x_own, scale_1, gain_1, d_one)
    d_tokens = unrotated(d_h + d_x)

    def columns_back(grad):
        return spread(grad.astype(BF16).reshape(QUAD, step // QUAD, -1)).transpose(1, 0, 2)

    def rows_back(grad):
        pieces = grad.astype(BF16).reshape(grad.shape[0], QUAD, -1).transpose(1, 0, 2)
        return spread(pieces).reshape(QUAD * grad.shape[0], -1).astype(F32)

    gu_back = columns_back(gu_grad)
    qkv_back = columns_back(qkv_grad)
    kk = step // QUAD

    def piece(v, start, size):
        return v[:, :, start : start + size].reshape(kk, -1).astype(F32)

    gains = sum_everywhere(
        jnp.concatenate([unrotated(d_attn_gain), unrotated(d_ffn_gain), d_head_gains[0], d_head_gains[1]])
    )
    return (
        out_tokens,
        d_tokens,
        gains[:model],
        gains[model : 2 * model],
        gains[2 * model : 2 * model + width],
        gains[2 * model + width :],
        piece(qkv_back, 0, qw),
        piece(qkv_back, qw, width),
        piece(qkv_back, qw + width, width),
        rows_back(out_grad),
        piece(gu_back, 0, hidden),
        piece(gu_back, hidden, hidden),
        rows_back(down_grad),
    )


def solution(mesh):
    return jax.shard_map(
        on_device,
        mesh=mesh,
        in_specs=(
            P(("ctx", "tp"), None),
            P(),
            P(),
            P(),
            P(),
            P("ctx", "tp"),
            P("ctx", "tp"),
            P("ctx", "tp"),
            P("tp", "ctx"),
            P("ctx", "tp"),
            P("ctx", "tp"),
            P("tp", "ctx"),
            P("ctx"),
            P(("ctx", "tp"), None),
        ),
        out_specs=(
            P(("ctx", "tp"), None),
            P(("ctx", "tp"), None),
            P(),
            P(),
            P(),
            P(),
            P("ctx", "tp"),
            P("ctx", "tp"),
            P("ctx", "tp"),
            P("tp", "ctx"),
            P("ctx", "tp"),
            P("ctx", "tp"),
            P("tp", "ctx"),
        ),
        check_vma=False,
    )
```

```python
import functools
import math

import jax
import jax.numpy as jnp
from jax import lax
from jax.experimental import pallas as pl
from jax.experimental.pallas import tpu as pltpu
from jax.sharding import PartitionSpec as P

WB = 6
EPSILON = 1e-05
ROPE_BASE = 1000000.0
LOG2E = math.log2(math.e)

QUAD = 4
KEY_BLOCK = 384

F32 = jnp.float32
BF16 = jnp.bfloat16


def swap_ctx(value, bit):
    n = lax.axis_size("ctx")
    return lax.ppermute(value, "ctx", [(i, i ^ bit) for i in range(n)])


def swap_core(value):
    return swap_ctx(value, 1)


def swap_b(value):
    return swap_ctx(value, 2)


def swap_x(value):
    return lax.ppermute(value, "tp", [(0, 1), (1, 0)])


def line_move(value, by, sources):
    pairs = [(s * QUAD + q, (s + by) * QUAD + q) for s in sources for q in range(QUAD)]
    return lax.ppermute(value, "ctx", pairs)


def line_groups(n):
    return [[p * QUAD + q for p in range(n)] for q in range(QUAD)]


def line_gather(own, n):
    return lax.all_gather(own, "ctx", axis=0, axis_index_groups=line_groups(n), tiled=True)


def line_scatter(partial, n):
    return lax.psum_scatter(partial, "ctx", scatter_dimension=0, axis_index_groups=line_groups(n), tiled=True)


def line_move(value, by, sources):
    pairs = [(s * QUAD + q, (s + by) * QUAD + q) for s in sources for q in range(QUAD)]
    return lax.ppermute(value, "ctx", pairs)


def tie(*values):
    return lax.optimization_barrier(values)


def add16(a, b):
    return (a.astype(F32) + b.astype(F32)).astype(BF16)


class Rows:
    def __init__(self, own):
        self.own, self.half = own, own.shape[0] // 2
        self.first = (swap_x(own), swap_b(own))

    def second(self):
        from_x, from_b = self.first
        self.last = (swap_x(from_b[: self.half]), swap_b(from_x[self.half :]))

    def third(self):
        near = [self.own, *self.first, *self.last]
        return jnp.concatenate(near + [swap_core(piece) for piece in near], axis=0)


def gather_rows(own, beside=None):
    rows = Rows(own)
    if beside is not None:
        rows.first, beside = tie(rows.first, beside)
    rows.second()
    return rows.third() if beside is None else (rows.third(), beside)


class Sums:
    def __init__(self, near, far):
        r = near.shape[0] // 4
        self.half = r // 2

        def fold(block):
            rows = slice(block * r, (block + 1) * r)
            return add16(near[rows], swap_core(far[rows]))

        self.parts = (fold(3), fold(1), fold(2), fold(0))

    def second(self):
        both, for_x, for_b, _ = self.parts
        half = self.half
        self.got = (swap_x(both[:half]), swap_b(both[half:]), swap_x(for_x[:half]), swap_b(for_b[half:]))

    def third(self):
        _, for_x, for_b, own = self.parts
        top, bottom, x_top, b_bottom = self.got
        half = self.half
        x_bottom = swap_x(add16(for_x[half:], bottom))
        b_top = swap_b(add16(for_b[:half], top))
        own = own.astype(F32)
        return jnp.concatenate(
            [
                own[:half] + x_top.astype(F32) + b_top.astype(F32),
                own[half:] + b_bottom.astype(F32) + x_bottom.astype(F32),
            ],
            axis=0,
        )


def scatter_rows(near, far, beside=None):
    sums = Sums(near, far)
    sums.second()
    if beside is not None:
        sums.got, beside = tie(sums.got, beside)
    return sums.third() if beside is None else (sums.third(), beside)


def spread(pieces):
    n = lax.axis_size("ctx")
    groups = [list(range(i, i + QUAD)) for i in range(0, n, QUAD)]
    return lax.all_to_all(pieces, "ctx", 0, 0, axis_index_groups=groups, tiled=True)


def sum_everywhere(value):
    bit = 1
    value = value + swap_x(value)
    while bit < lax.axis_size("ctx"):
        value = value + swap_ctx(value, bit)
        bit *= 2
    return value


def dot(a, b):
    return jnp.dot(a, b, preferred_element_type=F32)


def dot_nt(a, b):
    return lax.dot_general(a, b, (((1,), (1,)), ((), ())), preferred_element_type=F32)


def dot_tn(a, b):
    return lax.dot_general(a, b, (((0,), (0,)), ((), ())), preferred_element_type=F32)


def rms_scale(values):
    return lax.rsqrt(jnp.mean(values * values, axis=-1, keepdims=True) + EPSILON)


def norm_back(values, scale, gain, grad):
    unit = values * scale
    inner = grad * gain
    d_values = scale * (inner - unit * jnp.mean(inner * unit, axis=-1, keepdims=True))
    return d_values, jnp.sum(grad * unit, axis=0)


def swap_halves(u):
    h = u.shape[-1] // 2
    return jnp.concatenate([u[:, h:], u[:, :h]], axis=-1)


def prep_kernel(table, raw_ref, cos_ref, sin_ref, q_gain_ref, k_gain_ref, q_ref, kv_ref, *, heads, width):
    cos, sin = cos_ref[...], sin_ref[...]

    def ready(u, gain):
        u = u * rms_scale(u) * gain
        return (u * cos + swap_halves(u) * sin).astype(BF16)

    for h in range(heads):
        cols = slice(h * width, (h + 1) * width)
        q_ref[:, cols] = ready(raw_ref[:, cols], q_gain_ref[...])
    k0 = heads * width
    kv_ref[:, :width] = ready(raw_ref[:, k0 : k0 + width], k_gain_ref[...])
    kv_ref[:, width:] = raw_ref[:, k0 + width :].astype(BF16)


def prep_back_kernel(
    table, raw_ref, cos_ref, sin_ref, q_gain_ref, k_gain_ref, dq_ref, dkv_ref, out_ref, dg_ref, *, heads, width
):
    cos, sin = cos_ref[...], sin_ref[...]

    @pl.when(pl.program_id(0) == 0)
    def _():
        dg_ref[...] = jnp.zeros_like(dg_ref)

    def back(w, gain, grad):
        e = grad * cos - swap_halves(grad) * sin
        scale = rms_scale(w)
        unit = w * scale
        inner = e * gain
        dw = scale * (inner - unit * jnp.mean(inner * unit, axis=-1, keepdims=True))
        return dw.astype(BF16), jnp.sum(e * unit, axis=0, keepdims=True)

    total = jnp.zeros((1, width), F32)
    for h in range(heads):
        cols = slice(h * width, (h + 1) * width)
        dw, dg = back(raw_ref[:, cols], q_gain_ref[...], dq_ref[:, cols])
        out_ref[:, cols] = dw
        total = total + dg
    k0 = heads * width
    dw, dg = back(raw_ref[:, k0 : k0 + width], k_gain_ref[...], dkv_ref[:, :width])
    out_ref[:, k0 : k0 + width] = dw
    out_ref[:, k0 + width :] = dkv_ref[:, width:].astype(BF16)
    dg_ref[0:1, :] += total
    dg_ref[1:2, :] += dg


def stack_heads(block, heads, width):
    return jnp.concatenate([block[:, h * width : (h + 1) * width] for h in range(heads)], axis=0)


def attend_kernel(
    table, lo, hi, q_ref, start_ref, kv_ref, o_ref, of_ref, stat_ref, acc, ones_v, *, heads, width, reach, bk
):
    t = pl.program_id(0)
    r = q_ref.shape[0]

    @pl.when(t == 0)
    def _():
        lane = lax.broadcasted_iota(jnp.int32, kv_ref.shape, 1)
        ones_v[...] = jnp.where(lane < width, jnp.ones((), BF16), kv_ref[...])

    q = stack_heads(q_ref[...], heads, width)
    q = jnp.concatenate([q, jnp.zeros_like(q)], axis=-1)
    start = jnp.concatenate([start_ref[...]] * heads, axis=0)
    pos = reach + t * r + lax.broadcasted_iota(jnp.int32, (r, 1), 0)
    pos = jnp.concatenate([pos] * heads, axis=0)
    acc[...] = jnp.zeros_like(acc)
    c = LOG2E / math.sqrt(width)

    def step(kb, carry):
        k0 = pl.multiple_of(kb * bk, bk)
        s = dot_nt(q, kv_ref[pl.ds(k0, bk), :])
        key = k0 + lax.broadcasted_iota(jnp.int32, (1, bk), 1)
        p = jnp.where((key >= start) & (key <= pos), jnp.exp2(s * c), 0.0)
        acc[...] += dot(p.astype(BF16), ones_v[pl.ds(k0, bk), :])
        return carry

    lax.fori_loop(lo[t], hi[t], step, 0)
    total = acc[:, :1]
    o = acc[:, width:] / total
    stat_ref[...] = jnp.log2(total)
    for h in range(heads):
        part = o[h * r : (h + 1) * r]
        of_ref[:, h * width : (h + 1) * width] = part
        o_ref[:, h * width : (h + 1) * width] = part.astype(BF16)


def attend_back_kernel(
    table, lo, hi, q_ref, do_ref, of_ref, stat_ref, start_ref, kv_ref, dq_ref, dkv_ref, acc, *, heads, width, reach, bk
):
    t = pl.program_id(0)
    r = q_ref.shape[0]

    @pl.when(t == 0)
    def _():
        dkv_ref[...] = jnp.zeros_like(dkv_ref)

    scale = 1.0 / math.sqrt(width)
    q = stack_heads(q_ref[...], heads, width)
    do = stack_heads(do_ref[...], heads, width)
    of = stack_heads(of_ref[...], heads, width)
    delta = jnp.sum(do.astype(F32) * of, axis=-1, keepdims=True)
    lane = lax.broadcasted_iota(jnp.int32, (heads * r, 2 * width), 1)
    rows = jnp.transpose(jnp.where(lane == 0, stat_ref[...], delta))
    stat, delta = rows[0:1, :], rows[1:2, :]
    q = jnp.concatenate([q, jnp.zeros_like(q)], axis=-1)
    q_scaled = (q.astype(F32) * scale).astype(BF16)
    do = jnp.concatenate([jnp.zeros_like(do), do], axis=-1)
    start = jnp.concatenate([start_ref[0]] * heads, axis=-1)
    pos = reach + t * r + lax.broadcasted_iota(jnp.int32, (1, r), 1)
    pos = jnp.concatenate([pos] * heads, axis=-1)
    acc[...] = jnp.zeros_like(acc)

    def step(kb, carry):
        k0 = pl.multiple_of(kb * bk, bk)
        kv = kv_ref[pl.ds(k0, bk), :]
        s = dot_nt(kv, q_scaled)
        dp = dot_nt(kv, do)
        key = k0 + lax.broadcasted_iota(jnp.int32, (bk, 1), 0)
        p = jnp.where((key >= start) & (key <= pos), jnp.exp2(s * LOG2E - stat), 0.0)
        ds = (p * (dp - delta)).astype(BF16)
        dkv_ref[pl.ds(k0, bk), :] += dot(ds, q_scaled) + dot(p.astype(BF16), do)
        acc[...] += dot_tn(ds, kv)
        return carry

    lax.fori_loop(lo[t], hi[t], step, 0)
    dq = acc[...][:, :width] * scale
    for h in range(heads):
        dq_ref[:, h * width : (h + 1) * width] = dq[h * r : (h + 1) * r]


def feed_kernel(a_ref, c_ref, w_ref, *refs, hb, more):
    prev, (hid_ref, dgu_ref, near_ref, far_ref) = refs[:more], refs[more:]
    t = pl.program_id(0)
    half = pl.num_programs(0) // 2
    a, c = a_ref[...], c_ref[...]
    gate, up = dot(a, w_ref[:, :hb]), dot(a, w_ref[:, hb : 2 * hb])
    d_hid = dot(c, w_ref[:, 2 * hb :])
    sig = jax.nn.sigmoid(gate)
    silu = gate * sig
    hid_ref[...] = (silu * up).astype(BF16)
    dgu_ref[:, :hb] = (d_hid * up * (sig * (1.0 + gate * (1.0 - sig)))).astype(BF16)
    dgu_ref[:, hb:] = (d_hid * silu).astype(BF16)
    back = dot_nt(dgu_ref[...], w_ref[:, : 2 * hb])

    @pl.when(t < half)
    def _():
        near_ref[...] = (back + prev[0][...].astype(F32) if prev else back).astype(BF16)

    @pl.when(t >= half)
    def _():
        far_ref[...] = (back + prev[1][...].astype(F32) if prev else back).astype(BF16)


def feed_forward(a, c, w, prev, rows=256):
    total, model = a.shape
    hb = w.shape[1] // 3
    blocks = total // rows
    half = blocks // 2
    row = lambda cols: pl.BlockSpec((rows, cols), lambda t: (t, 0))
    near = pl.BlockSpec((rows, model), lambda t: (jnp.minimum(t, half - 1), 0))
    far = pl.BlockSpec((rows, model), lambda t: (jnp.maximum(t - half, 0), 0))
    whole = pl.BlockSpec((model, 3 * hb), lambda t: (0, 0), pipeline_mode=pl.Buffered(1))
    part = ((total // 2, model), BF16)
    return call(
        functools.partial(feed_kernel, hb=hb, more=len(prev)),
        blocks,
        0,
        [row(model), row(model), whole] + [near, far][: len(prev)],
        [((total, hb), BF16, row(hb)), ((total, 2 * hb), BF16, row(2 * hb)), (*part, near), (*part, far)],
        [],
        (a, c, w, *prev),
        10 * total * model * hb,
        2 * total * (3 * model + 3 * hb) + 6 * model * hb,
        total * hb,
    )


def pack_kernel(*refs, flip, widths):
    ins, outs = refs[: len(flip)], refs[len(flip) :]
    for quarter in range(QUAD):
        for o, out_ref in enumerate(outs):
            at = 0
            for ref, turned, width in zip(ins, flip, widths):
                part = width // len(outs)
                cut = slice(quarter * width + o * part, quarter * width + (o + 1) * part)
                out_ref[quarter, :, at : at + part] = jnp.transpose(ref[cut, :]) if turned else ref[:, cut]
                at += part


def whole_block(v):
    return pl.BlockSpec(v.shape, lambda t: (0,) * len(v.shape))


def packed(weights, flip, outs):
    rows = weights[0].shape[0]
    widths = [(w.shape[0] if f else w.shape[1]) // QUAD for w, f in zip(weights, flip)]
    shape = jax.ShapeDtypeStruct((QUAD, rows, sum(widths) // outs), BF16)
    return call(
        functools.partial(pack_kernel, flip=flip, widths=widths),
        1,
        0,
        [whole_block(w) for w in weights],
        [(shape.shape, BF16, whole_block(shape))] * outs,
        [],
        tuple(weights),
        1,
        4 * outs * math.prod(shape.shape),
    )


def weights_kernel(a_ref, b_ref, c_ref, d_ref, out_ref):
    cols = b_ref.shape[1]
    out_ref[:, :cols] = dot_tn(a_ref[...], b_ref[...]).astype(BF16)
    out_ref[:, cols:] = dot_tn(c_ref[...], d_ref[...]).astype(BF16)


def weight_grads(a, b, c, d, rows=512):
    total, model = a.shape
    cut = pl.BlockSpec((total, rows), lambda t: (0, t))

    def whole(v):
        return pl.BlockSpec(v.shape, lambda t: (0, 0), pipeline_mode=pl.Buffered(1))

    cols = b.shape[1] + d.shape[1]
    return call(
        weights_kernel,
        model // rows,
        0,
        [cut, whole(b), cut, whole(d)],
        [((model, cols), BF16, pl.BlockSpec((rows, cols), lambda t: (t, 0)))],
        [],
        (a, b, c, d),
        2 * total * model * cols,
        2 * (2 * total * model + (total + model) * cols),
    )[0]


def call(kernel, blocks, prefetch, ins, outs, scratch, args, flops, nbytes, transcendentals=0):
    return pl.pallas_call(
        kernel,
        out_shape=[jax.ShapeDtypeStruct(shape, dtype) for shape, dtype, _ in outs],
        grid_spec=pltpu.PrefetchScalarGridSpec(
            num_scalar_prefetch=prefetch,
            grid=(blocks,),
            in_specs=ins,
            out_specs=[spec for _, _, spec in outs],
            scratch_shapes=scratch,
        ),
        compiler_params=pltpu.CompilerParams(
            dimension_semantics=("arbitrary",), vmem_limit_bytes=48 * 1024 * 1024
        ),
        cost_estimate=pl.CostEstimate(
            flops=int(flops), bytes_accessed=int(nbytes), transcendentals=int(transcendentals)
        ),
    )(*args)


def on_device(
    tokens,
    attn_gain,
    ffn_gain,
    query_norm_gain,
    k_gain,
    w_query,
    key_projection,
    value_projection,
    w_out,
    w_gate,
    w_up,
    w_down,
    doc_start,
    cotangent,
):
    i, x = lax.axis_index("ctx"), lax.axis_index("tp")
    n = lax.axis_size("ctx") // QUAD
    line, b, core = i // QUAD, (i // 2) % 2, i % 2
    r, model = tokens.shape
    plane = 2 * QUAD * r
    width = query_norm_gain.shape[0]
    heads = w_query.shape[1] // QUAD // width
    qw = heads * width
    hidden = w_gate.shape[1] // QUAD
    step = model // n
    reach = WB * doc_start.shape[0]

    (sent,) = packed((w_query, key_projection, value_projection, w_out), (0, 0, 0, 1), 1)
    sent, tokens = tie(spread(sent), tokens)
    w_attn = line_gather(sent.reshape(step, -1), n)
    w_qkv, w_o = w_attn[:, : qw + 2 * width], w_attn[:, qw + 2 * width :]

    hid_block = hidden // 2
    sent, w_gate = tie(sent, w_gate)
    ffn_pieces = packed((w_gate, w_up, w_down), (0, 0, 1), 2)

    near_core, near_b = swap_core(doc_start), swap_b(doc_start)
    far = swap_core(near_b)
    rows0 = [jnp.where(core == c, doc_start, near_core) for c in range(2)]
    rows1 = [jnp.where(core == c, near_b, far) for c in range(2)]
    starts = jnp.concatenate([jnp.where(b == y, rows0[c], rows1[c]) for y in range(2) for c in range(2)])
    first = line * plane
    relative = first + jnp.arange(plane, dtype=jnp.int32) - starts
    inv_freq = jnp.power(ROPE_BASE, -2.0 * jnp.arange(width // 2, dtype=F32) / width)
    angles = relative.astype(F32)[:, None] * inv_freq[None, :]
    cos, sin = jnp.cos(angles), jnp.sin(angles)
    cos = jnp.concatenate([cos, cos], axis=-1)
    sin = jnp.concatenate([-sin, sin], axis=-1)
    blocks = jnp.arange(2 * QUAD, dtype=jnp.int32)
    table = (
        ((((blocks >> 1) & 1) ^ core) << 2) | (((blocks >> 2) ^ b) << 1) | ((blocks & 1) ^ x)
    ).astype(jnp.int32)
    local_start = starts - (first - reach)
    lo = local_start[::r] // KEY_BLOCK
    hi = (reach + (blocks + 1) * r - 1) // KEY_BLOCK + 1
    nb = 2 * QUAD

    gain_1, gain_2 = attn_gain, ffn_gain
    x_own = tokens.astype(F32)
    scale_1 = rms_scale(x_own)
    a_one, pieces_0 = tie(gather_rows((x_own * scale_1 * gain_1).astype(BF16)), ffn_pieces[0])
    sent_0, cot_own = tie(spread(pieces_0), cotangent)
    w_ffn_0 = line_gather(sent_0.reshape(step, -1), n)
    cot = Rows(cot_own)
    raw = dot(a_one, w_qkv)

    def here(cols):
        return pl.BlockSpec((r, cols), lambda t, *_: (t, 0))

    def moved(cols):
        return pl.BlockSpec((r, cols), lambda t, table, *_: (table[t], 0))

    def whole(shape):
        return pl.BlockSpec(shape, lambda t, *_: (0,) * len(shape))

    q_gain, key_gain = query_norm_gain[None, :], k_gain[None, :]
    q, kv = call(
        functools.partial(prep_kernel, heads=heads, width=width),
        nb,
        1,
        [moved(qw + 2 * width), here(width), here(width), whole((1, width)), whole((1, width))],
        [((plane, qw), BF16, here(qw)), ((plane, 2 * width), BF16, here(2 * width))],
        [],
        (table, raw, cos, sin, q_gain, key_gain),
        plane * (qw + width) * 10,
        plane * (qw + 2 * width) * 6,
    )
    spans = []
    left, distance = reach, 1
    while left > 0:
        spans.append((distance, min(left, plane)))
        left -= plane
        distance += 1
    halo = [line_move(kv[plane - rows :], d, range(0, max(n - d, 0))) for d, rows in spans]
    keys = jnp.concatenate(halo[::-1] + [kv], axis=0)
    keys, cot.first = tie(keys, cot.first)
    cot.second()
    q, pieces_1 = tie(q, ffn_pieces[1])
    nk = keys.shape[0]
    attn_flops = 2 * plane * heads * (plane // 2 + 2 * KEY_BLOCK) * width

    stacked = pl.BlockSpec((heads * r, 1), lambda t, *_: (t, 0))
    o, o_float, stat = call(
        functools.partial(attend_kernel, heads=heads, width=width, reach=reach, bk=KEY_BLOCK),
        nb,
        3,
        [here(qw), pl.BlockSpec((r, 1), lambda t, *_: (t, 0)), whole((nk, 2 * width))],
        [
            ((plane, qw), BF16, moved(qw)),
            ((plane, qw), F32, here(qw)),
            ((plane * heads, 1), F32, stacked),
        ],
        [pltpu.VMEM((heads * r, 2 * width), F32), pltpu.VMEM((nk, 2 * width), BF16)],
        (table, lo, hi, q, local_start[:, None], keys),
        8 * attn_flops,
        plane * qw * 8,
    )

    half = plane // 2
    o, sent_1 = tie(o, spread(pieces_1))
    w_ffn_1 = line_gather(sent_1.reshape(step, -1), n)
    keys, cot.last = tie(keys, cot.last)
    attn_sum, cot = scatter_rows(
        dot_nt(o[:half], w_o).astype(BF16), dot_nt(o[half:], w_o).astype(BF16), cot.third()
    )
    resid = x_own + attn_sum
    scale_2 = rms_scale(resid)
    a_two = gather_rows((resid * scale_2 * gain_2).astype(BF16))

    hid_0, d_gu_0, near, far = feed_forward(a_two, cot, w_ffn_0, ())
    ffn_grad_0 = weight_grads(a_two, d_gu_0, cot, hid_0)
    w_ffn_1, _ = tie(w_ffn_1, ffn_grad_0)
    ffn_grad_0 = line_scatter(ffn_grad_0, n)
    hid_1, d_gu_1, near, far = feed_forward(a_two, cot, w_ffn_1, (near, far))
    d_two, ffn_grad_1 = scatter_rows(near, far, weight_grads(a_two, d_gu_1, cot, hid_1))
    ffn_grad_1 = line_scatter(ffn_grad_1, n)
    d_res, d_ffn_gain = norm_back(resid, scale_2, gain_2, d_two)
    d_h = cotangent.astype(F32) + d_res

    def down_rows(cut):
        return (dot_nt(hid_0[cut], w_ffn_0[:, 2 * hid_block :]) + dot_nt(hid_1[cut], w_ffn_1[:, 2 * hid_block :])).astype(BF16)

    d_h_rows, down = gather_rows(
        d_h.astype(BF16), (down_rows(slice(0, half)), down_rows(slice(half, plane)))
    )
    ffn_sum = Sums(*down)

    def home(grad):
        return spread(grad.reshape(QUAD, step // QUAD, -1)).transpose(1, 0, 2)

    d_o = dot(d_h_rows, w_o).astype(BF16)
    d_o, ffn_sum.parts = tie(d_o, ffn_sum.parts)
    ffn_sum.second()
    dq, dkv = call(
        functools.partial(attend_back_kernel, heads=heads, width=width, reach=reach, bk=KEY_BLOCK),
        nb,
        3,
        [
            here(qw),
            moved(qw),
            here(qw),
            stacked,
            pl.BlockSpec((1, 1, r), lambda t, *_: (t, 0, 0)),
            whole((nk, 2 * width)),
        ],
        [((plane, qw), F32, here(qw)), ((nk, 2 * width), F32, whole((nk, 2 * width)))],
        [pltpu.VMEM((heads * r, 2 * width), F32)],
        (table, lo, hi, q, d_o, o_float, stat, local_start.reshape(nb, 1, r), keys),
        20 * attn_flops,
        plane * qw * 12,
    )
    dq, ffn_sum.got, ffn_grad_0 = tie(dq, ffn_sum.got, ffn_grad_0)
    back_0 = home(ffn_grad_0)
    out_tokens = (resid + ffn_sum.third()).astype(BF16)
    dkv_own = dkv[nk - plane :]
    offset = nk - plane
    for d, rows in spans:
        back = line_move(dkv[offset - rows : offset].astype(BF16), -d, range(d, n)).astype(F32)
        offset -= rows
        dkv_own = dkv_own + jnp.concatenate([jnp.zeros((plane - rows, 2 * width), F32), back], axis=0)
    d_raw, d_head_gains = call(
        functools.partial(prep_back_kernel, heads=heads, width=width),
        nb,
        1,
        [
            moved(qw + 2 * width),
            here(width),
            here(width),
            whole((1, width)),
            whole((1, width)),
            here(qw),
            here(2 * width),
        ],
        [((plane, qw + 2 * width), BF16, moved(qw + 2 * width)), ((8, width), F32, whole((8, width)))],
        [],
        (table, raw, cos, sin, q_gain, key_gain, dq, dkv_own),
        plane * (qw + width) * 20,
        plane * (qw + 2 * width) * 10,
    )
    attn_grad, ffn_grad_1 = tie(weight_grads(a_one, d_raw, d_h_rows, o), ffn_grad_1)
    attn_grad, back_0 = tie(attn_grad, back_0)
    attn_grad = line_scatter(attn_grad, n)
    back_1 = home(ffn_grad_1)
    attn_back = home(attn_grad)
    d_one, back_1 = scatter_rows(
        dot_nt(d_raw[:half], w_qkv).astype(BF16), dot_nt(d_raw[half:], w_qkv).astype(BF16), back_1
    )
    d_x, d_attn_gain = norm_back(x_own, scale_1, gain_1, d_one)
    d_tokens = d_h + d_x

    def piece(start, size):
        return attn_back[:, :, start : start + size].reshape(step // QUAD, -1).astype(F32)

    def joined(start):
        cols = [v[:, :, start : start + hid_block] for v in (back_0, back_1)]
        return jnp.concatenate(cols, axis=-1).reshape(step // QUAD, -1).astype(F32)

    gains = sum_everywhere(jnp.concatenate([d_attn_gain, d_ffn_gain, d_head_gains[0], d_head_gains[1]]))
    return (
        out_tokens,
        d_tokens,
        gains[:model],
        gains[model : 2 * model],
        gains[2 * model : 2 * model + width],
        gains[2 * model + width :],
        piece(0, qw),
        piece(qw, width),
        piece(qw + width, width),
        piece(qw + 2 * width, qw).T,
        joined(0),
        joined(hid_block),
        joined(2 * hid_block).T,
    )


def solution(mesh):
    return jax.shard_map(
        on_device,
        mesh=mesh,
        in_specs=(
            P(("ctx", "tp"), None),
            P(),
            P(),
            P(),
            P(),
            P("ctx", "tp"),
            P("ctx", "tp"),
            P("ctx", "tp"),
            P("tp", "ctx"),
            P("ctx", "tp"),
            P("ctx", "tp"),
            P("tp", "ctx"),
            P("ctx"),
            P(("ctx", "tp"), None),
        ),
        out_specs=(
            P(("ctx", "tp"), None),
            P(("ctx", "tp"), None),
            P(),
            P(),
            P(),
            P(),
            P("ctx", "tp"),
            P("ctx", "tp"),
            P("ctx", "tp"),
            P("tp", "ctx"),
            P("ctx", "tp"),
            P("ctx", "tp"),
            P("tp", "ctx"),
        ),
        check_vma=False,
    )
```

```python
import functools
import math

import jax
import jax.numpy as jnp
from jax import lax
from jax.experimental import pallas as pl
from jax.experimental.pallas import tpu as pltpu
from jax.sharding import PartitionSpec as P

WB = 6
EPSILON = 1e-05
ROPE_BASE = 1000000.0
LOG2E = math.log2(math.e)

QUAD = 4
KEY_BLOCK = 384
FIRST_BLOCK = 4

F32 = jnp.float32
BF16 = jnp.bfloat16


def swap_ctx(value, bit):
    n = lax.axis_size("ctx")
    return lax.ppermute(value, "ctx", [(i, i ^ bit) for i in range(n)])


def swap_core(value):
    return swap_ctx(value, 1)


def swap_b(value):
    return swap_ctx(value, 2)


def swap_x(value):
    return lax.ppermute(value, "tp", [(0, 1), (1, 0)])


def line_move(value, by, sources):
    pairs = [(s * QUAD + q, (s + by) * QUAD + q) for s in sources for q in range(QUAD)]
    return lax.ppermute(value, "ctx", pairs)


def line_groups(n):
    return [[p * QUAD + q for p in range(n)] for q in range(QUAD)]


def line_gather(own, n):
    return lax.all_gather(own, "ctx", axis=0, axis_index_groups=line_groups(n), tiled=True)


def line_scatter(partial, n):
    return lax.psum_scatter(partial, "ctx", scatter_dimension=0, axis_index_groups=line_groups(n), tiled=True)


def line_move(value, by, sources):
    pairs = [(s * QUAD + q, (s + by) * QUAD + q) for s in sources for q in range(QUAD)]
    return lax.ppermute(value, "ctx", pairs)


def tie(*values):
    return lax.optimization_barrier(values)


def add16(a, b):
    return (a.astype(F32) + b.astype(F32)).astype(BF16)


def swap_both(value):
    n = lax.axis_size("ctx")
    return lax.ppermute(value, ("ctx", "tp"), [(2 * i + x, 2 * (i ^ 2) + 1 - x) for i in range(n) for x in range(2)])


class Rows:
    def __init__(self, own):
        self.own, self.half = own, own.shape[0] // 2
        self.first = (swap_x(own), swap_b(own))

    def second(self):
        from_x, from_b = self.first
        self.last = (swap_x(from_b[: self.half]), swap_b(from_x[self.half :]))

    def third(self):
        near = [self.own, *self.first, *self.last]
        return near + [swap_core(piece) for piece in near]


def gather_rows(own, beside=None):
    rows = Rows(own)
    if beside is not None:
        rows.first, beside = tie(rows.first, beside)
    rows.second()
    return rows.third() if beside is None else (rows.third(), beside)


class Sums:
    def __init__(self, near, far):
        r = near.shape[0] // 4
        self.half = r // 2

        def fold(block):
            return add16(near[block * r : (block + 1) * r], swap_core(far[block]))

        self.parts = (fold(3), fold(1), fold(2), fold(0))

    def second(self):
        both, for_x, for_b, _ = self.parts
        half = self.half
        self.got = (swap_x(both[:half]), swap_b(both[half:]), swap_x(for_x[:half]), swap_b(for_b[half:]))

    def third(self):
        _, for_x, for_b, own = self.parts
        top, bottom, x_top, b_bottom = self.got
        half = self.half
        x_bottom = swap_x(add16(for_x[half:], bottom))
        b_top = swap_b(add16(for_b[:half], top))
        own = own.astype(F32)
        return jnp.concatenate(
            [
                own[:half] + x_top.astype(F32) + b_top.astype(F32),
                own[half:] + b_bottom.astype(F32) + x_bottom.astype(F32),
            ],
            axis=0,
        )


def scatter_rows(near, far, beside=None):
    sums = Sums(near, far)
    sums.second()
    if beside is not None:
        sums.got, beside = tie(sums.got, beside)
    return sums.third() if beside is None else (sums.third(), beside)


def blocks_of(rows):
    r = rows.shape[0] // 4
    return [rows[k * r : (k + 1) * r] for k in range(4)]


def spread(pieces, axis=0):
    n = lax.axis_size("ctx")
    groups = [list(range(i, i + QUAD)) for i in range(0, n, QUAD)]
    return lax.all_to_all(pieces, "ctx", axis, axis, axis_index_groups=groups, tiled=True)


def sum_over_ctx(value):
    bit = 1
    while bit < lax.axis_size("ctx"):
        value = value + swap_ctx(value, bit)
        bit *= 2
    return value


def dot(a, b):
    return jnp.dot(a, b, preferred_element_type=F32)


def dot_nt(a, b):
    return lax.dot_general(a, b, (((1,), (1,)), ((), ())), preferred_element_type=F32)


def dot_tn(a, b):
    return lax.dot_general(a, b, (((0,), (0,)), ((), ())), preferred_element_type=F32)


def rms_scale(values):
    return lax.rsqrt(jnp.mean(values * values, axis=-1, keepdims=True) + EPSILON)


def norm_back(values, scale, gain, grad):
    unit = values * scale
    inner = grad * gain
    d_values = scale * (inner - unit * jnp.mean(inner * unit, axis=-1, keepdims=True))
    return d_values, jnp.sum(grad * unit, axis=0)


def pick(refs, block, out_ref, at):
    r = refs[0].shape[0]
    for k in range(8):
        index = k // 4 * (len(refs) // 2) + k % 4

        @pl.when(block == k)
        def _():
            if k % 4 < 3 or len(refs) == 8:
                out_ref[at : at + r, :] = refs[index][...]
            else:
                out_ref[at : at + r // 2, :] = refs[index][...]
                out_ref[at + r // 2 : at + r, :] = refs[index + 1][...]


class Heads:
    def __init__(self, width, cos, sin):
        self.width, self.cos, self.sin = width, cos, sin
        lanes = 2 * width
        row = lax.broadcasted_iota(jnp.int32, (lanes, lanes), 0)
        col = lax.broadcasted_iota(jnp.int32, (lanes, lanes), 1)
        self.same = jnp.where(row // width == col // width, 1.0 / width, 0.0).astype(BF16)

    def mean(self, u):
        high = u.astype(BF16)
        low = (u - high.astype(F32)).astype(BF16)
        return dot(high, self.same) + dot(low, self.same)

    def swapped(self, u):
        half = self.width // 2
        lane = lax.broadcasted_iota(jnp.int32, u.shape, 1)
        return jnp.where((lane & half) == 0, pltpu.roll(u, 2 * self.width - half, 1), pltpu.roll(u, half, 1))

    def ready(self, u, gain):
        u = u * lax.rsqrt(self.mean(u * u) + EPSILON) * gain
        return u * self.cos + self.swapped(u) * self.sin

    def back(self, w, gain, grad):
        e = grad * self.cos - self.swapped(grad) * self.sin
        scale = lax.rsqrt(self.mean(w * w) + EPSILON)
        unit = w * scale
        inner = e * gain
        return scale * (inner - unit * self.mean(inner * unit)), jnp.sum(e * unit, axis=0, keepdims=True)


def project_kernel(table, *refs, heads, width):
    pieces, (w_ref, cos_ref, sin_ref, q_gain_ref, k_gain_ref, rows_ref, raw_ref, q_ref, kv_ref) = refs[:-9], refs[-9:]
    pick(pieces, pl.program_id(0), rows_ref, 0)
    raw = dot(rows_ref[...], w_ref[...])
    raw_ref[...] = raw
    math_of = Heads(width, cos_ref[...], sin_ref[...])
    lanes = 2 * width
    for c in range(heads // 2):
        cols = slice(c * lanes, (c + 1) * lanes)
        q_ref[:, cols] = math_of.ready(raw[:, cols], q_gain_ref[...]).astype(BF16)
    last = raw[:, heads * width :]
    lane = lax.broadcasted_iota(jnp.int32, last.shape, 1)
    kv_ref[...] = jnp.where(lane < width, math_of.ready(last, k_gain_ref[...]), last).astype(BF16)


def prep_back_kernel(
    table, raw_ref, cos_ref, sin_ref, q_gain_ref, k_gain_ref, dq_ref, dkv_ref, *refs, heads, width, plane
):
    halo, (out_ref, dg_ref) = refs[:-2], refs[-2:]
    t = pl.program_id(0)

    @pl.when(t == 0)
    def _():
        dg_ref[...] = jnp.zeros_like(dg_ref)

    math_of = Heads(width, cos_ref[...], sin_ref[...])
    lanes = 2 * width
    total = jnp.zeros((1, lanes), F32)
    for c in range(heads // 2):
        cols = slice(c * lanes, (c + 1) * lanes)
        dw, dg = math_of.back(raw_ref[:, cols], q_gain_ref[...], dq_ref[:, cols])
        out_ref[:, cols] = dw.astype(BF16)
        total = total + dg
    grad = dkv_ref[...]
    r = grad.shape[0]
    for ref in halo:
        missing = plane // r - ref.shape[0] // r
        at = pl.multiple_of(jnp.maximum(t - missing, 0) * r, r)
        grad = grad + jnp.where(t >= missing, ref[pl.ds(at, r), :].astype(F32), 0.0)
    dw, dg = math_of.back(raw_ref[:, heads * width :], k_gain_ref[...], grad)
    lane = lax.broadcasted_iota(jnp.int32, grad.shape, 1)
    out_ref[:, heads * width :] = jnp.where(lane < width, dw, grad).astype(BF16)
    dg_ref[0:1, :] += total
    dg_ref[1:2, :] += dg


def rows_dot_kernel(*refs):
    pieces, (w_ref, rows_ref, out_ref) = refs[:10], refs[10:]
    pick(pieces, pl.program_id(0), rows_ref, 0)
    out_ref[...] = dot(rows_ref[...], w_ref[...]).astype(BF16)


def stack_heads(block, heads, width):
    return jnp.concatenate([block[:, h * width : (h + 1) * width] for h in range(heads)], axis=0)


def attend_kernel(table, lo, hi, q_ref, start_ref, kv_ref, *refs, heads, width, base, bk, last):
    ones_v = refs[-1]
    if last:
        acc_in, o_ref, of_ref, stat_ref, acc = refs[:5]
    else:
        acc = refs[0]
    t = pl.program_id(0)
    r = q_ref.shape[0]

    @pl.when(t == 0)
    def _():
        lane = lax.broadcasted_iota(jnp.int32, kv_ref.shape, 1)
        ones_v[...] = jnp.where(lane < width, jnp.ones((), BF16), kv_ref[...])

    q = stack_heads(q_ref[...], heads, width)
    q = jnp.concatenate([q, jnp.zeros_like(q)], axis=-1)
    start = jnp.concatenate([start_ref[...]] * heads, axis=0)
    pos = base + t * r + lax.broadcasted_iota(jnp.int32, (r, 1), 0)
    pos = jnp.concatenate([pos] * heads, axis=0)
    acc[...] = acc_in[...] if last else jnp.zeros_like(acc)
    c = LOG2E / math.sqrt(width)

    def step(kb, carry):
        k0 = pl.multiple_of(kb * bk, bk)
        s = dot_nt(q, kv_ref[pl.ds(k0, bk), :])
        key = k0 + lax.broadcasted_iota(jnp.int32, (1, bk), 1)
        p = jnp.where((key >= start) & (key <= pos), jnp.exp2(s * c), 0.0)
        acc[...] += dot(p.astype(BF16), ones_v[pl.ds(k0, bk), :])
        return carry

    lax.fori_loop(lo[t], hi[t], step, 0)
    if last:
        total = acc[:, :1]
        o = acc[:, width:] / total
        stat_ref[...] = jnp.log2(total)
        for h in range(heads):
            part = o[h * r : (h + 1) * r]
            of_ref[:, h * width : (h + 1) * width] = part
            o_ref[:, h * width : (h + 1) * width] = part.astype(BF16)


def attend_back_kernel(
    table, lo, hi, q_ref, do_ref, of_ref, stat_ref, start_ref, kv_ref, *refs, heads, width, base, bk, last
):
    if last:
        acc_in, dq_ref, dkv, acc = refs
    else:
        acc, dkv_refs, dkv = refs[0], refs[1:-1], refs[-1]
    t = pl.program_id(0)
    r = q_ref.shape[0]

    @pl.when(t == 0)
    def _():
        dkv[...] = jnp.zeros_like(dkv)

    scale = 1.0 / math.sqrt(width)
    q = stack_heads(q_ref[...], heads, width)
    do = stack_heads(do_ref[...], heads, width)
    of = stack_heads(of_ref[...], heads, width)
    delta = jnp.sum(do.astype(F32) * of, axis=-1, keepdims=True)
    lane = lax.broadcasted_iota(jnp.int32, (heads * r, 2 * width), 1)
    rows = jnp.transpose(jnp.where(lane == 0, stat_ref[...], delta))
    stat, delta = rows[0:1, :], rows[1:2, :]
    q = jnp.concatenate([q, jnp.zeros_like(q)], axis=-1)
    q_scaled = (q.astype(F32) * scale).astype(BF16)
    do = jnp.concatenate([jnp.zeros_like(do), do], axis=-1)
    start = jnp.concatenate([start_ref[0]] * heads, axis=-1)
    pos = base + t * r + lax.broadcasted_iota(jnp.int32, (1, r), 1)
    pos = jnp.concatenate([pos] * heads, axis=-1)
    acc[...] = acc_in[...] if last else jnp.zeros_like(acc)

    def step(kb, carry):
        k0 = pl.multiple_of(kb * bk, bk)
        kv = kv_ref[pl.ds(k0, bk), :]
        s = dot_nt(kv, q_scaled)
        dp = dot_nt(kv, do)
        key = k0 + lax.broadcasted_iota(jnp.int32, (bk, 1), 0)
        p = jnp.where((key >= start) & (key <= pos), jnp.exp2(s * LOG2E - stat), 0.0)
        ds = (p * (dp - delta)).astype(BF16)
        dkv[pl.ds(k0, bk), :] += dot(ds, q_scaled) + dot(p.astype(BF16), do)
        acc[...] += dot_tn(ds, kv)
        return carry

    lax.fori_loop(lo[t], hi[t], step, 0)
    if last:
        dq = acc[...][:, :width] * scale
        for h in range(heads):
            dq_ref[:, h * width : (h + 1) * width] = dq[h * r : (h + 1) * r]
    else:

        @pl.when(t == pl.num_programs(0) - 1)
        def _():
            at = 0
            for ref in dkv_refs:
                ref[...] = dkv[at : at + ref.shape[0], :].astype(BF16)
                at += ref.shape[0]


def feed_first_kernel(*refs, hb):
    pieces, (c_ref, w_ref, hid_ref, dgu_ref, back_ref, rows_ref) = refs[:10], refs[10:]
    t = pl.program_id(0)
    r = pieces[0].shape[0]
    pick(pieces, 2 * t, rows_ref, 0)
    pick(pieces, 2 * t + 1, rows_ref, r)
    back_ref[...] = feed(rows_ref, c_ref, w_ref, hid_ref, dgu_ref, hb).astype(BF16)


def feed_last_kernel(a_ref, c_ref, w_ref, prev_ref, hid_ref, dgu_ref, near_ref, *far_refs, hb):
    t = pl.program_id(0)
    back = feed(a_ref, c_ref, w_ref, hid_ref, dgu_ref, hb) + prev_ref[...].astype(F32)
    split_store(back, t, near_ref, far_refs)


def feed(a_ref, c_ref, w_ref, hid_ref, dgu_ref, hb):
    a, c = a_ref[...], c_ref[...]
    gate, up = dot(a, w_ref[:, :hb]), dot(a, w_ref[:, hb : 2 * hb])
    d_hid = dot(c, w_ref[:, 2 * hb :])
    sig = jax.nn.sigmoid(gate)
    silu = gate * sig
    hid_ref[...] = (silu * up).astype(BF16)
    dgu_ref[:, :hb] = (d_hid * up * (sig * (1.0 + gate * (1.0 - sig)))).astype(BF16)
    dgu_ref[:, hb:] = (d_hid * silu).astype(BF16)
    return dot_nt(dgu_ref[...], w_ref[:, : 2 * hb])


def down_kernel(h0_ref, h1_ref, w0_ref, w1_ref, near_ref, *far_refs):
    t = pl.program_id(0)
    y = sum(dot_nt(h[...], w[:, 2 * h.shape[1] :]) for h, w in ((h0_ref, w0_ref), (h1_ref, w1_ref)))
    split_store(y, t, near_ref, far_refs)


def split_store(value, t, near_ref, far_refs):
    r = far_refs[0].shape[0]

    @pl.when(t < 2)
    def _():
        near_ref[...] = value.astype(BF16)

    for k, ref in enumerate(far_refs):

        @pl.when(t == 2 + k // 2)
        def _():
            ref[...] = value[k % 2 * r : (k % 2 + 1) * r].astype(BF16)


def split_outs(total, model):
    far = pl.BlockSpec((total // 8, model), lambda t: (0, 0))
    near = pl.BlockSpec((total // 4, model), lambda t: (jnp.minimum(t, 1), 0))
    return [((total // 2, model), BF16, near)] + [((total // 8, model), BF16, far)] * 4


def split_dot_kernel(a_ref, w_ref, near_ref, *far_refs):
    split_store(dot_nt(a_ref[...], w_ref[...]), pl.program_id(0), near_ref, far_refs)


def split_dot(a, w):
    total, cols = a.shape
    model = w.shape[0]
    near, *far = call(
        split_dot_kernel,
        4,
        0,
        [pl.BlockSpec((total // 4, cols), lambda t: (t, 0)), whole_block(w)],
        split_outs(total, model),
        [],
        (a, w),
        2 * total * model * cols,
        2 * total * (model + cols),
    )
    return near, far


def down_rows(h0, h1, w0, w1):
    total, hb = h0.shape[0], (h0.shape[1] + h1.shape[1]) // 2
    model = w0.shape[0]

    def row(h):
        return pl.BlockSpec((total // 4, h.shape[1]), lambda t: (t, 0))

    near, *far = call(
        down_kernel,
        4,
        0,
        [row(h0), row(h1), whole_block(w0), whole_block(w1)],
        split_outs(total, model),
        [],
        (h0, h1, w0, w1),
        4 * total * model * hb,
        2 * total * (model + 2 * hb) + 12 * model * hb,
    )
    return near, far


def whole_block(v):
    return pl.BlockSpec(v.shape, lambda t, *_: (0,) * len(v.shape), pipeline_mode=pl.Buffered(1))


def feed_forward(a, c, w, prev=None):
    total, model = c.shape
    rows = total // 4
    hb = w.shape[1] // 3

    def row(cols):
        return pl.BlockSpec((rows, cols), lambda t: (t, 0))

    outs = [((total, hb), BF16, row(hb)), ((total, 2 * hb), BF16, row(2 * hb))]
    if prev is None:
        kernel, args = feed_first_kernel, (*a, c, w)
        ins = [whole_block(piece) for piece in a] + [row(model), whole_block(w)]
        outs += [((total, model), BF16, row(model))] * 2
    else:
        kernel, args = feed_last_kernel, (a, c, w, prev)
        ins = [row(model), row(model), whole_block(w), row(model)]
        outs += split_outs(total, model)
    return call(
        functools.partial(kernel, hb=hb),
        4,
        0,
        ins,
        outs,
        [],
        args,
        12 * total * model * hb,
        2 * total * (4 * model + 3 * hb) + 6 * model * hb,
        total * hb,
    )


def pack_kernel(*refs, flip, widths, cuts):
    ins, outs = refs[: len(flip)], refs[len(flip) :]
    for quarter in range(QUAD):
        for out_ref, (low, high) in zip(outs, cuts):
            at = 0
            for ref, turned, width in zip(ins, flip, widths):
                start, end = low * width // high[1], high[0] * width // high[1]
                cut = slice(quarter * width + start, quarter * width + end)
                out_ref[quarter, :, at : at + end - start] = jnp.transpose(ref[cut, :]) if turned else ref[:, cut]
                at += end - start


def packed(weights, flip, cuts):
    rows = weights[0].shape[flip[0]]
    widths = [(w.shape[0] if f else w.shape[1]) // QUAD for w, f in zip(weights, flip)]
    shapes = [
        jax.ShapeDtypeStruct((QUAD, rows, sum((high - low) * w // of for w in widths)), BF16)
        for low, (high, of) in cuts
    ]
    return call(
        functools.partial(pack_kernel, flip=flip, widths=widths, cuts=cuts),
        1,
        0,
        [whole_block(w) for w in weights],
        [(shape.shape, BF16, whole_block(shape)) for shape in shapes],
        [],
        tuple(weights),
        1,
        sum(4 * math.prod(shape.shape) for shape in shapes),
    )


def weights_kernel(a_ref, b_ref, c_ref, d_ref, *refs):
    out_ref = refs[-1]
    cols = b_ref.shape[1]
    first = dot_tn(a_ref[...], b_ref[...])
    out_ref[:, :cols] = first.astype(BF16)
    out_ref[:, cols:] = dot_tn(c_ref[...], d_ref[...]).astype(BF16)
    if len(refs) > 1:
        w_ref, sums_ref = refs[:2]
        sums_ref[...] = jnp.sum(first * w_ref[...].astype(F32), axis=1, keepdims=True)


def weight_grads(a, b, c, d, w=None, rows=512):
    total, model = a.shape
    cut = pl.BlockSpec((total, rows), lambda t: (0, t))

    def whole(v):
        return pl.BlockSpec(v.shape, lambda t: (0, 0), pipeline_mode=pl.Buffered(1))

    def tall(cols):
        return pl.BlockSpec((rows, cols), lambda t: (t, 0))

    cols = b.shape[1] + d.shape[1]
    more = [] if w is None else [w]
    return call(
        weights_kernel,
        model // rows,
        0,
        [cut, whole(b), cut, whole(d)] + [tall(v.shape[1]) for v in more],
        [((model, 1), F32, tall(1))] * len(more) + [((model, cols), BF16, tall(cols))],
        [],
        (a, b, c, d, *more),
        2 * total * model * cols,
        2 * (2 * total * model + (total + model) * cols),
    )


def call(kernel, blocks, prefetch, ins, outs, scratch, args, flops, nbytes, transcendentals=0):
    return pl.pallas_call(
        kernel,
        out_shape=[jax.ShapeDtypeStruct(shape, dtype) for shape, dtype, _ in outs],
        grid_spec=pltpu.PrefetchScalarGridSpec(
            num_scalar_prefetch=prefetch,
            grid=(blocks,),
            in_specs=ins,
            out_specs=[spec for _, _, spec in outs],
            scratch_shapes=scratch,
        ),
        compiler_params=pltpu.CompilerParams(
            dimension_semantics=("arbitrary",), vmem_limit_bytes=56 * 1024 * 1024
        ),
        cost_estimate=pl.CostEstimate(
            flops=int(flops), bytes_accessed=int(nbytes), transcendentals=int(transcendentals)
        ),
    )(*args)


def on_device(
    tokens,
    attn_gain,
    ffn_gain,
    query_norm_gain,
    k_gain,
    w_query,
    key_projection,
    value_projection,
    w_out,
    w_gate,
    w_up,
    w_down,
    doc_start,
    cotangent,
):
    i, x = lax.axis_index("ctx"), lax.axis_index("tp")
    n = lax.axis_size("ctx") // QUAD
    line, b, core = i // QUAD, (i // 2) % 2, i % 2
    r, model = tokens.shape
    plane = 2 * QUAD * r
    width = query_norm_gain.shape[0]
    heads = w_query.shape[1] // QUAD // width
    qw = heads * width
    hidden = w_gate.shape[1] // QUAD
    step = model // n
    reach = WB * doc_start.shape[0]

    (sent,) = packed((w_query, key_projection, value_projection, w_out), (0, 0, 0, 1), [(0, (1, 1))])
    sent, tokens = tie(spread(sent), tokens)
    w_attn = line_gather(sent.reshape(step, -1), n)
    w_qkv, w_o = w_attn[:, : qw + 2 * width], w_attn[:, qw + 2 * width :]
    x_own = tokens.astype(F32)
    scale_1 = rms_scale(x_own)

    cut = FIRST_BLOCK
    ffn_pieces = packed((w_gate, w_up, w_down), (0, 0, 1), [(0, (cut, 8)), (cut, (8, 8))])
    a_own = (x_own * scale_1 * attn_gain).astype(BF16)
    a_near = (swap_x(a_own), swap_b(a_own), swap_both(a_own))

    near_core, near_b = swap_core(doc_start), swap_b(doc_start)
    far = swap_core(near_b)
    rows0 = [jnp.where(core == c, doc_start, near_core) for c in range(2)]
    rows1 = [jnp.where(core == c, near_b, far) for c in range(2)]
    starts = jnp.concatenate([jnp.where(b == y, rows0[c], rows1[c]) for y in range(2) for c in range(2)])
    first = line * plane
    relative = first + jnp.arange(plane, dtype=jnp.int32) - starts
    inv_freq = jnp.power(ROPE_BASE, -2.0 * jnp.arange(width // 2, dtype=F32) / width)
    angles = relative.astype(F32)[:, None] * inv_freq[None, :]
    cos, sin = jnp.cos(angles), jnp.sin(angles)
    cos = jnp.concatenate([cos] * 4, axis=-1)
    sin = jnp.concatenate([-sin, sin] * 2, axis=-1)
    sent_0 = spread(ffn_pieces[0])
    w_ffn_0 = line_gather(sent_0.reshape(step, -1), n)
    a_near, cos, sin, pieces_1, _ = tie(a_near, cos, sin, ffn_pieces[1], sent_0)
    sent_1 = spread(pieces_1)
    a_pieces = [a_own, *a_near]
    a_pieces = a_pieces + [swap_core(piece) for piece in a_pieces]

    blocks = jnp.arange(2 * QUAD, dtype=jnp.int32)
    table = (
        ((((blocks >> 1) & 1) ^ core) << 2) | (((blocks >> 2) ^ b) << 1) | ((blocks & 1) ^ x)
    ).astype(jnp.int32)
    inverse = (
        ((((blocks >> 1) & 1) ^ b) << 2) | (((blocks >> 2) ^ core) << 1) | ((blocks & 1) ^ x)
    ).astype(jnp.int32)
    nb = 2 * QUAD

    def key_range(base, keys):
        local = starts - (first - base)
        low = jnp.clip(local[::r] // KEY_BLOCK, 0, keys // KEY_BLOCK)
        high = jnp.clip((base + (blocks + 1) * r - 1) // KEY_BLOCK + 1, low, keys // KEY_BLOCK)
        return local, low, high

    own_part, halo_part = key_range(0, plane), key_range(reach, reach)

    gain_1, gain_2 = attn_gain, ffn_gain

    def here(cols):
        return pl.BlockSpec((r, cols), lambda t, *_: (t, 0))

    def moved(cols):
        return pl.BlockSpec((r, cols), lambda t, table, *_: (table[t], 0))

    lanes = 2 * width
    two = lambda gain: jnp.concatenate([gain, gain])[None, :]
    q_gain, key_gain = two(query_norm_gain), two(k_gain)
    a_one, raw, q, kv = call(
        functools.partial(project_kernel, heads=heads, width=width),
        nb,
        1,
        [whole_block(piece) for piece in a_pieces]
        + [whole_block(w_qkv), moved(lanes), moved(lanes), whole_block(q_gain), whole_block(key_gain)],
        [
            ((plane, model), BF16, here(model)),
            ((plane, qw + lanes), F32, here(qw + lanes)),
            ((plane, qw), BF16, moved(qw)),
            ((plane, lanes), BF16, moved(lanes)),
        ],
        [],
        (inverse, *a_pieces, w_qkv, cos, sin, q_gain, key_gain),
        2 * plane * model * (qw + lanes),
        plane * (4 * model + 10 * qw),
    )
    q, kv, sent_1, cot_own = tie(q, kv, sent_1, cotangent)
    w_ffn_1 = line_gather(sent_1.reshape(step, -1), n)
    spans = []
    left, distance = reach, 1
    while left > 0:
        spans.append((distance, min(left, plane)))
        left -= plane
        distance += 1
    halo = [line_move(kv[plane - rows :], d, range(0, max(n - d, 0))) for d, rows in spans]
    attn_flops = plane * heads * (plane // 2 + 2 * KEY_BLOCK) * width
    stacked = pl.BlockSpec((heads * r, 1), lambda t, *_: (t, 0))
    sums = ((plane * heads, lanes), F32, pl.BlockSpec((heads * r, lanes), lambda t, *_: (t, 0)))

    def attend(part, base, keys, *acc):
        local, low, high = part
        outs = [((plane, qw), BF16, moved(qw)), ((plane, qw), F32, here(qw)), ((plane * heads, 1), F32, stacked)]
        return call(
            functools.partial(attend_kernel, heads=heads, width=width, base=base, bk=KEY_BLOCK, last=len(acc)),
            nb,
            3,
            [here(qw), pl.BlockSpec((r, 1), lambda t, *_: (t, 0)), whole_block(keys)] + [sums[2]] * len(acc),
            outs if acc else [sums],
            [pltpu.VMEM((heads * r, lanes), F32)] * len(acc) + [pltpu.VMEM(keys.shape, BF16)],
            (table, low, high, q, local[:, None], keys, *acc),
            8 * attn_flops,
            plane * qw * 10,
        )

    (acc,) = attend(own_part, 0, kv)
    cot = Rows(cot_own)
    acc, halo, cot.first = tie(acc, halo, cot.first)
    cot.second()
    halo_keys = jnp.concatenate(halo[::-1], axis=0)
    o, o_float, stat = attend(halo_part, reach, halo_keys, acc)

    half = plane // 2
    o, cot.last = tie(o, cot.last)

    attn_sum, cot = scatter_rows(*split_dot(o, w_o), jnp.concatenate(cot.third(), axis=0))
    resid = x_own + attn_sum
    scale_2 = rms_scale(resid)
    a_pieces = gather_rows((resid * scale_2 * gain_2).astype(BF16))

    hid_0, d_gu_0, back, a_two = feed_forward(a_pieces, cot, w_ffn_0)
    (ffn_grad_0,) = weight_grads(a_two, d_gu_0, cot, hid_0)
    w_ffn_1, _ = tie(w_ffn_1, ffn_grad_0)
    ffn_grad_0 = line_scatter(ffn_grad_0, n)
    hid_1, d_gu_1, near, *far = feed_forward(a_two, cot, w_ffn_1, back)
    d_two, ffn_grad_1 = scatter_rows(near, far, weight_grads(a_two, d_gu_1, cot, hid_1)[0])
    ffn_grad_1 = line_scatter(ffn_grad_1, n)
    d_res, d_ffn_gain = norm_back(resid, scale_2, gain_2, d_two)
    d_h = cotangent.astype(F32) + d_res

    h_pieces, down = gather_rows(d_h.astype(BF16), down_rows(hid_0, hid_1, w_ffn_0, w_ffn_1))
    ffn_sum = Sums(*down)

    def home(grad):
        return spread(grad.reshape(QUAD, step // QUAD, -1)).transpose(1, 0, 2)

    d_h_rows, d_o = call(
        rows_dot_kernel,
        nb,
        0,
        [whole_block(piece) for piece in h_pieces] + [whole_block(w_o)],
        [((plane, model), BF16, here(model)), ((plane, qw), BF16, here(qw))],
        [],
        (*h_pieces, w_o),
        2 * plane * model * qw,
        4 * plane * model,
    )
    d_o, ffn_sum.parts = tie(d_o, ffn_sum.parts)
    ffn_sum.second()

    def attend_back(part, base, keys, *acc):
        local, low, high = part
        if acc:
            outs = [((plane, qw), F32, here(qw)), (keys.shape, F32, pl.BlockSpec(keys.shape, lambda t, *_: (0, 0)))]
            scratch = pltpu.VMEM((heads * r, lanes), F32)
        else:
            outs = [sums] + [
                ((rows, lanes), BF16, pl.BlockSpec((rows, lanes), lambda t, *_: (0, 0))) for _, rows in spans[::-1]
            ]
            scratch = pltpu.VMEM(keys.shape, F32)
        return call(
            functools.partial(
                attend_back_kernel, heads=heads, width=width, base=base, bk=KEY_BLOCK, last=len(acc)
            ),
            nb,
            3,
            [
                here(qw),
                moved(qw),
                here(qw),
                stacked,
                pl.BlockSpec((1, 1, r), lambda t, *_: (t, 0, 0)),
                whole_block(keys),
            ]
            + [sums[2]] * len(acc),
            outs,
            [scratch],
            (table, low, high, q, d_o, o_float, stat, local.reshape(nb, 1, r), keys, *acc),
            20 * attn_flops,
            plane * qw * 12,
        )

    acc, *halo_grads = attend_back(halo_part, reach, halo_keys)
    acc, halo_grads, ffn_sum.got, ffn_grad_0 = tie(acc, halo_grads, ffn_sum.got, ffn_grad_0)
    back_0 = home(ffn_grad_0)
    returned = [line_move(g, -d, range(d, n)) for g, (d, _) in zip(halo_grads[::-1], spans)]
    dq, dkv = attend_back(own_part, 0, kv, acc)
    dq, back_0, returned = tie(dq, back_0, returned)
    d_raw, d_head_gains = call(
        functools.partial(prep_back_kernel, heads=heads, width=width, plane=plane),
        nb,
        1,
        [moved(qw + lanes), here(lanes), here(lanes), whole_block(q_gain), whole_block(key_gain), here(qw), here(lanes)]
        + [whole_block(g) for g in returned],
        [
            ((plane, qw + lanes), BF16, moved(qw + lanes)),
            ((8, lanes), F32, pl.BlockSpec((8, lanes), lambda t, *_: (0, 0))),
        ],
        [],
        (table, raw, cos, sin, q_gain, key_gain, dq, dkv, *returned),
        plane * (qw + width) * 20,
        plane * (qw + 2 * width) * 10,
    )
    one = split_dot(d_raw, w_qkv)
    d_raw, one = tie(d_raw, one)
    one = Sums(*one)
    gain_sums, attn_grad = weight_grads(a_one, d_raw, d_h_rows, o, w_qkv)
    attn_grad = line_scatter(attn_grad, n)
    out_tokens = (resid + ffn_sum.third()).astype(BF16)
    back_1 = home(ffn_grad_1)

    def joined(part):
        cols = [jnp.split(v, 3, axis=-1)[part] for v in (back_0, back_1)]
        return jnp.concatenate(cols, axis=-1).reshape(step // QUAD, -1).astype(F32)

    ffn_outs = (joined(0), joined(1), joined(2).T)
    one.second()
    one.got, ffn_outs, gain_sums = tie(one.got, ffn_outs, gain_sums)
    d_attn_gain = gain_sums[:, 0] / gain_1
    d_q_gain = d_head_gains[0, :width] + d_head_gains[0, width:]
    gains = sum_over_ctx(jnp.concatenate([d_attn_gain, d_ffn_gain, d_q_gain, d_head_gains[1, :width]]))
    d_x, _ = norm_back(x_own, scale_1, gain_1, one.third())
    d_tokens = d_h + d_x

    attn_back = home(attn_grad)
    attn_back, gains = tie(attn_back, gains)
    gains = gains + swap_x(gains)

    def piece(start, size):
        return attn_back[:, :, start : start + size].reshape(step // QUAD, -1).astype(F32)

    return (
        out_tokens,
        d_tokens,
        gains[:model],
        gains[model : 2 * model],
        gains[2 * model : 2 * model + width],
        gains[2 * model + width :],
        piece(0, qw),
        piece(qw, width),
        piece(qw + width, width),
        piece(qw + 2 * width, qw).T,
        *ffn_outs,
    )


def solution(mesh):
    return jax.shard_map(
        on_device,
        mesh=mesh,
        in_specs=(
            P(("ctx", "tp"), None),
            P(),
            P(),
            P(),
            P(),
            P("ctx", "tp"),
            P("ctx", "tp"),
            P("ctx", "tp"),
            P("tp", "ctx"),
            P("ctx", "tp"),
            P("ctx", "tp"),
            P("tp", "ctx"),
            P("ctx"),
            P(("ctx", "tp"), None),
        ),
        out_specs=(
            P(("ctx", "tp"), None),
            P(("ctx", "tp"), None),
            P(),
            P(),
            P(),
            P(),
            P("ctx", "tp"),
            P("ctx", "tp"),
            P("ctx", "tp"),
            P("tp", "ctx"),
            P("ctx", "tp"),
            P("ctx", "tp"),
            P("tp", "ctx"),
        ),
        check_vma=False,
    )
```

```python
import functools
import math

import jax
import jax.numpy as jnp
from jax import lax
from jax.experimental import pallas as pl
from jax.experimental.pallas import tpu as pltpu
from jax.sharding import PartitionSpec as P

WB = 6
EPSILON = 1e-05
ROPE_BASE = 1000000.0
LOG2E = math.log2(math.e)

QUAD = 4
KEY_BLOCK = 384
FIRST_BLOCK = 4

F32 = jnp.float32
BF16 = jnp.bfloat16


def swap_ctx(value, bit):
    n = lax.axis_size("ctx")
    return lax.ppermute(value, "ctx", [(i, i ^ bit) for i in range(n)])


def swap_core(value):
    return swap_ctx(value, 1)


def swap_b(value):
    return swap_ctx(value, 2)


def swap_x(value):
    return lax.ppermute(value, "tp", [(0, 1), (1, 0)])


def line_move(value, by, sources):
    pairs = [(s * QUAD + q, (s + by) * QUAD + q) for s in sources for q in range(QUAD)]
    return lax.ppermute(value, "ctx", pairs)


def line_groups(n):
    return [[p * QUAD + q for p in range(n)] for q in range(QUAD)]


def line_gather(own, n):
    return lax.all_gather(own, "ctx", axis=0, axis_index_groups=line_groups(n), tiled=True)


def line_scatter(partial, n):
    return lax.psum_scatter(partial, "ctx", scatter_dimension=0, axis_index_groups=line_groups(n), tiled=True)


def line_move(value, by, sources):
    pairs = [(s * QUAD + q, (s + by) * QUAD + q) for s in sources for q in range(QUAD)]
    return lax.ppermute(value, "ctx", pairs)


def tie(*values):
    return lax.optimization_barrier(values)


def add16(a, b):
    return (a.astype(F32) + b.astype(F32)).astype(BF16)


def swap_both(value):
    n = lax.axis_size("ctx")
    return lax.ppermute(value, ("ctx", "tp"), [(2 * i + x, 2 * (i ^ 2) + 1 - x) for i in range(n) for x in range(2)])


class Rows:
    def __init__(self, own):
        self.own, self.half = own, own.shape[0] // 2
        self.first = (swap_x(own), swap_b(own))

    def second(self):
        from_x, from_b = self.first
        self.last = (swap_x(from_b[: self.half]), swap_b(from_x[self.half :]))

    def third(self):
        near = [self.own, *self.first, *self.last]
        return near + [swap_core(piece) for piece in near]


def gather_rows(own, beside=None):
    rows = Rows(own)
    if beside is not None:
        rows.first, beside = tie(rows.first, beside)
    rows.second()
    return rows.third() if beside is None else (rows.third(), beside)


class Sums:
    def __init__(self, near, far):
        r = near.shape[0] // 4
        self.half = r // 2

        def fold(block):
            return add16(near[block * r : (block + 1) * r], swap_core(far[block]))

        self.parts = (fold(3), fold(1), fold(2), fold(0))

    def second(self):
        both, for_x, for_b, _ = self.parts
        half = self.half
        self.got = (swap_x(both[:half]), swap_b(both[half:]), swap_x(for_x[:half]), swap_b(for_b[half:]))

    def third(self):
        _, for_x, for_b, own = self.parts
        top, bottom, x_top, b_bottom = self.got
        half = self.half
        x_bottom = swap_x(add16(for_x[half:], bottom))
        b_top = swap_b(add16(for_b[:half], top))
        own = own.astype(F32)
        return jnp.concatenate(
            [
                own[:half] + x_top.astype(F32) + b_top.astype(F32),
                own[half:] + b_bottom.astype(F32) + x_bottom.astype(F32),
            ],
            axis=0,
        )


    def second_x(self):
        self.got = swap_x(self.parts[0])

    def third_x(self, beside):
        _, for_x, for_b, own = self.parts
        for_b, for_x, beside = tie(add16(for_b, self.got), for_x, beside)
        return own.astype(F32) + swap_x(for_x).astype(F32) + swap_b(for_b).astype(F32), beside


def scatter_rows(near, far, beside=None):
    sums = Sums(near, far)
    sums.second()
    if beside is not None:
        sums.got, beside = tie(sums.got, beside)
    return sums.third() if beside is None else (sums.third(), beside)


def blocks_of(rows):
    r = rows.shape[0] // 4
    return [rows[k * r : (k + 1) * r] for k in range(4)]


def spread(pieces, axis=0):
    n = lax.axis_size("ctx")
    groups = [list(range(i, i + QUAD)) for i in range(0, n, QUAD)]
    return lax.all_to_all(pieces, "ctx", axis, axis, axis_index_groups=groups, tiled=True)


def sum_over_ctx(value, bit, end):
    while bit < end:
        value = value + swap_ctx(value, bit)
        bit *= 2
    return value


def dot(a, b):
    return jnp.dot(a, b, preferred_element_type=F32)


def dot_nt(a, b):
    return lax.dot_general(a, b, (((1,), (1,)), ((), ())), preferred_element_type=F32)


def dot_tn(a, b):
    return lax.dot_general(a, b, (((0,), (0,)), ((), ())), preferred_element_type=F32)


def rms_scale(values):
    return lax.rsqrt(jnp.mean(values * values, axis=-1, keepdims=True) + EPSILON)


def norm_back(values, scale, gain, grad):
    unit = values * scale
    inner = grad * gain
    d_values = scale * (inner - unit * jnp.mean(inner * unit, axis=-1, keepdims=True))
    return d_values, jnp.sum(grad * unit, axis=0)


def pick(refs, block, out_ref, at):
    r = refs[0].shape[0]
    for k in range(8):
        index = k // 4 * (len(refs) // 2) + k % 4

        @pl.when(block == k)
        def _():
            if k % 4 < 3 or len(refs) == 8:
                out_ref[at : at + r, :] = refs[index][...]
            else:
                out_ref[at : at + r // 2, :] = refs[index][...]
                out_ref[at + r // 2 : at + r, :] = refs[index + 1][...]


class Heads:
    def __init__(self, width, cos, sin):
        self.width, self.cos, self.sin = width, cos, sin
        lanes = 2 * width
        row = lax.broadcasted_iota(jnp.int32, (lanes, lanes), 0)
        col = lax.broadcasted_iota(jnp.int32, (lanes, lanes), 1)
        self.same = jnp.where(row // width == col // width, 1.0 / width, 0.0).astype(BF16)

    def mean(self, u):
        high = u.astype(BF16)
        low = (u - high.astype(F32)).astype(BF16)
        return dot(high, self.same) + dot(low, self.same)

    def swapped(self, u):
        half = self.width // 2
        lane = lax.broadcasted_iota(jnp.int32, u.shape, 1)
        return jnp.where((lane & half) == 0, pltpu.roll(u, 2 * self.width - half, 1), pltpu.roll(u, half, 1))

    def ready(self, u, gain):
        u = u * lax.rsqrt(self.mean(u * u) + EPSILON) * gain
        return u * self.cos + self.swapped(u) * self.sin

    def back(self, w, gain, grad):
        e = grad * self.cos - self.swapped(grad) * self.sin
        scale = lax.rsqrt(self.mean(w * w) + EPSILON)
        unit = w * scale
        inner = e * gain
        return scale * (inner - unit * self.mean(inner * unit)), jnp.sum(e * unit, axis=0, keepdims=True)


def project_kernel(table, *refs, heads, width):
    pieces, (w_ref, cos_ref, sin_ref, q_gain_ref, k_gain_ref, rows_ref, raw_ref, q_ref, kv_ref) = refs[:-9], refs[-9:]
    pick(pieces, pl.program_id(0), rows_ref, 0)
    raw = dot(rows_ref[...], w_ref[...])
    raw_ref[...] = raw
    math_of = Heads(width, cos_ref[...], sin_ref[...])
    lanes = 2 * width
    for c in range(heads // 2):
        cols = slice(c * lanes, (c + 1) * lanes)
        q_ref[:, cols] = math_of.ready(raw[:, cols], q_gain_ref[...]).astype(BF16)
    last = raw[:, heads * width :]
    lane = lax.broadcasted_iota(jnp.int32, last.shape, 1)
    kv_ref[...] = jnp.where(lane < width, math_of.ready(last, k_gain_ref[...]), last).astype(BF16)


def prep_back_kernel(
    table, raw_ref, cos_ref, sin_ref, q_gain_ref, k_gain_ref, dq_ref, dkv_ref, *refs, heads, width, plane
):
    halo, (out_ref, dg_ref) = refs[:-2], refs[-2:]
    t = pl.program_id(0)

    @pl.when(t == 0)
    def _():
        dg_ref[...] = jnp.zeros_like(dg_ref)

    math_of = Heads(width, cos_ref[...], sin_ref[...])
    lanes = 2 * width
    total = jnp.zeros((1, lanes), F32)
    for c in range(heads // 2):
        cols = slice(c * lanes, (c + 1) * lanes)
        dw, dg = math_of.back(raw_ref[:, cols], q_gain_ref[...], dq_ref[:, cols])
        out_ref[:, cols] = dw.astype(BF16)
        total = total + dg
    grad = dkv_ref[...]
    r = grad.shape[0]
    for ref in halo:
        missing = plane // r - ref.shape[0] // r
        at = pl.multiple_of(jnp.maximum(t - missing, 0) * r, r)
        grad = grad + jnp.where(t >= missing, ref[pl.ds(at, r), :].astype(F32), 0.0)
    dw, dg = math_of.back(raw_ref[:, heads * width :], k_gain_ref[...], grad)
    lane = lax.broadcasted_iota(jnp.int32, grad.shape, 1)
    out_ref[:, heads * width :] = jnp.where(lane < width, dw, grad).astype(BF16)
    dg_ref[0:1, :] += total
    dg_ref[1:2, :] += dg


def rows_dot_kernel(*refs):
    pieces, (w_ref, rows_ref, out_ref) = refs[:10], refs[10:]
    pick(pieces, pl.program_id(0), rows_ref, 0)
    out_ref[...] = dot(rows_ref[...], w_ref[...]).astype(BF16)


def stack_heads(block, heads, width):
    return jnp.concatenate([block[:, h * width : (h + 1) * width] for h in range(heads)], axis=0)


def attend_kernel(table, lo, hi, q_ref, start_ref, kv_ref, *refs, heads, width, base, bk, last):
    ones_v = refs[-1]
    if last:
        acc_in, o_ref, of_ref, stat_ref, acc = refs[:5]
    else:
        acc = refs[0]
    t = pl.program_id(0)
    r = q_ref.shape[0]

    @pl.when(t == 0)
    def _():
        lane = lax.broadcasted_iota(jnp.int32, kv_ref.shape, 1)
        ones_v[...] = jnp.where(lane < width, jnp.ones((), BF16), kv_ref[...])

    q = stack_heads(q_ref[...], heads, width)
    q = jnp.concatenate([q, jnp.zeros_like(q)], axis=-1)
    start = jnp.concatenate([start_ref[...]] * heads, axis=0)
    pos = base + t * r + lax.broadcasted_iota(jnp.int32, (r, 1), 0)
    pos = jnp.concatenate([pos] * heads, axis=0)
    acc[...] = acc_in[...] if last else jnp.zeros_like(acc)
    c = LOG2E / math.sqrt(width)

    def step(kb, carry):
        k0 = pl.multiple_of(kb * bk, bk)
        s = dot_nt(q, kv_ref[pl.ds(k0, bk), :])
        key = k0 + lax.broadcasted_iota(jnp.int32, (1, bk), 1)
        p = jnp.where((key >= start) & (key <= pos), jnp.exp2(s * c), 0.0)
        acc[...] += dot(p.astype(BF16), ones_v[pl.ds(k0, bk), :])
        return carry

    lax.fori_loop(lo[t], hi[t], step, 0)
    if last:
        total = acc[:, :1]
        o = acc[:, width:] / total
        stat_ref[...] = jnp.log2(total)
        for h in range(heads):
            part = o[h * r : (h + 1) * r]
            of_ref[:, h * width : (h + 1) * width] = part
            o_ref[:, h * width : (h + 1) * width] = part.astype(BF16)


def attend_back_kernel(
    table, lo, hi, q_ref, do_ref, of_ref, stat_ref, start_ref, kv_ref, *refs, heads, width, base, bk, last
):
    if last:
        acc_in, dq_ref, dkv, acc = refs
    else:
        acc, dkv_refs, dkv = refs[0], refs[1:-1], refs[-1]
    t = pl.program_id(0)
    r = q_ref.shape[0]

    @pl.when(t == 0)
    def _():
        dkv[...] = jnp.zeros_like(dkv)

    scale = 1.0 / math.sqrt(width)
    q = stack_heads(q_ref[...], heads, width)
    do = stack_heads(do_ref[...], heads, width)
    of = stack_heads(of_ref[...], heads, width)
    delta = jnp.sum(do.astype(F32) * of, axis=-1, keepdims=True)
    lane = lax.broadcasted_iota(jnp.int32, (heads * r, 2 * width), 1)
    rows = jnp.transpose(jnp.where(lane == 0, stat_ref[...], delta))
    stat, delta = rows[0:1, :], rows[1:2, :]
    q = jnp.concatenate([q, jnp.zeros_like(q)], axis=-1)
    q_scaled = (q.astype(F32) * scale).astype(BF16)
    do = jnp.concatenate([jnp.zeros_like(do), do], axis=-1)
    start = jnp.concatenate([start_ref[0]] * heads, axis=-1)
    pos = base + t * r + lax.broadcasted_iota(jnp.int32, (1, r), 1)
    pos = jnp.concatenate([pos] * heads, axis=-1)
    acc[...] = acc_in[...] if last else jnp.zeros_like(acc)

    def step(kb, carry):
        k0 = pl.multiple_of(kb * bk, bk)
        kv = kv_ref[pl.ds(k0, bk), :]
        s = dot_nt(kv, q_scaled)
        dp = dot_nt(kv, do)
        key = k0 + lax.broadcasted_iota(jnp.int32, (bk, 1), 0)
        p = jnp.where((key >= start) & (key <= pos), jnp.exp2(s * LOG2E - stat), 0.0)
        ds = (p * (dp - delta)).astype(BF16)
        dkv[pl.ds(k0, bk), :] += dot(ds, q_scaled) + dot(p.astype(BF16), do)
        acc[...] += dot_tn(ds, kv)
        return carry

    lax.fori_loop(lo[t], hi[t], step, 0)
    if last:
        dq = acc[...][:, :width] * scale
        for h in range(heads):
            dq_ref[:, h * width : (h + 1) * width] = dq[h * r : (h + 1) * r]
    else:

        @pl.when(t == pl.num_programs(0) - 1)
        def _():
            at = 0
            for ref in dkv_refs:
                ref[...] = dkv[at : at + ref.shape[0], :].astype(BF16)
                at += ref.shape[0]


def feed_first_kernel(*refs, hb):
    pieces, (c_ref, w_ref, hid_ref, dgu_ref, back_ref, rows_ref) = refs[:10], refs[10:]
    t = pl.program_id(0)
    r = pieces[0].shape[0]
    pick(pieces, 2 * t, rows_ref, 0)
    pick(pieces, 2 * t + 1, rows_ref, r)
    back_ref[...] = feed(rows_ref, c_ref, w_ref, hid_ref, dgu_ref, hb).astype(BF16)


def feed_last_kernel(a_ref, c_ref, w_ref, prev_ref, hid_ref, dgu_ref, near_ref, *far_refs, hb):
    t = pl.program_id(0)
    back = feed(a_ref, c_ref, w_ref, hid_ref, dgu_ref, hb) + prev_ref[...].astype(F32)
    split_store(back, t, near_ref, far_refs)


def feed(a_ref, c_ref, w_ref, hid_ref, dgu_ref, hb):
    a, c = a_ref[...], c_ref[...]
    gate, up = dot(a, w_ref[:, :hb]), dot(a, w_ref[:, hb : 2 * hb])
    d_hid = dot(c, w_ref[:, 2 * hb :])
    sig = jax.nn.sigmoid(gate)
    silu = gate * sig
    hid_ref[...] = (silu * up).astype(BF16)
    dgu_ref[:, :hb] = (d_hid * up * (sig * (1.0 + gate * (1.0 - sig)))).astype(BF16)
    dgu_ref[:, hb:] = (d_hid * silu).astype(BF16)
    return dot_nt(dgu_ref[...], w_ref[:, : 2 * hb])


def down_kernel(h0_ref, h1_ref, w0_ref, w1_ref, near_ref, *far_refs):
    t = pl.program_id(0)
    y = sum(dot_nt(h[...], w[:, 2 * h.shape[1] :]) for h, w in ((h0_ref, w0_ref), (h1_ref, w1_ref)))
    split_store(y, t, near_ref, far_refs)


def split_store(value, t, near_ref, far_refs):
    r = far_refs[0].shape[0]

    @pl.when(t < 2)
    def _():
        near_ref[...] = value.astype(BF16)

    for k, ref in enumerate(far_refs):

        @pl.when(t == 2 + k // 2)
        def _():
            ref[...] = value[k % 2 * r : (k % 2 + 1) * r].astype(BF16)


def split_outs(total, model):
    far = pl.BlockSpec((total // 8, model), lambda t: (0, 0))
    near = pl.BlockSpec((total // 4, model), lambda t: (jnp.minimum(t, 1), 0))
    return [((total // 2, model), BF16, near)] + [((total // 8, model), BF16, far)] * 4


def split_dot_kernel(a_ref, w_ref, near_ref, *far_refs):
    split_store(dot_nt(a_ref[...], w_ref[...]), pl.program_id(0), near_ref, far_refs)


def split_dot(a, w):
    total, cols = a.shape
    model = w.shape[0]
    near, *far = call(
        split_dot_kernel,
        4,
        0,
        [pl.BlockSpec((total // 4, cols), lambda t: (t, 0)), whole_block(w)],
        split_outs(total, model),
        [],
        (a, w),
        2 * total * model * cols,
        2 * total * (model + cols),
    )
    return near, far


def down_rows(h0, h1, w0, w1):
    total, hb = h0.shape[0], (h0.shape[1] + h1.shape[1]) // 2
    model = w0.shape[0]

    def row(h):
        return pl.BlockSpec((total // 4, h.shape[1]), lambda t: (t, 0))

    near, *far = call(
        down_kernel,
        4,
        0,
        [row(h0), row(h1), whole_block(w0), whole_block(w1)],
        split_outs(total, model),
        [],
        (h0, h1, w0, w1),
        4 * total * model * hb,
        2 * total * (model + 2 * hb) + 12 * model * hb,
    )
    return near, far


def whole_block(v):
    return pl.BlockSpec(v.shape, lambda t, *_: (0,) * len(v.shape), pipeline_mode=pl.Buffered(1))


def feed_forward(a, c, w, prev=None):
    total, model = c.shape
    rows = total // 4
    hb = w.shape[1] // 3

    def row(cols):
        return pl.BlockSpec((rows, cols), lambda t: (t, 0))

    outs = [((total, hb), BF16, row(hb)), ((total, 2 * hb), BF16, row(2 * hb))]
    if prev is None:
        kernel, args = feed_first_kernel, (*a, c, w)
        ins = [whole_block(piece) for piece in a] + [row(model), whole_block(w)]
        outs += [((total, model), BF16, row(model))] * 2
    else:
        kernel, args = feed_last_kernel, (a, c, w, prev)
        ins = [row(model), row(model), whole_block(w), row(model)]
        outs += split_outs(total, model)
    return call(
        functools.partial(kernel, hb=hb),
        4,
        0,
        ins,
        outs,
        [],
        args,
        12 * total * model * hb,
        2 * total * (4 * model + 3 * hb) + 6 * model * hb,
        total * hb,
    )


def pack_kernel(*refs, flip, widths, cuts):
    ins, outs = refs[: len(flip)], refs[len(flip) :]
    for quarter in range(QUAD):
        for out_ref, (low, high) in zip(outs, cuts):
            at = 0
            for ref, turned, width in zip(ins, flip, widths):
                start, end = low * width // high[1], high[0] * width // high[1]
                cut = slice(quarter * width + start, quarter * width + end)
                out_ref[quarter, :, at : at + end - start] = jnp.transpose(ref[cut, :]) if turned else ref[:, cut]
                at += end - start


def packed(weights, flip, cuts):
    rows = weights[0].shape[flip[0]]
    widths = [(w.shape[0] if f else w.shape[1]) // QUAD for w, f in zip(weights, flip)]
    shapes = [
        jax.ShapeDtypeStruct((QUAD, rows, sum((high - low) * w // of for w in widths)), BF16)
        for low, (high, of) in cuts
    ]
    return call(
        functools.partial(pack_kernel, flip=flip, widths=widths, cuts=cuts),
        1,
        0,
        [whole_block(w) for w in weights],
        [(shape.shape, BF16, whole_block(shape)) for shape in shapes],
        [],
        tuple(weights),
        1,
        sum(4 * math.prod(shape.shape) for shape in shapes),
    )


def unpack_kernel(*refs, flip, cuts):
    blocks, outs = refs[: len(cuts)], refs[len(cuts) :]
    for block, (low, high) in zip(blocks, cuts):
        at = 0
        for ref, turned in zip(outs, flip):
            width = (ref.shape[0] if turned else ref.shape[1]) // QUAD
            start, end = low * width // high[1], high[0] * width // high[1]
            for quarter in range(QUAD):
                part = block[quarter, :, at : at + end - start].astype(F32)
                cut = slice(quarter * width + start, quarter * width + end)
                if turned:
                    ref[cut, :] = jnp.transpose(part)
                else:
                    ref[:, cut] = part
            at += end - start


def unpacked(blocks, shapes, flip, cuts):
    return call(
        functools.partial(unpack_kernel, flip=flip, cuts=cuts),
        1,
        0,
        [whole_block(v) for v in blocks],
        [(shape, F32, whole_block(jax.ShapeDtypeStruct(shape, F32))) for shape in shapes],
        [],
        tuple(blocks),
        1,
        sum(6 * math.prod(v.shape) for v in blocks),
    )


def weights_kernel(a_ref, b_ref, c_ref, d_ref, *refs):
    out_ref = refs[-1]
    cols = b_ref.shape[1]
    first = dot_tn(a_ref[...], b_ref[...])
    out_ref[:, :cols] = first.astype(BF16)
    out_ref[:, cols:] = dot_tn(c_ref[...], d_ref[...]).astype(BF16)
    if len(refs) > 1:
        w_ref, sums_ref = refs[:2]
        both = first * w_ref[...].astype(F32)
        high = both.astype(BF16)
        low = (both - high.astype(F32)).astype(BF16)
        ones = jnp.ones((sums_ref.shape[0], cols), BF16)
        sums_ref[...] = dot_nt(ones, high) + dot_nt(ones, low)


def weight_grads(a, b, c, d, w=None, rows=512):
    total, model = a.shape
    cut = pl.BlockSpec((total, rows), lambda t: (0, t))

    def whole(v):
        return pl.BlockSpec(v.shape, lambda t: (0, 0), pipeline_mode=pl.Buffered(1))

    def tall(cols):
        return pl.BlockSpec((rows, cols), lambda t: (t, 0))

    cols = b.shape[1] + d.shape[1]
    more = [] if w is None else [w]
    return call(
        weights_kernel,
        model // rows,
        0,
        [cut, whole(b), cut, whole(d)] + [tall(v.shape[1]) for v in more],
        [((8, model), F32, pl.BlockSpec((8, rows), lambda t: (0, t)))] * len(more) + [((model, cols), BF16, tall(cols))],
        [],
        (a, b, c, d, *more),
        2 * total * model * cols,
        2 * (2 * total * model + (total + model) * cols),
    )


def call(kernel, blocks, prefetch, ins, outs, scratch, args, flops, nbytes, transcendentals=0):
    return pl.pallas_call(
        kernel,
        out_shape=[jax.ShapeDtypeStruct(shape, dtype) for shape, dtype, _ in outs],
        grid_spec=pltpu.PrefetchScalarGridSpec(
            num_scalar_prefetch=prefetch,
            grid=(blocks,),
            in_specs=ins,
            out_specs=[spec for _, _, spec in outs],
            scratch_shapes=scratch,
        ),
        compiler_params=pltpu.CompilerParams(
            dimension_semantics=("arbitrary",), vmem_limit_bytes=56 * 1024 * 1024
        ),
        cost_estimate=pl.CostEstimate(
            flops=int(flops), bytes_accessed=int(nbytes), transcendentals=int(transcendentals)
        ),
    )(*args)


def on_device(
    tokens,
    attn_gain,
    ffn_gain,
    query_norm_gain,
    k_gain,
    w_query,
    key_projection,
    value_projection,
    w_out,
    w_gate,
    w_up,
    w_down,
    doc_start,
    cotangent,
):
    i, x = lax.axis_index("ctx"), lax.axis_index("tp")
    n = lax.axis_size("ctx") // QUAD
    line, b, core = i // QUAD, (i // 2) % 2, i % 2
    r, model = tokens.shape
    plane = 2 * QUAD * r
    width = query_norm_gain.shape[0]
    heads = w_query.shape[1] // QUAD // width
    qw = heads * width
    hidden = w_gate.shape[1] // QUAD
    step = model // n
    reach = WB * doc_start.shape[0]

    (sent,) = packed((w_query, key_projection, value_projection, w_out), (0, 0, 0, 1), [(0, (1, 1))])
    sent, tokens = tie(spread(sent), tokens)
    w_attn = line_gather(sent.reshape(step, -1), n)
    w_qkv, w_o = w_attn[:, : qw + 2 * width], w_attn[:, qw + 2 * width :]
    x_own = tokens.astype(F32)
    scale_1 = rms_scale(x_own)

    cut = FIRST_BLOCK
    ffn_cuts = [(0, (cut, 8)), (cut, (8, 8))]
    ffn_pieces = packed((w_gate, w_up, w_down), (0, 0, 1), ffn_cuts)
    a_own = (x_own * scale_1 * attn_gain).astype(BF16)
    a_near = (swap_x(a_own), swap_b(a_own), swap_both(a_own))

    near_core, near_b = swap_core(doc_start), swap_b(doc_start)
    far = swap_core(near_b)
    rows0 = [jnp.where(core == c, doc_start, near_core) for c in range(2)]
    rows1 = [jnp.where(core == c, near_b, far) for c in range(2)]
    starts = jnp.concatenate([jnp.where(b == y, rows0[c], rows1[c]) for y in range(2) for c in range(2)])
    first = line * plane
    relative = first + jnp.arange(plane, dtype=jnp.int32) - starts
    inv_freq = jnp.power(ROPE_BASE, -2.0 * jnp.arange(width // 2, dtype=F32) / width)
    angles = relative.astype(F32)[:, None] * inv_freq[None, :]
    cos, sin = jnp.cos(angles), jnp.sin(angles)
    cos = jnp.concatenate([cos] * 4, axis=-1)
    sin = jnp.concatenate([-sin, sin] * 2, axis=-1)
    sent_0 = spread(ffn_pieces[0])
    w_ffn_0 = line_gather(sent_0.reshape(step, -1), n)
    a_near, cos, sin, pieces_1, _ = tie(a_near, cos, sin, ffn_pieces[1], sent_0)
    sent_1 = spread(pieces_1)
    a_pieces = [a_own, *a_near]
    a_pieces = a_pieces + [swap_core(piece) for piece in a_pieces]

    blocks = jnp.arange(2 * QUAD, dtype=jnp.int32)
    table = (
        ((((blocks >> 1) & 1) ^ core) << 2) | (((blocks >> 2) ^ b) << 1) | ((blocks & 1) ^ x)
    ).astype(jnp.int32)
    inverse = (
        ((((blocks >> 1) & 1) ^ b) << 2) | (((blocks >> 2) ^ core) << 1) | ((blocks & 1) ^ x)
    ).astype(jnp.int32)
    nb = 2 * QUAD

    def key_range(base, keys):
        local = starts - (first - base)
        low = jnp.clip(local[::r] // KEY_BLOCK, 0, keys // KEY_BLOCK)
        high = jnp.clip((base + (blocks + 1) * r - 1) // KEY_BLOCK + 1, low, keys // KEY_BLOCK)
        return local, low, high

    own_part, halo_part = key_range(0, plane), key_range(reach, reach)

    gain_1, gain_2 = attn_gain, ffn_gain

    def here(cols):
        return pl.BlockSpec((r, cols), lambda t, *_: (t, 0))

    def moved(cols):
        return pl.BlockSpec((r, cols), lambda t, table, *_: (table[t], 0))

    lanes = 2 * width
    two = lambda gain: jnp.concatenate([gain, gain])[None, :]
    q_gain, key_gain = two(query_norm_gain), two(k_gain)
    a_one, raw, q, kv = call(
        functools.partial(project_kernel, heads=heads, width=width),
        nb,
        1,
        [whole_block(piece) for piece in a_pieces]
        + [whole_block(w_qkv), moved(lanes), moved(lanes), whole_block(q_gain), whole_block(key_gain)],
        [
            ((plane, model), BF16, here(model)),
            ((plane, qw + lanes), F32, here(qw + lanes)),
            ((plane, qw), BF16, moved(qw)),
            ((plane, lanes), BF16, moved(lanes)),
        ],
        [],
        (inverse, *a_pieces, w_qkv, cos, sin, q_gain, key_gain),
        2 * plane * model * (qw + lanes),
        plane * (4 * model + 10 * qw),
    )
    q, kv, sent_1, cot_own = tie(q, kv, sent_1, cotangent)
    w_ffn_1 = line_gather(sent_1.reshape(step, -1), n)
    spans = []
    left, distance = reach, 1
    while left > 0:
        spans.append((distance, min(left, plane)))
        left -= plane
        distance += 1
    halo = [line_move(kv[plane - rows :], d, range(0, max(n - d, 0))) for d, rows in spans]
    attn_flops = plane * heads * (plane // 2 + 2 * KEY_BLOCK) * width
    stacked = pl.BlockSpec((heads * r, 1), lambda t, *_: (t, 0))
    sums = ((plane * heads, lanes), F32, pl.BlockSpec((heads * r, lanes), lambda t, *_: (t, 0)))

    def attend(part, base, keys, *acc):
        local, low, high = part
        outs = [((plane, qw), BF16, moved(qw)), ((plane, qw), F32, here(qw)), ((plane * heads, 1), F32, stacked)]
        return call(
            functools.partial(attend_kernel, heads=heads, width=width, base=base, bk=KEY_BLOCK, last=len(acc)),
            nb,
            3,
            [here(qw), pl.BlockSpec((r, 1), lambda t, *_: (t, 0)), whole_block(keys)] + [sums[2]] * len(acc),
            outs if acc else [sums],
            [pltpu.VMEM((heads * r, lanes), F32)] * len(acc) + [pltpu.VMEM(keys.shape, BF16)],
            (table, low, high, q, local[:, None], keys, *acc),
            8 * attn_flops,
            plane * qw * 10,
        )

    (acc,) = attend(own_part, 0, kv)
    cot = Rows(cot_own)
    acc, halo, cot.first = tie(acc, halo, cot.first)
    cot.second()
    halo_keys = jnp.concatenate(halo[::-1], axis=0)
    o, o_float, stat = attend(halo_part, reach, halo_keys, acc)

    half = plane // 2
    o, cot.last = tie(o, cot.last)

    attn_sum, cot = scatter_rows(*split_dot(o, w_o), jnp.concatenate(cot.third(), axis=0))
    resid = x_own + attn_sum
    scale_2 = rms_scale(resid)
    a_pieces = gather_rows((resid * scale_2 * gain_2).astype(BF16))

    hid_0, d_gu_0, back, a_two = feed_forward(a_pieces, cot, w_ffn_0)
    (ffn_grad_0,) = weight_grads(a_two, d_gu_0, cot, hid_0)
    w_ffn_1, _ = tie(w_ffn_1, ffn_grad_0)
    ffn_grad_0 = line_scatter(ffn_grad_0, n)
    hid_1, d_gu_1, near, *far = feed_forward(a_two, cot, w_ffn_1, back)
    d_two, ffn_grad_1 = scatter_rows(near, far, weight_grads(a_two, d_gu_1, cot, hid_1)[0])
    ffn_grad_1 = line_scatter(ffn_grad_1, n)
    d_res, d_ffn_gain = norm_back(resid, scale_2, gain_2, d_two)
    d_h = cotangent.astype(F32) + d_res

    h_pieces, down = gather_rows(d_h.astype(BF16), down_rows(hid_0, hid_1, w_ffn_0, w_ffn_1))
    ffn_sum = Sums(*down)

    def home(grad):
        return spread(grad.reshape(QUAD, step // QUAD, -1))

    d_h_rows, d_o = call(
        rows_dot_kernel,
        nb,
        0,
        [whole_block(piece) for piece in h_pieces] + [whole_block(w_o)],
        [((plane, model), BF16, here(model)), ((plane, qw), BF16, here(qw))],
        [],
        (*h_pieces, w_o),
        2 * plane * model * qw,
        4 * plane * model,
    )
    d_o, ffn_sum.parts = tie(d_o, ffn_sum.parts)
    ffn_sum.second()

    def attend_back(part, base, keys, *acc):
        local, low, high = part
        if acc:
            outs = [((plane, qw), F32, here(qw)), (keys.shape, F32, pl.BlockSpec(keys.shape, lambda t, *_: (0, 0)))]
            scratch = pltpu.VMEM((heads * r, lanes), F32)
        else:
            outs = [sums] + [
                ((rows, lanes), BF16, pl.BlockSpec((rows, lanes), lambda t, *_: (0, 0))) for _, rows in spans[::-1]
            ]
            scratch = pltpu.VMEM(keys.shape, F32)
        return call(
            functools.partial(
                attend_back_kernel, heads=heads, width=width, base=base, bk=KEY_BLOCK, last=len(acc)
            ),
            nb,
            3,
            [
                here(qw),
                moved(qw),
                here(qw),
                stacked,
                pl.BlockSpec((1, 1, r), lambda t, *_: (t, 0, 0)),
                whole_block(keys),
            ]
            + [sums[2]] * len(acc),
            outs,
            [scratch],
            (table, low, high, q, d_o, o_float, stat, local.reshape(nb, 1, r), keys, *acc),
            20 * attn_flops,
            plane * qw * 12,
        )

    acc, *halo_grads = attend_back(halo_part, reach, halo_keys)
    acc, halo_grads, ffn_sum.got, ffn_grad_0 = tie(acc, halo_grads, ffn_sum.got, ffn_grad_0)
    back_0 = home(ffn_grad_0)
    returned = [line_move(g, -d, range(d, n)) for g, (d, _) in zip(halo_grads[::-1], spans)]
    dq, dkv = attend_back(own_part, 0, kv, acc)
    dq, back_0, returned = tie(dq, back_0, returned)
    d_raw, d_head_gains = call(
        functools.partial(prep_back_kernel, heads=heads, width=width, plane=plane),
        nb,
        1,
        [moved(qw + lanes), here(lanes), here(lanes), whole_block(q_gain), whole_block(key_gain), here(qw), here(lanes)]
        + [whole_block(g) for g in returned],
        [
            ((plane, qw + lanes), BF16, moved(qw + lanes)),
            ((8, lanes), F32, pl.BlockSpec((8, lanes), lambda t, *_: (0, 0))),
        ],
        [],
        (table, raw, cos, sin, q_gain, key_gain, dq, dkv, *returned),
        plane * (qw + width) * 20,
        plane * (qw + 2 * width) * 10,
    )
    one = split_dot(d_raw, w_qkv)
    d_raw, one = tie(d_raw, one)
    one = Sums(*one)
    gain_sums, attn_grad = weight_grads(a_one, d_raw, d_h_rows, o, w_qkv)
    gain_sums = gain_sums[0]
    attn_grad = line_scatter(attn_grad, n)
    gain_sums, ffn_grad_1 = tie(gain_sums, ffn_grad_1)
    one.second_x()
    back_1 = home(ffn_grad_1)
    d_one, back_1 = one.third_x(back_1)
    ffn_outs = unpacked((back_0, back_1), [v.shape for v in (w_gate, w_up, w_down)], (0, 0, 1), ffn_cuts)
    d_one, ffn_outs, gain_sums, ffn_sum.got = tie(d_one, ffn_outs, gain_sums, ffn_sum.got)
    d_attn_gain = gain_sums / gain_1
    d_q_gain = d_head_gains[0, :width] + d_head_gains[0, width:]
    gains = jnp.concatenate([d_attn_gain, d_ffn_gain, d_q_gain, d_head_gains[1, :width]])
    gains = sum_over_ctx(gains + swap_x(gains), 1, QUAD)
    d_x, _ = norm_back(x_own, scale_1, gain_1, d_one)
    d_tokens = d_h + d_x
    out_tokens = (resid + ffn_sum.third()).astype(BF16)

    attn_grad, back_1 = tie(attn_grad, back_1)
    attn_back = home(attn_grad)
    attn_back, gains = tie(attn_back, gains)
    gains = sum_over_ctx(gains, QUAD, QUAD * n)
    attn_outs = unpacked(
        [attn_back],
        [v.shape for v in (w_query, key_projection, value_projection, w_out)],
        (0, 0, 0, 1),
        [(0, (1, 1))],
    )
    return (
        out_tokens,
        d_tokens,
        gains[:model],
        gains[model : 2 * model],
        gains[2 * model : 2 * model + width],
        gains[2 * model + width :],
        *attn_outs,
        *ffn_outs,
    )


def solution(mesh):
    return jax.shard_map(
        on_device,
        mesh=mesh,
        in_specs=(
            P(("ctx", "tp"), None),
            P(),
            P(),
            P(),
            P(),
            P("ctx", "tp"),
            P("ctx", "tp"),
            P("ctx", "tp"),
            P("tp", "ctx"),
            P("ctx", "tp"),
            P("ctx", "tp"),
            P("tp", "ctx"),
            P("ctx"),
            P(("ctx", "tp"), None),
        ),
        out_specs=(
            P(("ctx", "tp"), None),
            P(("ctx", "tp"), None),
            P(),
            P(),
            P(),
            P(),
            P("ctx", "tp"),
            P("ctx", "tp"),
            P("ctx", "tp"),
            P("tp", "ctx"),
            P("ctx", "tp"),
            P("ctx", "tp"),
            P("tp", "ctx"),
        ),
        check_vma=False,
    )
```

```python
import functools
import math

import jax
import jax.numpy as jnp
from jax import lax
from jax.experimental import pallas as pl
from jax.experimental.pallas import tpu as pltpu
from jax.sharding import PartitionSpec as P

WB = 6
EPSILON = 1e-05
ROPE_BASE = 1000000.0
LOG2E = math.log2(math.e)

QUAD = 4
KEY_BLOCK = 384
FIRST_BLOCK = 4

F32 = jnp.float32
BF16 = jnp.bfloat16


def swap_ctx(value, bit):
    n = lax.axis_size("ctx")
    return lax.ppermute(value, "ctx", [(i, i ^ bit) for i in range(n)])


def swap_core(value):
    return swap_ctx(value, 1)


def swap_b(value):
    return swap_ctx(value, 2)


def swap_x(value):
    return lax.ppermute(value, "tp", [(0, 1), (1, 0)])


def line_move(value, by, sources):
    pairs = [(s * QUAD + q, (s + by) * QUAD + q) for s in sources for q in range(QUAD)]
    return lax.ppermute(value, "ctx", pairs)


def line_groups(n):
    return [[p * QUAD + q for p in range(n)] for q in range(QUAD)]


def line_gather(own, n):
    return lax.all_gather(own, "ctx", axis=0, axis_index_groups=line_groups(n), tiled=True)


def line_scatter(partial, n):
    return lax.psum_scatter(partial, "ctx", scatter_dimension=0, axis_index_groups=line_groups(n), tiled=True)


def line_move(value, by, sources):
    pairs = [(s * QUAD + q, (s + by) * QUAD + q) for s in sources for q in range(QUAD)]
    return lax.ppermute(value, "ctx", pairs)


def tie(*values):
    return lax.optimization_barrier(values)


def add16(a, b):
    return (a.astype(F32) + b.astype(F32)).astype(BF16)


def swap_both(value):
    n = lax.axis_size("ctx")
    return lax.ppermute(value, ("ctx", "tp"), [(2 * i + x, 2 * (i ^ 2) + 1 - x) for i in range(n) for x in range(2)])


class Rows:
    def __init__(self, own):
        self.own, self.half = own, own.shape[0] // 2
        self.first = (swap_x(own), swap_b(own))

    def second(self):
        from_x, from_b = self.first
        self.last = (swap_x(from_b[: self.half]), swap_b(from_x[self.half :]))

    def third(self):
        near = [self.own, *self.first, *self.last]
        return near + [swap_core(piece) for piece in near]


def gather_rows(own, beside=None):
    rows = Rows(own)
    if beside is not None:
        rows.first, beside = tie(rows.first, beside)
    rows.second()
    return rows.third() if beside is None else (rows.third(), beside)


class Sums:
    def __init__(self, near, far):
        r = near.shape[0] // 4
        self.half = r // 2

        def fold(block):
            return add16(near[block * r : (block + 1) * r], swap_core(far[block]))

        self.parts = (fold(3), fold(1), fold(2), fold(0))

    def second(self):
        both, for_x, for_b, _ = self.parts
        half = self.half
        self.got = (swap_x(both[:half]), swap_b(both[half:]), swap_x(for_x[:half]), swap_b(for_b[half:]))

    def third(self):
        _, for_x, for_b, own = self.parts
        top, bottom, x_top, b_bottom = self.got
        half = self.half
        x_bottom = swap_x(add16(for_x[half:], bottom))
        b_top = swap_b(add16(for_b[:half], top))
        own = own.astype(F32)
        return jnp.concatenate(
            [
                own[:half] + x_top.astype(F32) + b_top.astype(F32),
                own[half:] + b_bottom.astype(F32) + x_bottom.astype(F32),
            ],
            axis=0,
        )


    def second_x(self):
        self.got = swap_x(self.parts[0])

    def third_x(self, beside):
        _, for_x, for_b, own = self.parts
        for_b, for_x, beside = tie(add16(for_b, self.got), for_x, beside)
        return own.astype(F32) + swap_x(for_x).astype(F32) + swap_b(for_b).astype(F32), beside


def scatter_rows(near, far, beside=None):
    sums = Sums(near, far)
    sums.second()
    if beside is not None:
        sums.got, beside = tie(sums.got, beside)
    return sums.third() if beside is None else (sums.third(), beside)


def blocks_of(rows):
    r = rows.shape[0] // 4
    return [rows[k * r : (k + 1) * r] for k in range(4)]


def spread(pieces, axis=0):
    n = lax.axis_size("ctx")
    groups = [list(range(i, i + QUAD)) for i in range(0, n, QUAD)]
    return lax.all_to_all(pieces, "ctx", axis, axis, axis_index_groups=groups, tiled=True)


def sum_over_ctx(value, bit, end):
    while bit < end:
        value = value + swap_ctx(value, bit)
        bit *= 2
    return value


def dot(a, b):
    return jnp.dot(a, b, preferred_element_type=F32)


def dot_nt(a, b):
    return lax.dot_general(a, b, (((1,), (1,)), ((), ())), preferred_element_type=F32)


def dot_tn(a, b):
    return lax.dot_general(a, b, (((0,), (0,)), ((), ())), preferred_element_type=F32)


def rms_scale(values):
    return lax.rsqrt(jnp.mean(values * values, axis=-1, keepdims=True) + EPSILON)


def norm_back(values, scale, gain, grad):
    unit = values * scale
    inner = grad * gain
    d_values = scale * (inner - unit * jnp.mean(inner * unit, axis=-1, keepdims=True))
    return d_values, jnp.sum(grad * unit, axis=0)


def pick(refs, block, out_ref, at):
    r = refs[0].shape[0]
    for k in range(8):
        index = k // 4 * (len(refs) // 2) + k % 4

        @pl.when(block == k)
        def _():
            if k % 4 < 3 or len(refs) == 8:
                out_ref[at : at + r, :] = refs[index][...]
            else:
                out_ref[at : at + r // 2, :] = refs[index][...]
                out_ref[at + r // 2 : at + r, :] = refs[index + 1][...]


class Heads:
    def __init__(self, width, cos, sin):
        self.width, self.cos, self.sin = width, cos, sin
        lanes = 2 * width
        row = lax.broadcasted_iota(jnp.int32, (lanes, lanes), 0)
        col = lax.broadcasted_iota(jnp.int32, (lanes, lanes), 1)
        self.same = jnp.where(row // width == col // width, 1.0 / width, 0.0).astype(BF16)

    def mean(self, u):
        high = u.astype(BF16)
        low = (u - high.astype(F32)).astype(BF16)
        return dot(high, self.same) + dot(low, self.same)

    def swapped(self, u):
        half = self.width // 2
        lane = lax.broadcasted_iota(jnp.int32, u.shape, 1)
        return jnp.where((lane & half) == 0, pltpu.roll(u, 2 * self.width - half, 1), pltpu.roll(u, half, 1))

    def ready(self, u, gain):
        u = u * lax.rsqrt(self.mean(u * u) + EPSILON) * gain
        return u * self.cos + self.swapped(u) * self.sin

    def back(self, w, gain, grad):
        e = grad * self.cos - self.swapped(grad) * self.sin
        scale = lax.rsqrt(self.mean(w * w) + EPSILON)
        unit = w * scale
        inner = e * gain
        return scale * (inner - unit * self.mean(inner * unit)), jnp.sum(e * unit, axis=0, keepdims=True)


def project_kernel(table, *refs, heads, width):
    pieces, (w_ref, cos_ref, sin_ref, q_gain_ref, k_gain_ref, rows_ref, raw_ref, q_ref, kv_ref) = refs[:-9], refs[-9:]
    pick(pieces, pl.program_id(0), rows_ref, 0)
    raw = dot(rows_ref[...], w_ref[...])
    raw_ref[...] = raw
    math_of = Heads(width, cos_ref[...], sin_ref[...])
    lanes = 2 * width
    for c in range(heads // 2):
        cols = slice(c * lanes, (c + 1) * lanes)
        q_ref[:, cols] = math_of.ready(raw[:, cols], q_gain_ref[...]).astype(BF16)
    last = raw[:, heads * width :]
    lane = lax.broadcasted_iota(jnp.int32, last.shape, 1)
    kv_ref[...] = jnp.where(lane < width, math_of.ready(last, k_gain_ref[...]), last).astype(BF16)


def prep_back_kernel(
    table, raw_ref, cos_ref, sin_ref, q_gain_ref, k_gain_ref, dq_ref, dkv_ref, *refs, heads, width, plane
):
    halo, (out_ref, dg_ref) = refs[:-2], refs[-2:]
    t = pl.program_id(0)

    @pl.when(t == 0)
    def _():
        dg_ref[...] = jnp.zeros_like(dg_ref)

    math_of = Heads(width, cos_ref[...], sin_ref[...])
    lanes = 2 * width
    total = jnp.zeros((1, lanes), F32)
    for c in range(heads // 2):
        cols = slice(c * lanes, (c + 1) * lanes)
        dw, dg = math_of.back(raw_ref[:, cols], q_gain_ref[...], dq_ref[:, cols])
        out_ref[:, cols] = dw.astype(BF16)
        total = total + dg
    grad = dkv_ref[...]
    r = grad.shape[0]
    for ref in halo:
        missing = plane // r - ref.shape[0] // r
        at = pl.multiple_of(jnp.maximum(t - missing, 0) * r, r)
        grad = grad + jnp.where(t >= missing, ref[pl.ds(at, r), :].astype(F32), 0.0)
    dw, dg = math_of.back(raw_ref[:, heads * width :], k_gain_ref[...], grad)
    lane = lax.broadcasted_iota(jnp.int32, grad.shape, 1)
    out_ref[:, heads * width :] = jnp.where(lane < width, dw, grad).astype(BF16)
    dg_ref[0:1, :] += total
    dg_ref[1:2, :] += dg


def rows_dot_kernel(*refs):
    pieces, (w_ref, rows_ref, out_ref) = refs[:10], refs[10:]
    pick(pieces, pl.program_id(0), rows_ref, 0)
    out_ref[...] = dot(rows_ref[...], w_ref[...]).astype(BF16)


def stack_heads(block, heads, width):
    return jnp.concatenate([block[:, h * width : (h + 1) * width] for h in range(heads)], axis=0)


def attend_kernel(table, lo, hi, q_ref, start_ref, kv_ref, *refs, heads, width, base, bk, last):
    ones_v = refs[-1]
    if last:
        acc_in, o_ref, of_ref, stat_ref, acc = refs[:5]
    else:
        acc = refs[0]
    t = pl.program_id(0)
    r = q_ref.shape[0]

    @pl.when(t == 0)
    def _():
        lane = lax.broadcasted_iota(jnp.int32, kv_ref.shape, 1)
        ones_v[...] = jnp.where(lane < width, jnp.ones((), BF16), kv_ref[...])

    q = stack_heads(q_ref[...], heads, width)
    q = jnp.concatenate([q, jnp.zeros_like(q)], axis=-1)
    start = jnp.concatenate([start_ref[...]] * heads, axis=0)
    pos = base + t * r + lax.broadcasted_iota(jnp.int32, (r, 1), 0)
    pos = jnp.concatenate([pos] * heads, axis=0)
    acc[...] = acc_in[...] if last else jnp.zeros_like(acc)
    c = LOG2E / math.sqrt(width)

    def step(kb, carry):
        k0 = pl.multiple_of(kb * bk, bk)
        s = dot_nt(q, kv_ref[pl.ds(k0, bk), :])
        key = k0 + lax.broadcasted_iota(jnp.int32, (1, bk), 1)
        p = jnp.where((key >= start) & (key <= pos), jnp.exp2(s * c), 0.0)
        acc[...] += dot(p.astype(BF16), ones_v[pl.ds(k0, bk), :])
        return carry

    lax.fori_loop(lo[t], hi[t], step, 0)
    if last:
        total = acc[:, :1]
        o = acc[:, width:] / total
        stat_ref[...] = jnp.log2(total)
        for h in range(heads):
            part = o[h * r : (h + 1) * r]
            of_ref[:, h * width : (h + 1) * width] = part
            o_ref[:, h * width : (h + 1) * width] = part.astype(BF16)


def attend_back_kernel(
    table, lo, hi, q_ref, do_ref, of_ref, stat_ref, start_ref, kv_ref, *refs, heads, width, base, bk, last
):
    if last:
        acc_in, dq_ref, dkv, acc = refs
    else:
        acc, dkv_refs, dkv = refs[0], refs[1:-1], refs[-1]
    t = pl.program_id(0)
    r = q_ref.shape[0]

    @pl.when(t == 0)
    def _():
        dkv[...] = jnp.zeros_like(dkv)

    scale = 1.0 / math.sqrt(width)
    q = stack_heads(q_ref[...], heads, width)
    do = stack_heads(do_ref[...], heads, width)
    of = stack_heads(of_ref[...], heads, width)
    delta = jnp.sum(do.astype(F32) * of, axis=-1, keepdims=True)
    lane = lax.broadcasted_iota(jnp.int32, (heads * r, 2 * width), 1)
    rows = jnp.transpose(jnp.where(lane == 0, stat_ref[...], delta))
    stat, delta = rows[0:1, :], rows[1:2, :]
    q = jnp.concatenate([q, jnp.zeros_like(q)], axis=-1)
    q_scaled = (q.astype(F32) * scale).astype(BF16)
    do = jnp.concatenate([jnp.zeros_like(do), do], axis=-1)
    start = jnp.concatenate([start_ref[0]] * heads, axis=-1)
    pos = base + t * r + lax.broadcasted_iota(jnp.int32, (1, r), 1)
    pos = jnp.concatenate([pos] * heads, axis=-1)
    acc[...] = acc_in[...] if last else jnp.zeros_like(acc)

    def step(kb, carry):
        k0 = pl.multiple_of(kb * bk, bk)
        kv = kv_ref[pl.ds(k0, bk), :]
        s = dot_nt(kv, q_scaled)
        dp = dot_nt(kv, do)
        key = k0 + lax.broadcasted_iota(jnp.int32, (bk, 1), 0)
        p = jnp.where((key >= start) & (key <= pos), jnp.exp2(s * LOG2E - stat), 0.0)
        ds = (p * (dp - delta)).astype(BF16)
        dkv[pl.ds(k0, bk), :] += dot(ds, q_scaled) + dot(p.astype(BF16), do)
        acc[...] += dot_tn(ds, kv)
        return carry

    lax.fori_loop(lo[t], hi[t], step, 0)
    if last:
        dq = acc[...][:, :width] * scale
        for h in range(heads):
            dq_ref[:, h * width : (h + 1) * width] = dq[h * r : (h + 1) * r]
    else:

        @pl.when(t == pl.num_programs(0) - 1)
        def _():
            at = 0
            for ref in dkv_refs:
                ref[...] = dkv[at : at + ref.shape[0], :].astype(BF16)
                at += ref.shape[0]


def feed_first_kernel(*refs, hb):
    pieces, (c_ref, w_ref, hid_ref, dgu_ref, back_ref, rows_ref) = refs[:10], refs[10:]
    t = pl.program_id(0)
    r = pieces[0].shape[0]
    pick(pieces, 2 * t, rows_ref, 0)
    pick(pieces, 2 * t + 1, rows_ref, r)
    back_ref[...] = feed(rows_ref, c_ref, w_ref, hid_ref, dgu_ref, hb).astype(BF16)


def feed_last_kernel(a_ref, c_ref, w_ref, prev_ref, hid_ref, dgu_ref, near_ref, *far_refs, hb):
    t = pl.program_id(0)
    back = feed(a_ref, c_ref, w_ref, hid_ref, dgu_ref, hb) + prev_ref[...].astype(F32)
    split_store(back, t, near_ref, far_refs)


def feed(a_ref, c_ref, w_ref, hid_ref, dgu_ref, hb):
    a, c = a_ref[...], c_ref[...]
    gate, up = dot(a, w_ref[:, :hb]), dot(a, w_ref[:, hb : 2 * hb])
    d_hid = dot(c, w_ref[:, 2 * hb :])
    sig = jax.nn.sigmoid(gate)
    silu = gate * sig
    hid_ref[...] = (silu * up).astype(BF16)
    dgu_ref[:, :hb] = (d_hid * up * (sig * (1.0 + gate * (1.0 - sig)))).astype(BF16)
    dgu_ref[:, hb:] = (d_hid * silu).astype(BF16)
    return dot_nt(dgu_ref[...], w_ref[:, : 2 * hb])


def down_kernel(h0_ref, h1_ref, w0_ref, w1_ref, near_ref, *far_refs):
    t = pl.program_id(0)
    y = sum(dot_nt(h[...], w[:, 2 * h.shape[1] :]) for h, w in ((h0_ref, w0_ref), (h1_ref, w1_ref)))
    split_store(y, t, near_ref, far_refs)


def split_store(value, t, near_ref, far_refs):
    r = far_refs[0].shape[0]

    @pl.when(t < 2)
    def _():
        near_ref[...] = value.astype(BF16)

    for k, ref in enumerate(far_refs):

        @pl.when(t == 2 + k // 2)
        def _():
            ref[...] = value[k % 2 * r : (k % 2 + 1) * r].astype(BF16)


def split_outs(total, model):
    far = pl.BlockSpec((total // 8, model), lambda t: (0, 0))
    near = pl.BlockSpec((total // 4, model), lambda t: (jnp.minimum(t, 1), 0))
    return [((total // 2, model), BF16, near)] + [((total // 8, model), BF16, far)] * 4


def split_dot_kernel(a_ref, w_ref, near_ref, *far_refs):
    split_store(dot_nt(a_ref[...], w_ref[...]), pl.program_id(0), near_ref, far_refs)


def split_dot(a, w):
    total, cols = a.shape
    model = w.shape[0]
    near, *far = call(
        split_dot_kernel,
        4,
        0,
        [pl.BlockSpec((total // 4, cols), lambda t: (t, 0)), whole_block(w)],
        split_outs(total, model),
        [],
        (a, w),
        2 * total * model * cols,
        2 * total * (model + cols),
    )
    return near, far


def down_rows(h0, h1, w0, w1):
    total, hb = h0.shape[0], (h0.shape[1] + h1.shape[1]) // 2
    model = w0.shape[0]

    def row(h):
        return pl.BlockSpec((total // 4, h.shape[1]), lambda t: (t, 0))

    near, *far = call(
        down_kernel,
        4,
        0,
        [row(h0), row(h1), whole_block(w0), whole_block(w1)],
        split_outs(total, model),
        [],
        (h0, h1, w0, w1),
        4 * total * model * hb,
        2 * total * (model + 2 * hb) + 12 * model * hb,
    )
    return near, far


def whole_block(v):
    return pl.BlockSpec(v.shape, lambda t, *_: (0,) * len(v.shape), pipeline_mode=pl.Buffered(1))


def feed_forward(a, c, w, prev=None):
    total, model = c.shape
    rows = total // 4
    hb = w.shape[1] // 3

    def row(cols):
        return pl.BlockSpec((rows, cols), lambda t: (t, 0))

    outs = [((total, hb), BF16, row(hb)), ((total, 2 * hb), BF16, row(2 * hb))]
    if prev is None:
        kernel, args = feed_first_kernel, (*a, c, w)
        ins = [whole_block(piece) for piece in a] + [row(model), whole_block(w)]
        outs += [((total, model), BF16, row(model))] * 2
    else:
        kernel, args = feed_last_kernel, (a, c, w, prev)
        ins = [row(model), row(model), whole_block(w), row(model)]
        outs += split_outs(total, model)
    return call(
        functools.partial(kernel, hb=hb),
        4,
        0,
        ins,
        outs,
        [],
        args,
        12 * total * model * hb,
        2 * total * (4 * model + 3 * hb) + 6 * model * hb,
        total * hb,
    )


def pack_kernel(*refs, flip, widths, cuts):
    ins, outs = refs[: len(flip)], refs[len(flip) :]
    for quarter in range(QUAD):
        for out_ref, (low, high) in zip(outs, cuts):
            at = 0
            for ref, turned, width in zip(ins, flip, widths):
                start, end = low * width // high[1], high[0] * width // high[1]
                cut = slice(quarter * width + start, quarter * width + end)
                out_ref[quarter, :, at : at + end - start] = jnp.transpose(ref[cut, :]) if turned else ref[:, cut]
                at += end - start


def packed(weights, flip, cuts):
    rows = weights[0].shape[flip[0]]
    widths = [(w.shape[0] if f else w.shape[1]) // QUAD for w, f in zip(weights, flip)]
    shapes = [
        jax.ShapeDtypeStruct((QUAD, rows, sum((high - low) * w // of for w in widths)), BF16)
        for low, (high, of) in cuts
    ]
    return call(
        functools.partial(pack_kernel, flip=flip, widths=widths, cuts=cuts),
        1,
        0,
        [whole_block(w) for w in weights],
        [(shape.shape, BF16, whole_block(shape)) for shape in shapes],
        [],
        tuple(weights),
        1,
        sum(4 * math.prod(shape.shape) for shape in shapes),
    )


def unpack_kernel(*refs, flip, cuts):
    blocks, outs = refs[: len(cuts)], refs[len(cuts) :]
    for block, (low, high) in zip(blocks, cuts):
        at = 0
        for ref, turned in zip(outs, flip):
            width = (ref.shape[0] if turned else ref.shape[1]) // QUAD
            start, end = low * width // high[1], high[0] * width // high[1]
            for quarter in range(QUAD):
                part = block[quarter, :, at : at + end - start].astype(F32)
                cut = slice(quarter * width + start, quarter * width + end)
                if turned:
                    ref[cut, :] = jnp.transpose(part)
                else:
                    ref[:, cut] = part
            at += end - start


def unpacked(blocks, shapes, flip, cuts):
    return call(
        functools.partial(unpack_kernel, flip=flip, cuts=cuts),
        1,
        0,
        [whole_block(v) for v in blocks],
        [(shape, F32, whole_block(jax.ShapeDtypeStruct(shape, F32))) for shape in shapes],
        [],
        tuple(blocks),
        1,
        sum(6 * math.prod(v.shape) for v in blocks),
    )


def weights_kernel(a_ref, b_ref, c_ref, d_ref, *refs):
    out_ref = refs[-1]
    cols = b_ref.shape[1]
    first = dot_tn(a_ref[...], b_ref[...])
    out_ref[:, :cols] = first.astype(BF16)
    out_ref[:, cols:] = dot_tn(c_ref[...], d_ref[...]).astype(BF16)
    if len(refs) > 1:
        w_ref, sums_ref = refs[:2]
        both = first * w_ref[...].astype(F32)
        high = both.astype(BF16)
        low = (both - high.astype(F32)).astype(BF16)
        ones = jnp.ones((sums_ref.shape[0], cols), BF16)
        sums_ref[...] = dot_nt(ones, high) + dot_nt(ones, low)


def weight_grads(a, b, c, d, w=None, rows=512):
    total, model = a.shape
    cut = pl.BlockSpec((total, rows), lambda t: (0, t))

    def whole(v):
        return pl.BlockSpec(v.shape, lambda t: (0, 0), pipeline_mode=pl.Buffered(1))

    def tall(cols):
        return pl.BlockSpec((rows, cols), lambda t: (t, 0))

    cols = b.shape[1] + d.shape[1]
    more = [] if w is None else [w]
    return call(
        weights_kernel,
        model // rows,
        0,
        [cut, whole(b), cut, whole(d)] + [tall(v.shape[1]) for v in more],
        [((8, model), F32, pl.BlockSpec((8, rows), lambda t: (0, t)))] * len(more) + [((model, cols), BF16, tall(cols))],
        [],
        (a, b, c, d, *more),
        2 * total * model * cols,
        2 * (2 * total * model + (total + model) * cols),
    )


def call(kernel, blocks, prefetch, ins, outs, scratch, args, flops, nbytes, transcendentals=0):
    return pl.pallas_call(
        kernel,
        out_shape=[jax.ShapeDtypeStruct(shape, dtype) for shape, dtype, _ in outs],
        grid_spec=pltpu.PrefetchScalarGridSpec(
            num_scalar_prefetch=prefetch,
            grid=(blocks,),
            in_specs=ins,
            out_specs=[spec for _, _, spec in outs],
            scratch_shapes=scratch,
        ),
        compiler_params=pltpu.CompilerParams(
            dimension_semantics=("arbitrary",), vmem_limit_bytes=56 * 1024 * 1024
        ),
        cost_estimate=pl.CostEstimate(
            flops=int(flops), bytes_accessed=int(nbytes), transcendentals=int(transcendentals)
        ),
    )(*args)


def on_device(
    tokens,
    attn_gain,
    ffn_gain,
    query_norm_gain,
    k_gain,
    w_query,
    key_projection,
    value_projection,
    w_out,
    w_gate,
    w_up,
    w_down,
    doc_start,
    cotangent,
):
    i, x = lax.axis_index("ctx"), lax.axis_index("tp")
    n = lax.axis_size("ctx") // QUAD
    line, b, core = i // QUAD, (i // 2) % 2, i % 2
    r, model = tokens.shape
    plane = 2 * QUAD * r
    width = query_norm_gain.shape[0]
    heads = w_query.shape[1] // QUAD // width
    qw = heads * width
    hidden = w_gate.shape[1] // QUAD
    step = model // n
    reach = WB * doc_start.shape[0]

    (sent,) = packed((w_query, key_projection, value_projection, w_out), (0, 0, 0, 1), [(0, (1, 1))])
    sent, tokens = tie(spread(sent), tokens)
    w_attn = line_gather(sent.reshape(step, -1), n)
    w_qkv, w_o = w_attn[:, : qw + 2 * width], w_attn[:, qw + 2 * width :]
    x_own = tokens.astype(F32)
    scale_1 = rms_scale(x_own)

    cut = FIRST_BLOCK
    ffn_cuts = [(0, (cut, 8)), (cut, (8, 8))]
    ffn_pieces = packed((w_gate, w_up, w_down), (0, 0, 1), ffn_cuts)
    a_own = (x_own * scale_1 * attn_gain).astype(BF16)
    a_near = (swap_x(a_own), swap_b(a_own), swap_both(a_own))

    near_core, near_b = swap_core(doc_start), swap_b(doc_start)
    far = swap_core(near_b)
    rows0 = [jnp.where(core == c, doc_start, near_core) for c in range(2)]
    rows1 = [jnp.where(core == c, near_b, far) for c in range(2)]
    starts = jnp.concatenate([jnp.where(b == y, rows0[c], rows1[c]) for y in range(2) for c in range(2)])
    first = line * plane
    relative = first + jnp.arange(plane, dtype=jnp.int32) - starts
    inv_freq = jnp.power(ROPE_BASE, -2.0 * jnp.arange(width // 2, dtype=F32) / width)
    angles = relative.astype(F32)[:, None] * inv_freq[None, :]
    cos, sin = jnp.cos(angles), jnp.sin(angles)
    cos = jnp.concatenate([cos] * 4, axis=-1)
    sin = jnp.concatenate([-sin, sin] * 2, axis=-1)
    sent_0 = spread(ffn_pieces[0])
    w_ffn_0 = line_gather(sent_0.reshape(step, -1), n)
    a_near, cos, sin, pieces_1, _ = tie(a_near, cos, sin, ffn_pieces[1], sent_0)
    sent_1 = spread(pieces_1)
    a_pieces = [a_own, *a_near]
    a_pieces = a_pieces + [swap_core(piece) for piece in a_pieces]

    blocks = jnp.arange(2 * QUAD, dtype=jnp.int32)
    table = (
        ((((blocks >> 1) & 1) ^ core) << 2) | (((blocks >> 2) ^ b) << 1) | ((blocks & 1) ^ x)
    ).astype(jnp.int32)
    inverse = (
        ((((blocks >> 1) & 1) ^ b) << 2) | (((blocks >> 2) ^ core) << 1) | ((blocks & 1) ^ x)
    ).astype(jnp.int32)
    nb = 2 * QUAD

    def key_range(base, keys):
        local = starts - (first - base)
        low = jnp.clip(local[::r] // KEY_BLOCK, 0, keys // KEY_BLOCK)
        high = jnp.clip((base + (blocks + 1) * r - 1) // KEY_BLOCK + 1, low, keys // KEY_BLOCK)
        return local, low, high

    own_part, halo_part = key_range(0, plane), key_range(reach, reach)

    gain_1, gain_2 = attn_gain, ffn_gain

    def here(cols):
        return pl.BlockSpec((r, cols), lambda t, *_: (t, 0))

    def moved(cols):
        return pl.BlockSpec((r, cols), lambda t, table, *_: (table[t], 0))

    lanes = 2 * width
    two = lambda gain: jnp.concatenate([gain, gain])[None, :]
    q_gain, key_gain = two(query_norm_gain), two(k_gain)
    a_one, raw, q, kv = call(
        functools.partial(project_kernel, heads=heads, width=width),
        nb,
        1,
        [whole_block(piece) for piece in a_pieces]
        + [whole_block(w_qkv), moved(lanes), moved(lanes), whole_block(q_gain), whole_block(key_gain)],
        [
            ((plane, model), BF16, here(model)),
            ((plane, qw + lanes), F32, here(qw + lanes)),
            ((plane, qw), BF16, moved(qw)),
            ((plane, lanes), BF16, moved(lanes)),
        ],
        [],
        (inverse, *a_pieces, w_qkv, cos, sin, q_gain, key_gain),
        2 * plane * model * (qw + lanes),
        plane * (4 * model + 10 * qw),
    )
    q, kv, sent_1, cot_own = tie(q, kv, sent_1, cotangent)
    w_ffn_1 = line_gather(sent_1.reshape(step, -1), n)
    spans = []
    left, distance = reach, 1
    while left > 0:
        spans.append((distance, min(left, plane)))
        left -= plane
        distance += 1
    halo = [line_move(kv[plane - rows :], d, range(0, max(n - d, 0))) for d, rows in spans]
    attn_flops = plane * heads * (plane // 2 + 2 * KEY_BLOCK) * width
    stacked = pl.BlockSpec((heads * r, 1), lambda t, *_: (t, 0))
    sums = ((plane * heads, lanes), F32, pl.BlockSpec((heads * r, lanes), lambda t, *_: (t, 0)))

    def attend(part, base, keys, *acc):
        local, low, high = part
        outs = [((plane, qw), BF16, moved(qw)), ((plane, qw), F32, here(qw)), ((plane * heads, 1), F32, stacked)]
        return call(
            functools.partial(attend_kernel, heads=heads, width=width, base=base, bk=KEY_BLOCK, last=len(acc)),
            nb,
            3,
            [here(qw), pl.BlockSpec((r, 1), lambda t, *_: (t, 0)), whole_block(keys)] + [sums[2]] * len(acc),
            outs if acc else [sums],
            [pltpu.VMEM((heads * r, lanes), F32)] * len(acc) + [pltpu.VMEM(keys.shape, BF16)],
            (table, low, high, q, local[:, None], keys, *acc),
            8 * attn_flops,
            plane * qw * 10,
        )

    (acc,) = attend(own_part, 0, kv)
    cot = Rows(cot_own)
    acc, halo, cot.first = tie(acc, halo, cot.first)
    cot.second()
    halo_keys = jnp.concatenate(halo[::-1], axis=0)
    o, o_float, stat = attend(halo_part, reach, halo_keys, acc)

    half = plane // 2
    o, cot.last = tie(o, cot.last)

    attn_sum, cot = scatter_rows(*split_dot(o, w_o), jnp.concatenate(cot.third(), axis=0))
    resid = x_own + attn_sum
    scale_2 = rms_scale(resid)
    a_pieces = gather_rows((resid * scale_2 * gain_2).astype(BF16))

    hid_0, d_gu_0, back, a_two = feed_forward(a_pieces, cot, w_ffn_0)
    (ffn_grad_0,) = weight_grads(a_two, d_gu_0, cot, hid_0)
    w_ffn_1, _ = tie(w_ffn_1, ffn_grad_0)
    ffn_grad_0 = line_scatter(ffn_grad_0, n)
    hid_1, d_gu_1, near, *far = feed_forward(a_two, cot, w_ffn_1, back)
    d_two, ffn_grad_1 = scatter_rows(near, far, weight_grads(a_two, d_gu_1, cot, hid_1)[0])
    ffn_grad_1 = line_scatter(ffn_grad_1, n)
    d_res, d_ffn_gain = norm_back(resid, scale_2, gain_2, d_two)
    d_h = cotangent.astype(F32) + d_res

    h_pieces, down = gather_rows(d_h.astype(BF16), down_rows(hid_0, hid_1, w_ffn_0, w_ffn_1))
    ffn_sum = Sums(*down)

    def home(grad):
        return spread(grad.reshape(QUAD, step // QUAD, -1))

    d_h_rows, d_o = call(
        rows_dot_kernel,
        nb,
        0,
        [whole_block(piece) for piece in h_pieces] + [whole_block(w_o)],
        [((plane, model), BF16, here(model)), ((plane, qw), BF16, here(qw))],
        [],
        (*h_pieces, w_o),
        2 * plane * model * qw,
        4 * plane * model,
    )
    d_o, ffn_sum.parts = tie(d_o, ffn_sum.parts)
    ffn_sum.second()

    def attend_back(part, base, keys, *acc):
        local, low, high = part
        if acc:
            outs = [((plane, qw), F32, here(qw)), (keys.shape, F32, pl.BlockSpec(keys.shape, lambda t, *_: (0, 0)))]
            scratch = pltpu.VMEM((heads * r, lanes), F32)
        else:
            outs = [sums] + [
                ((rows, lanes), BF16, pl.BlockSpec((rows, lanes), lambda t, *_: (0, 0))) for _, rows in spans[::-1]
            ]
            scratch = pltpu.VMEM(keys.shape, F32)
        return call(
            functools.partial(
                attend_back_kernel, heads=heads, width=width, base=base, bk=KEY_BLOCK, last=len(acc)
            ),
            nb,
            3,
            [
                here(qw),
                moved(qw),
                here(qw),
                stacked,
                pl.BlockSpec((1, 1, r), lambda t, *_: (t, 0, 0)),
                whole_block(keys),
            ]
            + [sums[2]] * len(acc),
            outs,
            [scratch],
            (table, low, high, q, d_o, o_float, stat, local.reshape(nb, 1, r), keys, *acc),
            20 * attn_flops,
            plane * qw * 12,
        )

    acc, *halo_grads = attend_back(halo_part, reach, halo_keys)
    acc, halo_grads, ffn_sum.got, ffn_grad_0 = tie(acc, halo_grads, ffn_sum.got, ffn_grad_0)
    back_0 = home(ffn_grad_0)
    returned = [line_move(g, -d, range(d, n)) for g, (d, _) in zip(halo_grads[::-1], spans)]
    dq, dkv = attend_back(own_part, 0, kv, acc)
    dq, back_0, returned = tie(dq, back_0, returned)
    d_raw, d_head_gains = call(
        functools.partial(prep_back_kernel, heads=heads, width=width, plane=plane),
        nb,
        1,
        [moved(qw + lanes), here(lanes), here(lanes), whole_block(q_gain), whole_block(key_gain), here(qw), here(lanes)]
        + [whole_block(g) for g in returned],
        [
            ((plane, qw + lanes), BF16, moved(qw + lanes)),
            ((8, lanes), F32, pl.BlockSpec((8, lanes), lambda t, *_: (0, 0))),
        ],
        [],
        (table, raw, cos, sin, q_gain, key_gain, dq, dkv, *returned),
        plane * (qw + width) * 20,
        plane * (qw + 2 * width) * 10,
    )
    one = split_dot(d_raw, w_qkv)
    d_raw, one = tie(d_raw, one)
    one = Sums(*one)
    gain_sums, attn_grad = weight_grads(a_one, d_raw, d_h_rows, o, w_qkv)
    gain_sums = gain_sums[0]
    attn_grad = line_scatter(attn_grad, n)
    gain_sums, ffn_grad_1 = tie(gain_sums, ffn_grad_1)
    one.parts, gain_sums, ffn_sum.got = tie(one.parts, gain_sums, ffn_sum.got)
    one.second_x()
    back_1 = home(ffn_grad_1)
    out_tokens = (resid + ffn_sum.third()).astype(BF16)
    d_one, (back_1, out_tokens) = one.third_x((back_1, out_tokens))
    ffn_outs = unpacked((back_0, back_1), [v.shape for v in (w_gate, w_up, w_down)], (0, 0, 1), ffn_cuts)
    d_one, ffn_outs, gain_sums = tie(d_one, ffn_outs, gain_sums)
    d_attn_gain = gain_sums / gain_1
    d_q_gain = d_head_gains[0, :width] + d_head_gains[0, width:]
    gains = jnp.concatenate([d_attn_gain, d_ffn_gain, d_q_gain, d_head_gains[1, :width]])
    gains = sum_over_ctx(gains + swap_x(gains), 1, QUAD)
    d_x, _ = norm_back(x_own, scale_1, gain_1, d_one)
    d_tokens = d_h + d_x

    attn_grad, back_1 = tie(attn_grad, back_1)
    attn_back = home(attn_grad)
    attn_back, gains = tie(attn_back, gains)
    gains = sum_over_ctx(gains, QUAD, QUAD * n)
    attn_outs = unpacked(
        [attn_back],
        [v.shape for v in (w_query, key_projection, value_projection, w_out)],
        (0, 0, 0, 1),
        [(0, (1, 1))],
    )
    return (
        out_tokens,
        d_tokens,
        gains[:model],
        gains[model : 2 * model],
        gains[2 * model : 2 * model + width],
        gains[2 * model + width :],
        *attn_outs,
        *ffn_outs,
    )


def solution(mesh):
    return jax.shard_map(
        on_device,
        mesh=mesh,
        in_specs=(
            P(("ctx", "tp"), None),
            P(),
            P(),
            P(),
            P(),
            P("ctx", "tp"),
            P("ctx", "tp"),
            P("ctx", "tp"),
            P("tp", "ctx"),
            P("ctx", "tp"),
            P("ctx", "tp"),
            P("tp", "ctx"),
            P("ctx"),
            P(("ctx", "tp"), None),
        ),
        out_specs=(
            P(("ctx", "tp"), None),
            P(("ctx", "tp"), None),
            P(),
            P(),
            P(),
            P(),
            P("ctx", "tp"),
            P("ctx", "tp"),
            P("ctx", "tp"),
            P("tp", "ctx"),
            P("ctx", "tp"),
            P("ctx", "tp"),
            P("tp", "ctx"),
        ),
        check_vma=False,
    )
```

```python
import functools
import math

import jax
import jax.numpy as jnp
from jax import lax
from jax.experimental import pallas as pl
from jax.experimental.pallas import tpu as pltpu
from jax.sharding import PartitionSpec as P

WB = 6
EPSILON = 1e-05
ROPE_BASE = 1000000.0
LOG2E = math.log2(math.e)

QUAD = 4
KEY_BLOCK = 384
FIRST_BLOCK = 4

F32 = jnp.float32
BF16 = jnp.bfloat16


def swap_ctx(value, bit):
    n = lax.axis_size("ctx")
    return lax.ppermute(value, "ctx", [(i, i ^ bit) for i in range(n)])


def swap_core(value):
    return swap_ctx(value, 1)


def swap_b(value):
    return swap_ctx(value, 2)


def swap_x(value):
    return lax.ppermute(value, "tp", [(0, 1), (1, 0)])


def line_move(value, by, sources):
    pairs = [(s * QUAD + q, (s + by) * QUAD + q) for s in sources for q in range(QUAD)]
    return lax.ppermute(value, "ctx", pairs)


def line_groups(n):
    return [[p * QUAD + q for p in range(n)] for q in range(QUAD)]


def line_gather(own, n):
    return lax.all_gather(own, "ctx", axis=0, axis_index_groups=line_groups(n), tiled=True)


def line_scatter(partial, n):
    return lax.psum_scatter(partial, "ctx", scatter_dimension=0, axis_index_groups=line_groups(n), tiled=True)


def line_move(value, by, sources):
    pairs = [(s * QUAD + q, (s + by) * QUAD + q) for s in sources for q in range(QUAD)]
    return lax.ppermute(value, "ctx", pairs)


def tie(*values):
    return lax.optimization_barrier(values)


def add16(a, b):
    return (a.astype(F32) + b.astype(F32)).astype(BF16)


def swap_both(value):
    n = lax.axis_size("ctx")
    return lax.ppermute(value, ("ctx", "tp"), [(2 * i + x, 2 * (i ^ 2) + 1 - x) for i in range(n) for x in range(2)])


class Rows:
    def __init__(self, own):
        self.own, self.half = own, own.shape[0] // 2
        self.first = (swap_x(own), swap_b(own))

    def second(self):
        from_x, from_b = self.first
        self.last = (swap_x(from_b[: self.half]), swap_b(from_x[self.half :]))

    def third(self):
        near = [self.own, *self.first, *self.last]
        return near + [swap_core(piece) for piece in near]


def gather_rows(own, beside=None):
    rows = Rows(own)
    if beside is not None:
        rows.first, beside = tie(rows.first, beside)
    rows.second()
    return rows.third() if beside is None else (rows.third(), beside)


class Sums:
    def __init__(self, near, far):
        r = near.shape[0] // 4
        self.half = r // 2

        def fold(block):
            return add16(near[block * r : (block + 1) * r], swap_core(far[block]))

        self.parts = (fold(3), fold(1), fold(2), fold(0))

    def second(self):
        both, for_x, for_b, _ = self.parts
        half = self.half
        self.got = (swap_x(both[:half]), swap_b(both[half:]), swap_x(for_x[:half]), swap_b(for_b[half:]))

    def third(self):
        _, for_x, for_b, own = self.parts
        top, bottom, x_top, b_bottom = self.got
        half = self.half
        x_bottom = swap_x(add16(for_x[half:], bottom))
        b_top = swap_b(add16(for_b[:half], top))
        own = own.astype(F32)
        return jnp.concatenate(
            [
                own[:half] + x_top.astype(F32) + b_top.astype(F32),
                own[half:] + b_bottom.astype(F32) + x_bottom.astype(F32),
            ],
            axis=0,
        )


    def second_x(self):
        self.got = swap_x(self.parts[0])

    def third_x(self, beside):
        _, for_x, for_b, own = self.parts
        for_b, for_x, beside = tie(add16(for_b, self.got), for_x, beside)
        return own.astype(F32) + swap_x(for_x).astype(F32) + swap_b(for_b).astype(F32), beside


def scatter_rows(near, far, beside=None):
    sums = Sums(near, far)
    sums.second()
    if beside is not None:
        sums.got, beside = tie(sums.got, beside)
    return sums.third() if beside is None else (sums.third(), beside)


def blocks_of(rows):
    r = rows.shape[0] // 4
    return [rows[k * r : (k + 1) * r] for k in range(4)]


def spread(pieces, axis=0):
    n = lax.axis_size("ctx")
    groups = [list(range(i, i + QUAD)) for i in range(0, n, QUAD)]
    return lax.all_to_all(pieces, "ctx", axis, axis, axis_index_groups=groups, tiled=True)


def sum_over_ctx(value, bit, end):
    while bit < end:
        value = value + swap_ctx(value, bit)
        bit *= 2
    return value


def dot(a, b):
    return jnp.dot(a, b, preferred_element_type=F32)


def dot_nt(a, b):
    return lax.dot_general(a, b, (((1,), (1,)), ((), ())), preferred_element_type=F32)


def dot_tn(a, b):
    return lax.dot_general(a, b, (((0,), (0,)), ((), ())), preferred_element_type=F32)


def rms_scale(values):
    return lax.rsqrt(jnp.mean(values * values, axis=-1, keepdims=True) + EPSILON)


def norm_back(values, scale, gain, grad):
    unit = values * scale
    inner = grad * gain
    d_values = scale * (inner - unit * jnp.mean(inner * unit, axis=-1, keepdims=True))
    return d_values, jnp.sum(grad * unit, axis=0)


def pick(refs, block, out_ref, at):
    r = refs[0].shape[0]
    for k in range(8):
        index = k // 4 * (len(refs) // 2) + k % 4

        @pl.when(block == k)
        def _():
            if k % 4 < 3 or len(refs) == 8:
                out_ref[at : at + r, :] = refs[index][...]
            else:
                out_ref[at : at + r // 2, :] = refs[index][...]
                out_ref[at + r // 2 : at + r, :] = refs[index + 1][...]


class Heads:
    def __init__(self, width, cos, sin):
        self.width, self.cos, self.sin = width, cos, sin
        lanes = 2 * width
        row = lax.broadcasted_iota(jnp.int32, (lanes, lanes), 0)
        col = lax.broadcasted_iota(jnp.int32, (lanes, lanes), 1)
        self.same = jnp.where(row // width == col // width, 1.0 / width, 0.0).astype(BF16)

    def mean(self, u):
        high = u.astype(BF16)
        low = (u - high.astype(F32)).astype(BF16)
        return dot(high, self.same) + dot(low, self.same)

    def swapped(self, u):
        half = self.width // 2
        lane = lax.broadcasted_iota(jnp.int32, u.shape, 1)
        return jnp.where((lane & half) == 0, pltpu.roll(u, 2 * self.width - half, 1), pltpu.roll(u, half, 1))

    def ready(self, u, gain):
        u = u * lax.rsqrt(self.mean(u * u) + EPSILON) * gain
        return u * self.cos + self.swapped(u) * self.sin

    def back(self, w, gain, grad):
        e = grad * self.cos - self.swapped(grad) * self.sin
        scale = lax.rsqrt(self.mean(w * w) + EPSILON)
        unit = w * scale
        inner = e * gain
        return scale * (inner - unit * self.mean(inner * unit)), jnp.sum(e * unit, axis=0, keepdims=True)


def project_kernel(table, *refs, heads, width):
    pieces, (w_ref, cos_ref, sin_ref, q_gain_ref, k_gain_ref, rows_ref, raw_ref, q_ref, kv_ref) = refs[:-9], refs[-9:]
    pick(pieces, pl.program_id(0), rows_ref, 0)
    raw = dot(rows_ref[...], w_ref[...])
    raw_ref[...] = raw
    math_of = Heads(width, cos_ref[...], sin_ref[...])
    lanes = 2 * width
    for c in range(heads // 2):
        cols = slice(c * lanes, (c + 1) * lanes)
        q_ref[:, cols] = math_of.ready(raw[:, cols], q_gain_ref[...]).astype(BF16)
    last = raw[:, heads * width :]
    lane = lax.broadcasted_iota(jnp.int32, last.shape, 1)
    kv_ref[...] = jnp.where(lane < width, math_of.ready(last, k_gain_ref[...]), last).astype(BF16)


def prep_back_kernel(
    table, raw_ref, cos_ref, sin_ref, q_gain_ref, k_gain_ref, dq_ref, dkv_ref, *refs, heads, width, plane
):
    halo, (out_ref, dg_ref) = refs[:-2], refs[-2:]
    t = pl.program_id(0)

    @pl.when(t == 0)
    def _():
        dg_ref[...] = jnp.zeros_like(dg_ref)

    math_of = Heads(width, cos_ref[...], sin_ref[...])
    lanes = 2 * width
    total = jnp.zeros((1, lanes), F32)
    for c in range(heads // 2):
        cols = slice(c * lanes, (c + 1) * lanes)
        dw, dg = math_of.back(raw_ref[:, cols], q_gain_ref[...], dq_ref[:, cols])
        out_ref[:, cols] = dw.astype(BF16)
        total = total + dg
    grad = dkv_ref[...]
    r = grad.shape[0]
    for ref in halo:
        missing = plane // r - ref.shape[0] // r
        at = pl.multiple_of(jnp.maximum(t - missing, 0) * r, r)
        grad = grad + jnp.where(t >= missing, ref[pl.ds(at, r), :].astype(F32), 0.0)
    dw, dg = math_of.back(raw_ref[:, heads * width :], k_gain_ref[...], grad)
    lane = lax.broadcasted_iota(jnp.int32, grad.shape, 1)
    out_ref[:, heads * width :] = jnp.where(lane < width, dw, grad).astype(BF16)
    dg_ref[0:1, :] += total
    dg_ref[1:2, :] += dg


def rows_dot_kernel(*refs):
    pieces, (w_ref, rows_ref, out_ref) = refs[:10], refs[10:]
    pick(pieces, pl.program_id(0), rows_ref, 0)
    out_ref[...] = dot(rows_ref[...], w_ref[...]).astype(BF16)


def stack_heads(block, heads, width):
    return jnp.concatenate([block[:, h * width : (h + 1) * width] for h in range(heads)], axis=0)


def attend_kernel(table, lo, hi, q_ref, start_ref, kv_ref, *refs, heads, width, base, bk, last):
    ones_v = refs[-1]
    if last:
        acc_in, o_ref, of_ref, stat_ref, acc = refs[:5]
    else:
        acc = refs[0]
    t = pl.program_id(0)
    r = q_ref.shape[0]

    @pl.when(t == 0)
    def _():
        lane = lax.broadcasted_iota(jnp.int32, kv_ref.shape, 1)
        ones_v[...] = jnp.where(lane < width, jnp.ones((), BF16), kv_ref[...])

    q = stack_heads(q_ref[...], heads, width)
    q = jnp.concatenate([q, jnp.zeros_like(q)], axis=-1)
    start = jnp.concatenate([start_ref[...]] * heads, axis=0)
    pos = base + t * r + lax.broadcasted_iota(jnp.int32, (r, 1), 0)
    pos = jnp.concatenate([pos] * heads, axis=0)
    acc[...] = acc_in[...] if last else jnp.zeros_like(acc)
    c = LOG2E / math.sqrt(width)

    def step(kb, carry):
        k0 = pl.multiple_of(kb * bk, bk)
        s = dot_nt(q, kv_ref[pl.ds(k0, bk), :])
        key = k0 + lax.broadcasted_iota(jnp.int32, (1, bk), 1)
        p = jnp.where((key >= start) & (key <= pos), jnp.exp2(s * c), 0.0)
        acc[...] += dot(p.astype(BF16), ones_v[pl.ds(k0, bk), :])
        return carry

    lax.fori_loop(lo[t], hi[t], step, 0)
    if last:
        total = acc[:, :1]
        o = acc[:, width:] / total
        stat_ref[...] = jnp.log2(total)
        for h in range(heads):
            part = o[h * r : (h + 1) * r]
            of_ref[:, h * width : (h + 1) * width] = part
            o_ref[:, h * width : (h + 1) * width] = part.astype(BF16)


def attend_back_kernel(
    table, lo, hi, q_ref, do_ref, of_ref, stat_ref, start_ref, kv_ref, *refs, heads, width, base, bk, last
):
    if last:
        acc_in, dq_ref, dkv, acc = refs
    else:
        acc, dkv_refs, dkv = refs[0], refs[1:-1], refs[-1]
    t = pl.program_id(0)
    r = q_ref.shape[0]

    @pl.when(t == 0)
    def _():
        dkv[...] = jnp.zeros_like(dkv)

    scale = 1.0 / math.sqrt(width)
    q = stack_heads(q_ref[...], heads, width)
    do = stack_heads(do_ref[...], heads, width)
    of = stack_heads(of_ref[...], heads, width)
    delta = jnp.sum(do.astype(F32) * of, axis=-1, keepdims=True)
    lane = lax.broadcasted_iota(jnp.int32, (heads * r, 2 * width), 1)
    rows = jnp.transpose(jnp.where(lane == 0, stat_ref[...], delta))
    stat, delta = rows[0:1, :], rows[1:2, :]
    q = jnp.concatenate([q, jnp.zeros_like(q)], axis=-1)
    q_scaled = (q.astype(F32) * scale).astype(BF16)
    do = jnp.concatenate([jnp.zeros_like(do), do], axis=-1)
    start = jnp.concatenate([start_ref[0]] * heads, axis=-1)
    pos = base + t * r + lax.broadcasted_iota(jnp.int32, (1, r), 1)
    pos = jnp.concatenate([pos] * heads, axis=-1)
    acc[...] = acc_in[...] if last else jnp.zeros_like(acc)

    def step(kb, carry):
        k0 = pl.multiple_of(kb * bk, bk)
        kv = kv_ref[pl.ds(k0, bk), :]
        s = dot_nt(kv, q_scaled)
        dp = dot_nt(kv, do)
        key = k0 + lax.broadcasted_iota(jnp.int32, (bk, 1), 0)
        p = jnp.where((key >= start) & (key <= pos), jnp.exp2(s * LOG2E - stat), 0.0)
        ds = (p * (dp - delta)).astype(BF16)
        dkv[pl.ds(k0, bk), :] += dot(ds, q_scaled) + dot(p.astype(BF16), do)
        acc[...] += dot_tn(ds, kv)
        return carry

    lax.fori_loop(lo[t], hi[t], step, 0)
    if last:
        dq = acc[...][:, :width] * scale
        for h in range(heads):
            dq_ref[:, h * width : (h + 1) * width] = dq[h * r : (h + 1) * r]
    else:

        @pl.when(t == pl.num_programs(0) - 1)
        def _():
            at = 0
            for ref in dkv_refs:
                ref[...] = dkv[at : at + ref.shape[0], :].astype(BF16)
                at += ref.shape[0]


def feed_first_kernel(*refs, hb):
    pieces, (c_ref, w_ref, hid_ref, dgu_ref, back_ref, rows_ref) = refs[:10], refs[10:]
    t = pl.program_id(0)
    r = pieces[0].shape[0]
    pick(pieces, 2 * t, rows_ref, 0)
    pick(pieces, 2 * t + 1, rows_ref, r)
    back_ref[...] = feed(rows_ref, c_ref, w_ref, hid_ref, dgu_ref, hb).astype(BF16)


def feed_last_kernel(a_ref, c_ref, w_ref, prev_ref, hid_ref, dgu_ref, near_ref, *far_refs, hb):
    t = pl.program_id(0)
    back = feed(a_ref, c_ref, w_ref, hid_ref, dgu_ref, hb) + prev_ref[...].astype(F32)
    split_store(back, t, near_ref, far_refs)


def feed(a_ref, c_ref, w_ref, hid_ref, dgu_ref, hb):
    a, c = a_ref[...], c_ref[...]
    gate, up = dot(a, w_ref[:, :hb]), dot(a, w_ref[:, hb : 2 * hb])
    d_hid = dot(c, w_ref[:, 2 * hb :])
    sig = jax.nn.sigmoid(gate)
    silu = gate * sig
    hid_ref[...] = (silu * up).astype(BF16)
    dgu_ref[:, :hb] = (d_hid * up * (sig * (1.0 + gate * (1.0 - sig)))).astype(BF16)
    dgu_ref[:, hb:] = (d_hid * silu).astype(BF16)
    return dot_nt(dgu_ref[...], w_ref[:, : 2 * hb])


def down_kernel(h0_ref, h1_ref, w0_ref, w1_ref, near_ref, *far_refs):
    t = pl.program_id(0)
    y = sum(dot_nt(h[...], w[:, 2 * h.shape[1] :]) for h, w in ((h0_ref, w0_ref), (h1_ref, w1_ref)))
    split_store(y, t, near_ref, far_refs)


def split_store(value, t, near_ref, far_refs):
    r = far_refs[0].shape[0]

    @pl.when(t < 2)
    def _():
        near_ref[...] = value.astype(BF16)

    for k, ref in enumerate(far_refs):

        @pl.when(t == 2 + k // 2)
        def _():
            ref[...] = value[k % 2 * r : (k % 2 + 1) * r].astype(BF16)


def split_outs(total, model):
    far = pl.BlockSpec((total // 8, model), lambda t: (0, 0))
    near = pl.BlockSpec((total // 4, model), lambda t: (jnp.minimum(t, 1), 0))
    return [((total // 2, model), BF16, near)] + [((total // 8, model), BF16, far)] * 4


def split_dot_kernel(a_ref, w_ref, near_ref, *far_refs):
    split_store(dot_nt(a_ref[...], w_ref[...]), pl.program_id(0), near_ref, far_refs)


def split_dot(a, w):
    total, cols = a.shape
    model = w.shape[0]
    near, *far = call(
        split_dot_kernel,
        4,
        0,
        [pl.BlockSpec((total // 4, cols), lambda t: (t, 0)), whole_block(w)],
        split_outs(total, model),
        [],
        (a, w),
        2 * total * model * cols,
        2 * total * (model + cols),
    )
    return near, far


def down_rows(h0, h1, w0, w1):
    total, hb = h0.shape[0], (h0.shape[1] + h1.shape[1]) // 2
    model = w0.shape[0]

    def row(h):
        return pl.BlockSpec((total // 4, h.shape[1]), lambda t: (t, 0))

    near, *far = call(
        down_kernel,
        4,
        0,
        [row(h0), row(h1), whole_block(w0), whole_block(w1)],
        split_outs(total, model),
        [],
        (h0, h1, w0, w1),
        4 * total * model * hb,
        2 * total * (model + 2 * hb) + 12 * model * hb,
    )
    return near, far


def whole_block(v):
    return pl.BlockSpec(v.shape, lambda t, *_: (0,) * len(v.shape), pipeline_mode=pl.Buffered(1))


def feed_forward(a, c, w, prev=None):
    total, model = c.shape
    rows = total // 4
    hb = w.shape[1] // 3

    def row(cols):
        return pl.BlockSpec((rows, cols), lambda t: (t, 0))

    outs = [((total, hb), BF16, row(hb)), ((total, 2 * hb), BF16, row(2 * hb))]
    if prev is None:
        kernel, args = feed_first_kernel, (*a, c, w)
        ins = [whole_block(piece) for piece in a] + [row(model), whole_block(w)]
        outs += [((total, model), BF16, row(model))] * 2
    else:
        kernel, args = feed_last_kernel, (a, c, w, prev)
        ins = [row(model), row(model), whole_block(w), row(model)]
        outs += split_outs(total, model)
    return call(
        functools.partial(kernel, hb=hb),
        4,
        0,
        ins,
        outs,
        [],
        args,
        12 * total * model * hb,
        2 * total * (4 * model + 3 * hb) + 6 * model * hb,
        total * hb,
    )


def pack_kernel(*refs, flip, widths, cuts):
    ins, outs = refs[: len(flip)], refs[len(flip) :]
    for quarter in range(QUAD):
        for out_ref, (low, high) in zip(outs, cuts):
            at = 0
            for ref, turned, width in zip(ins, flip, widths):
                start, end = low * width // high[1], high[0] * width // high[1]
                cut = slice(quarter * width + start, quarter * width + end)
                out_ref[quarter, :, at : at + end - start] = jnp.transpose(ref[cut, :]) if turned else ref[:, cut]
                at += end - start


def packed(weights, flip, cuts):
    rows = weights[0].shape[flip[0]]
    widths = [(w.shape[0] if f else w.shape[1]) // QUAD for w, f in zip(weights, flip)]
    shapes = [
        jax.ShapeDtypeStruct((QUAD, rows, sum((high - low) * w // of for w in widths)), BF16)
        for low, (high, of) in cuts
    ]
    return call(
        functools.partial(pack_kernel, flip=flip, widths=widths, cuts=cuts),
        1,
        0,
        [whole_block(w) for w in weights],
        [(shape.shape, BF16, whole_block(shape)) for shape in shapes],
        [],
        tuple(weights),
        1,
        sum(4 * math.prod(shape.shape) for shape in shapes),
    )


def unpack_kernel(*refs, flip, cuts):
    blocks, outs = refs[: len(cuts)], refs[len(cuts) :]
    for block, (low, high) in zip(blocks, cuts):
        at = 0
        for ref, turned in zip(outs, flip):
            width = (ref.shape[0] if turned else ref.shape[1]) // QUAD
            start, end = low * width // high[1], high[0] * width // high[1]
            for quarter in range(QUAD):
                part = block[quarter, :, at : at + end - start].astype(F32)
                cut = slice(quarter * width + start, quarter * width + end)
                if turned:
                    ref[cut, :] = jnp.transpose(part)
                else:
                    ref[:, cut] = part
            at += end - start


def unpacked(blocks, shapes, flip, cuts):
    return call(
        functools.partial(unpack_kernel, flip=flip, cuts=cuts),
        1,
        0,
        [whole_block(v) for v in blocks],
        [(shape, F32, whole_block(jax.ShapeDtypeStruct(shape, F32))) for shape in shapes],
        [],
        tuple(blocks),
        1,
        sum(6 * math.prod(v.shape) for v in blocks),
    )


def weights_kernel(a_ref, b_ref, c_ref, d_ref, *refs):
    out_ref = refs[-1]
    cols = b_ref.shape[1]
    first = dot_tn(a_ref[...], b_ref[...])
    out_ref[:, :cols] = first.astype(BF16)
    out_ref[:, cols:] = dot_tn(c_ref[...], d_ref[...]).astype(BF16)
    if len(refs) > 1:
        w_ref, sums_ref = refs[:2]
        both = first * w_ref[...].astype(F32)
        high = both.astype(BF16)
        low = (both - high.astype(F32)).astype(BF16)
        ones = jnp.ones((sums_ref.shape[0], cols), BF16)
        sums_ref[...] = dot_nt(ones, high) + dot_nt(ones, low)


def weight_grads(a, b, c, d, w=None, rows=512):
    total, model = a.shape
    cut = pl.BlockSpec((total, rows), lambda t: (0, t))

    def whole(v):
        return pl.BlockSpec(v.shape, lambda t: (0, 0), pipeline_mode=pl.Buffered(1))

    def tall(cols):
        return pl.BlockSpec((rows, cols), lambda t: (t, 0))

    cols = b.shape[1] + d.shape[1]
    more = [] if w is None else [w]
    return call(
        weights_kernel,
        model // rows,
        0,
        [cut, whole(b), cut, whole(d)] + [tall(v.shape[1]) for v in more],
        [((8, model), F32, pl.BlockSpec((8, rows), lambda t: (0, t)))] * len(more) + [((model, cols), BF16, tall(cols))],
        [],
        (a, b, c, d, *more),
        2 * total * model * cols,
        2 * (2 * total * model + (total + model) * cols),
    )


def call(kernel, blocks, prefetch, ins, outs, scratch, args, flops, nbytes, transcendentals=0):
    return pl.pallas_call(
        kernel,
        out_shape=[jax.ShapeDtypeStruct(shape, dtype) for shape, dtype, _ in outs],
        grid_spec=pltpu.PrefetchScalarGridSpec(
            num_scalar_prefetch=prefetch,
            grid=(blocks,),
            in_specs=ins,
            out_specs=[spec for _, _, spec in outs],
            scratch_shapes=scratch,
        ),
        compiler_params=pltpu.CompilerParams(
            dimension_semantics=("arbitrary",), vmem_limit_bytes=56 * 1024 * 1024
        ),
        cost_estimate=pl.CostEstimate(
            flops=int(flops), bytes_accessed=int(nbytes), transcendentals=int(transcendentals)
        ),
    )(*args)


def on_device(
    tokens,
    attn_gain,
    ffn_gain,
    query_norm_gain,
    k_gain,
    w_query,
    key_projection,
    value_projection,
    w_out,
    w_gate,
    w_up,
    w_down,
    doc_start,
    cotangent,
):
    i, x = lax.axis_index("ctx"), lax.axis_index("tp")
    n = lax.axis_size("ctx") // QUAD
    line, b, core = i // QUAD, (i // 2) % 2, i % 2
    r, model = tokens.shape
    plane = 2 * QUAD * r
    width = query_norm_gain.shape[0]
    heads = w_query.shape[1] // QUAD // width
    qw = heads * width
    hidden = w_gate.shape[1] // QUAD
    step = model // n
    reach = WB * doc_start.shape[0]

    (sent,) = packed((w_query, key_projection, value_projection, w_out), (0, 0, 0, 1), [(0, (1, 1))])
    sent, tokens = tie(spread(sent), tokens)
    w_attn = line_gather(sent.reshape(step, -1), n)
    w_qkv, w_o = w_attn[:, : qw + 2 * width], w_attn[:, qw + 2 * width :]
    x_own = tokens.astype(F32)
    scale_1 = rms_scale(x_own)

    cut = FIRST_BLOCK
    ffn_cuts = [(0, (cut, 8)), (cut, (8, 8))]
    ffn_pieces = packed((w_gate, w_up, w_down), (0, 0, 1), ffn_cuts)
    a_own = (x_own * scale_1 * attn_gain).astype(BF16)
    a_near = (swap_x(a_own), swap_b(a_own), swap_both(a_own))

    near_core, near_b = swap_core(doc_start), swap_b(doc_start)
    far = swap_core(near_b)
    rows0 = [jnp.where(core == c, doc_start, near_core) for c in range(2)]
    rows1 = [jnp.where(core == c, near_b, far) for c in range(2)]
    starts = jnp.concatenate([jnp.where(b == y, rows0[c], rows1[c]) for y in range(2) for c in range(2)])
    first = line * plane
    relative = first + jnp.arange(plane, dtype=jnp.int32) - starts
    inv_freq = jnp.power(ROPE_BASE, -2.0 * jnp.arange(width // 2, dtype=F32) / width)
    angles = relative.astype(F32)[:, None] * inv_freq[None, :]
    cos, sin = jnp.cos(angles), jnp.sin(angles)
    cos = jnp.concatenate([cos] * 4, axis=-1)
    sin = jnp.concatenate([-sin, sin] * 2, axis=-1)
    sent_0 = spread(ffn_pieces[0])
    w_ffn_0 = line_gather(sent_0.reshape(step, -1), n)
    a_near, cos, sin, pieces_1, _ = tie(a_near, cos, sin, ffn_pieces[1], sent_0)
    sent_1 = spread(pieces_1)
    a_pieces = [a_own, *a_near]
    a_pieces = a_pieces + [swap_core(piece) for piece in a_pieces]

    blocks = jnp.arange(2 * QUAD, dtype=jnp.int32)
    table = (
        ((((blocks >> 1) & 1) ^ core) << 2) | (((blocks >> 2) ^ b) << 1) | ((blocks & 1) ^ x)
    ).astype(jnp.int32)
    inverse = (
        ((((blocks >> 1) & 1) ^ b) << 2) | (((blocks >> 2) ^ core) << 1) | ((blocks & 1) ^ x)
    ).astype(jnp.int32)
    nb = 2 * QUAD

    def key_range(base, keys):
        local = starts - (first - base)
        low = jnp.clip(local[::r] // KEY_BLOCK, 0, keys // KEY_BLOCK)
        high = jnp.clip((base + (blocks + 1) * r - 1) // KEY_BLOCK + 1, low, keys // KEY_BLOCK)
        return local, low, high

    own_part, halo_part = key_range(0, plane), key_range(reach, reach)

    gain_1, gain_2 = attn_gain, ffn_gain

    def here(cols):
        return pl.BlockSpec((r, cols), lambda t, *_: (t, 0))

    def moved(cols):
        return pl.BlockSpec((r, cols), lambda t, table, *_: (table[t], 0))

    lanes = 2 * width
    two = lambda gain: jnp.concatenate([gain, gain])[None, :]
    q_gain, key_gain = two(query_norm_gain), two(k_gain)
    a_one, raw, q, kv = call(
        functools.partial(project_kernel, heads=heads, width=width),
        nb,
        1,
        [whole_block(piece) for piece in a_pieces]
        + [whole_block(w_qkv), moved(lanes), moved(lanes), whole_block(q_gain), whole_block(key_gain)],
        [
            ((plane, model), BF16, here(model)),
            ((plane, qw + lanes), F32, here(qw + lanes)),
            ((plane, qw), BF16, moved(qw)),
            ((plane, lanes), BF16, moved(lanes)),
        ],
        [],
        (inverse, *a_pieces, w_qkv, cos, sin, q_gain, key_gain),
        2 * plane * model * (qw + lanes),
        plane * (4 * model + 10 * qw),
    )
    q, kv, sent_1, cot_own = tie(q, kv, sent_1, cotangent)
    w_ffn_1 = line_gather(sent_1.reshape(step, -1), n)
    spans = []
    left, distance = reach, 1
    while left > 0:
        spans.append((distance, min(left, plane)))
        left -= plane
        distance += 1
    halo = [line_move(kv[plane - rows :], d, range(0, max(n - d, 0))) for d, rows in spans]
    attn_flops = plane * heads * (plane // 2 + 2 * KEY_BLOCK) * width
    stacked = pl.BlockSpec((heads * r, 1), lambda t, *_: (t, 0))
    sums = ((plane * heads, lanes), F32, pl.BlockSpec((heads * r, lanes), lambda t, *_: (t, 0)))

    def attend(part, base, keys, *acc):
        local, low, high = part
        outs = [((plane, qw), BF16, moved(qw)), ((plane, qw), F32, here(qw)), ((plane * heads, 1), F32, stacked)]
        return call(
            functools.partial(attend_kernel, heads=heads, width=width, base=base, bk=KEY_BLOCK, last=len(acc)),
            nb,
            3,
            [here(qw), pl.BlockSpec((r, 1), lambda t, *_: (t, 0)), whole_block(keys)] + [sums[2]] * len(acc),
            outs if acc else [sums],
            [pltpu.VMEM((heads * r, lanes), F32)] * len(acc) + [pltpu.VMEM(keys.shape, BF16)],
            (table, low, high, q, local[:, None], keys, *acc),
            8 * attn_flops,
            plane * qw * 10,
        )

    (acc,) = attend(own_part, 0, kv)
    cot = Rows(cot_own)
    acc, halo, cot.first = tie(acc, halo, cot.first)
    cot.second()
    halo_keys = jnp.concatenate(halo[::-1], axis=0)
    o, o_float, stat = attend(halo_part, reach, halo_keys, acc)

    half = plane // 2
    o, cot.last = tie(o, cot.last)

    attn_sum, cot = scatter_rows(*split_dot(o, w_o), jnp.concatenate(cot.third(), axis=0))
    resid = x_own + attn_sum
    scale_2 = rms_scale(resid)
    a_pieces = gather_rows((resid * scale_2 * gain_2).astype(BF16))

    hid_0, d_gu_0, back, a_two = feed_forward(a_pieces, cot, w_ffn_0)
    (ffn_grad_0,) = weight_grads(a_two, d_gu_0, cot, hid_0)
    w_ffn_1, _ = tie(w_ffn_1, ffn_grad_0)
    ffn_grad_0 = line_scatter(ffn_grad_0, n)
    hid_1, d_gu_1, near, *far = feed_forward(a_two, cot, w_ffn_1, back)
    d_two, ffn_grad_1 = scatter_rows(near, far, weight_grads(a_two, d_gu_1, cot, hid_1)[0])
    ffn_grad_1 = line_scatter(ffn_grad_1, n)
    d_res, d_ffn_gain = norm_back(resid, scale_2, gain_2, d_two)
    d_h = cotangent.astype(F32) + d_res

    h_pieces, down = gather_rows(d_h.astype(BF16), down_rows(hid_0, hid_1, w_ffn_0, w_ffn_1))
    ffn_sum = Sums(*down)

    def home(grad):
        return spread(grad.reshape(QUAD, step // QUAD, -1))

    d_h_rows, d_o = call(
        rows_dot_kernel,
        nb,
        0,
        [whole_block(piece) for piece in h_pieces] + [whole_block(w_o)],
        [((plane, model), BF16, here(model)), ((plane, qw), BF16, here(qw))],
        [],
        (*h_pieces, w_o),
        2 * plane * model * qw,
        4 * plane * model,
    )
    d_o, ffn_sum.parts = tie(d_o, ffn_sum.parts)
    ffn_sum.second()

    def attend_back(part, base, keys, *acc):
        local, low, high = part
        if acc:
            outs = [((plane, qw), F32, here(qw)), (keys.shape, F32, pl.BlockSpec(keys.shape, lambda t, *_: (0, 0)))]
            scratch = pltpu.VMEM((heads * r, lanes), F32)
        else:
            outs = [sums] + [
                ((rows, lanes), BF16, pl.BlockSpec((rows, lanes), lambda t, *_: (0, 0))) for _, rows in spans[::-1]
            ]
            scratch = pltpu.VMEM(keys.shape, F32)
        return call(
            functools.partial(
                attend_back_kernel, heads=heads, width=width, base=base, bk=KEY_BLOCK, last=len(acc)
            ),
            nb,
            3,
            [
                here(qw),
                moved(qw),
                here(qw),
                stacked,
                pl.BlockSpec((1, 1, r), lambda t, *_: (t, 0, 0)),
                whole_block(keys),
            ]
            + [sums[2]] * len(acc),
            outs,
            [scratch],
            (table, low, high, q, d_o, o_float, stat, local.reshape(nb, 1, r), keys, *acc),
            20 * attn_flops,
            plane * qw * 12,
        )

    acc, *halo_grads = attend_back(halo_part, reach, halo_keys)
    acc, halo_grads, ffn_sum.got, ffn_grad_0 = tie(acc, halo_grads, ffn_sum.got, ffn_grad_0)
    back_0 = home(ffn_grad_0)
    returned = [line_move(g, -d, range(d, n)) for g, (d, _) in zip(halo_grads[::-1], spans)]
    dq, dkv = attend_back(own_part, 0, kv, acc)
    out_tokens = (resid + ffn_sum.third()).astype(BF16)
    dq, back_0, returned, out_tokens = tie(dq, back_0, returned, out_tokens)
    d_raw, d_head_gains = call(
        functools.partial(prep_back_kernel, heads=heads, width=width, plane=plane),
        nb,
        1,
        [moved(qw + lanes), here(lanes), here(lanes), whole_block(q_gain), whole_block(key_gain), here(qw), here(lanes)]
        + [whole_block(g) for g in returned],
        [
            ((plane, qw + lanes), BF16, moved(qw + lanes)),
            ((8, lanes), F32, pl.BlockSpec((8, lanes), lambda t, *_: (0, 0))),
        ],
        [],
        (table, raw, cos, sin, q_gain, key_gain, dq, dkv, *returned),
        plane * (qw + width) * 20,
        plane * (qw + 2 * width) * 10,
    )
    one = split_dot(d_raw, w_qkv)
    d_raw, one = tie(d_raw, one)
    one = Sums(*one)
    gain_sums, attn_grad = weight_grads(a_one, d_raw, d_h_rows, o, w_qkv)
    gain_sums = gain_sums[0]
    attn_grad = line_scatter(attn_grad, n)
    gain_sums, ffn_grad_1 = tie(gain_sums, ffn_grad_1)
    one.parts, gain_sums = tie(one.parts, gain_sums)
    one.second_x()
    back_1 = home(ffn_grad_1)
    d_one, back_1 = one.third_x(back_1)
    ffn_outs = unpacked((back_0, back_1), [v.shape for v in (w_gate, w_up, w_down)], (0, 0, 1), ffn_cuts)
    d_one, ffn_outs, gain_sums = tie(d_one, ffn_outs, gain_sums)
    d_attn_gain = gain_sums / gain_1
    d_q_gain = d_head_gains[0, :width] + d_head_gains[0, width:]
    gains = jnp.concatenate([d_attn_gain, d_ffn_gain, d_q_gain, d_head_gains[1, :width]])
    gains = sum_over_ctx(gains + swap_x(gains), 1, QUAD)
    d_x, _ = norm_back(x_own, scale_1, gain_1, d_one)
    d_tokens = d_h + d_x

    attn_grad, back_1 = tie(attn_grad, back_1)
    attn_back = home(attn_grad)
    attn_back, gains = tie(attn_back, gains)
    gains = sum_over_ctx(gains, QUAD, QUAD * n)
    attn_outs = unpacked(
        [attn_back],
        [v.shape for v in (w_query, key_projection, value_projection, w_out)],
        (0, 0, 0, 1),
        [(0, (1, 1))],
    )
    return (
        out_tokens,
        d_tokens,
        gains[:model],
        gains[model : 2 * model],
        gains[2 * model : 2 * model + width],
        gains[2 * model + width :],
        *attn_outs,
        *ffn_outs,
    )


def solution(mesh):
    return jax.shard_map(
        on_device,
        mesh=mesh,
        in_specs=(
            P(("ctx", "tp"), None),
            P(),
            P(),
            P(),
            P(),
            P("ctx", "tp"),
            P("ctx", "tp"),
            P("ctx", "tp"),
            P("tp", "ctx"),
            P("ctx", "tp"),
            P("ctx", "tp"),
            P("tp", "ctx"),
            P("ctx"),
            P(("ctx", "tp"), None),
        ),
        out_specs=(
            P(("ctx", "tp"), None),
            P(("ctx", "tp"), None),
            P(),
            P(),
            P(),
            P(),
            P("ctx", "tp"),
            P("ctx", "tp"),
            P("ctx", "tp"),
            P("tp", "ctx"),
            P("ctx", "tp"),
            P("ctx", "tp"),
            P("tp", "ctx"),
        ),
        check_vma=False,
    )
```

```python
import functools
import math

import jax
import jax.numpy as jnp
from jax import lax
from jax.experimental import pallas as pl
from jax.experimental.pallas import tpu as pltpu
from jax.sharding import PartitionSpec as P

WB = 6
EPSILON = 1e-05
ROPE_BASE = 1000000.0
LOG2E = math.log2(math.e)

QUAD = 4
KEY_BLOCK = 384
FIRST_BLOCK = 4

F32 = jnp.float32
BF16 = jnp.bfloat16


def swap_ctx(value, bit):
    n = lax.axis_size("ctx")
    return lax.ppermute(value, "ctx", [(i, i ^ bit) for i in range(n)])


def swap_core(value):
    return swap_ctx(value, 1)


def swap_b(value):
    return swap_ctx(value, 2)


def swap_x(value):
    return lax.ppermute(value, "tp", [(0, 1), (1, 0)])


def line_move(value, by, sources):
    pairs = [(s * QUAD + q, (s + by) * QUAD + q) for s in sources for q in range(QUAD)]
    return lax.ppermute(value, "ctx", pairs)


def line_groups(n):
    return [[p * QUAD + q for p in range(n)] for q in range(QUAD)]


def line_gather(own, n):
    return lax.all_gather(own, "ctx", axis=0, axis_index_groups=line_groups(n), tiled=True)


def line_scatter(partial, n):
    return lax.psum_scatter(partial, "ctx", scatter_dimension=0, axis_index_groups=line_groups(n), tiled=True)


def line_move(value, by, sources):
    pairs = [(s * QUAD + q, (s + by) * QUAD + q) for s in sources for q in range(QUAD)]
    return lax.ppermute(value, "ctx", pairs)


def tie(*values):
    return lax.optimization_barrier(values)


def add16(a, b):
    return (a.astype(F32) + b.astype(F32)).astype(BF16)


def swap_both(value):
    n = lax.axis_size("ctx")
    return lax.ppermute(value, ("ctx", "tp"), [(2 * i + x, 2 * (i ^ 2) + 1 - x) for i in range(n) for x in range(2)])


class Rows:
    def __init__(self, own):
        self.own, self.half = own, own.shape[0] // 2
        self.first = (swap_x(own), swap_b(own))

    def second(self):
        from_x, from_b = self.first
        self.last = (swap_x(from_b[: self.half]), swap_b(from_x[self.half :]))

    def third(self):
        near = [self.own, *self.first, *self.last]
        return near + [swap_core(piece) for piece in near]


def gather_rows(own, beside=None):
    rows = Rows(own)
    if beside is not None:
        rows.first, beside = tie(rows.first, beside)
    rows.second()
    return rows.third() if beside is None else (rows.third(), beside)


class Sums:
    def __init__(self, near, far):
        r = near.shape[0] // 4
        self.half = r // 2

        def fold(block):
            return add16(near[block * r : (block + 1) * r], swap_core(far[block]))

        self.parts = (fold(3), fold(1), fold(2), fold(0))

    def second(self):
        both, for_x, for_b, _ = self.parts
        half = self.half
        self.got = (swap_x(both[:half]), swap_b(both[half:]), swap_x(for_x[:half]), swap_b(for_b[half:]))

    def third(self):
        _, for_x, for_b, own = self.parts
        top, bottom, x_top, b_bottom = self.got
        half = self.half
        x_bottom = swap_x(add16(for_x[half:], bottom))
        b_top = swap_b(add16(for_b[:half], top))
        own = own.astype(F32)
        return jnp.concatenate(
            [
                own[:half] + x_top.astype(F32) + b_top.astype(F32),
                own[half:] + b_bottom.astype(F32) + x_bottom.astype(F32),
            ],
            axis=0,
        )


    def second_x(self):
        self.got = swap_x(self.parts[0])

    def third_x(self, beside):
        _, for_x, for_b, own = self.parts
        for_b, for_x, beside = tie(add16(for_b, self.got), for_x, beside)
        return own.astype(F32) + swap_x(for_x).astype(F32) + swap_b(for_b).astype(F32), beside


def scatter_rows(near, far, beside=None):
    sums = Sums(near, far)
    sums.second()
    if beside is not None:
        sums.got, beside = tie(sums.got, beside)
    return sums.third() if beside is None else (sums.third(), beside)


def blocks_of(rows):
    r = rows.shape[0] // 4
    return [rows[k * r : (k + 1) * r] for k in range(4)]


def spread(pieces, axis=0):
    n = lax.axis_size("ctx")
    groups = [list(range(i, i + QUAD)) for i in range(0, n, QUAD)]
    return lax.all_to_all(pieces, "ctx", axis, axis, axis_index_groups=groups, tiled=True)


def sum_over_ctx(value, bit, end):
    while bit < end:
        value = value + swap_ctx(value, bit)
        bit *= 2
    return value


def dot(a, b):
    return jnp.dot(a, b, preferred_element_type=F32)


def dot_nt(a, b):
    return lax.dot_general(a, b, (((1,), (1,)), ((), ())), preferred_element_type=F32)


def dot_tn(a, b):
    return lax.dot_general(a, b, (((0,), (0,)), ((), ())), preferred_element_type=F32)


def rms_scale(values):
    return lax.rsqrt(jnp.mean(values * values, axis=-1, keepdims=True) + EPSILON)


def norm_back(values, scale, gain, grad):
    unit = values * scale
    inner = grad * gain
    d_values = scale * (inner - unit * jnp.mean(inner * unit, axis=-1, keepdims=True))
    return d_values, jnp.sum(grad * unit, axis=0)


def pick(refs, block, out_ref, at):
    r = refs[0].shape[0]
    for k in range(8):
        index = k // 4 * (len(refs) // 2) + k % 4

        @pl.when(block == k)
        def _():
            if k % 4 < 3 or len(refs) == 8:
                out_ref[at : at + r, :] = refs[index][...]
            else:
                out_ref[at : at + r // 2, :] = refs[index][...]
                out_ref[at + r // 2 : at + r, :] = refs[index + 1][...]


class Heads:
    def __init__(self, width, cos, sin):
        self.width, self.cos, self.sin = width, cos, sin
        lanes = 2 * width
        row = lax.broadcasted_iota(jnp.int32, (lanes, lanes), 0)
        col = lax.broadcasted_iota(jnp.int32, (lanes, lanes), 1)
        self.same = jnp.where(row // width == col // width, 1.0 / width, 0.0).astype(BF16)

    def mean(self, u):
        high = u.astype(BF16)
        low = (u - high.astype(F32)).astype(BF16)
        return dot(high, self.same) + dot(low, self.same)

    def swapped(self, u):
        half = self.width // 2
        lane = lax.broadcasted_iota(jnp.int32, u.shape, 1)
        return jnp.where((lane & half) == 0, pltpu.roll(u, 2 * self.width - half, 1), pltpu.roll(u, half, 1))

    def ready(self, u, gain):
        u = u * lax.rsqrt(self.mean(u * u) + EPSILON) * gain
        return u * self.cos + self.swapped(u) * self.sin

    def back(self, w, gain, grad):
        e = grad * self.cos - self.swapped(grad) * self.sin
        scale = lax.rsqrt(self.mean(w * w) + EPSILON)
        unit = w * scale
        inner = e * gain
        return scale * (inner - unit * self.mean(inner * unit)), jnp.sum(e * unit, axis=0, keepdims=True)


def project_kernel(table, *refs, heads, width):
    pieces, (w_ref, cos_ref, sin_ref, q_gain_ref, k_gain_ref, rows_ref, raw_ref, q_ref, kv_ref) = refs[:-9], refs[-9:]
    pick(pieces, pl.program_id(0), rows_ref, 0)
    raw = dot(rows_ref[...], w_ref[...])
    raw_ref[...] = raw
    math_of = Heads(width, cos_ref[...], sin_ref[...])
    lanes = 2 * width
    for c in range(heads // 2):
        cols = slice(c * lanes, (c + 1) * lanes)
        q_ref[:, cols] = math_of.ready(raw[:, cols], q_gain_ref[...]).astype(BF16)
    last = raw[:, heads * width :]
    lane = lax.broadcasted_iota(jnp.int32, last.shape, 1)
    kv_ref[...] = jnp.where(lane < width, math_of.ready(last, k_gain_ref[...]), last).astype(BF16)


def prep_back_kernel(
    table, raw_ref, cos_ref, sin_ref, q_gain_ref, k_gain_ref, dq_ref, dkv_ref, *refs, heads, width, plane
):
    halo, (out_ref, dg_ref) = refs[:-2], refs[-2:]
    t = pl.program_id(0)

    @pl.when(t == 0)
    def _():
        dg_ref[...] = jnp.zeros_like(dg_ref)

    math_of = Heads(width, cos_ref[...], sin_ref[...])
    lanes = 2 * width
    total = jnp.zeros((1, lanes), F32)
    for c in range(heads // 2):
        cols = slice(c * lanes, (c + 1) * lanes)
        dw, dg = math_of.back(raw_ref[:, cols], q_gain_ref[...], dq_ref[:, cols])
        out_ref[:, cols] = dw.astype(BF16)
        total = total + dg
    grad = dkv_ref[...]
    r = grad.shape[0]
    for ref in halo:
        missing = plane // r - ref.shape[0] // r
        at = pl.multiple_of(jnp.maximum(t - missing, 0) * r, r)
        grad = grad + jnp.where(t >= missing, ref[pl.ds(at, r), :].astype(F32), 0.0)
    dw, dg = math_of.back(raw_ref[:, heads * width :], k_gain_ref[...], grad)
    lane = lax.broadcasted_iota(jnp.int32, grad.shape, 1)
    out_ref[:, heads * width :] = jnp.where(lane < width, dw, grad).astype(BF16)
    dg_ref[0:1, :] += total
    dg_ref[1:2, :] += dg


def rows_dot_kernel(*refs):
    pieces, (w_ref, rows_ref, out_ref) = refs[:10], refs[10:]
    pick(pieces, pl.program_id(0), rows_ref, 0)
    out_ref[...] = dot(rows_ref[...], w_ref[...]).astype(BF16)


def stack_heads(block, heads, width):
    return jnp.concatenate([block[:, h * width : (h + 1) * width] for h in range(heads)], axis=0)


def attend_kernel(table, lo, hi, q_ref, start_ref, kv_ref, *refs, heads, width, base, bk, last):
    ones_v = refs[-1]
    if last:
        acc_in, o_ref, of_ref, stat_ref, acc = refs[:5]
    else:
        acc = refs[0]
    t = pl.program_id(0)
    r = q_ref.shape[0]

    @pl.when(t == 0)
    def _():
        lane = lax.broadcasted_iota(jnp.int32, kv_ref.shape, 1)
        ones_v[...] = jnp.where(lane < width, jnp.ones((), BF16), kv_ref[...])

    q = stack_heads(q_ref[...], heads, width)
    q = jnp.concatenate([q, jnp.zeros_like(q)], axis=-1)
    start = jnp.concatenate([start_ref[...]] * heads, axis=0)
    pos = base + t * r + lax.broadcasted_iota(jnp.int32, (r, 1), 0)
    pos = jnp.concatenate([pos] * heads, axis=0)
    acc[...] = acc_in[...] if last else jnp.zeros_like(acc)
    c = LOG2E / math.sqrt(width)

    def step(kb, carry):
        k0 = pl.multiple_of(kb * bk, bk)
        s = dot_nt(q, kv_ref[pl.ds(k0, bk), :])
        key = k0 + lax.broadcasted_iota(jnp.int32, (1, bk), 1)
        p = jnp.where((key >= start) & (key <= pos), jnp.exp2(s * c), 0.0)
        acc[...] += dot(p.astype(BF16), ones_v[pl.ds(k0, bk), :])
        return carry

    lax.fori_loop(lo[t], hi[t], step, 0)
    if last:
        total = acc[:, :1]
        o = acc[:, width:] / total
        stat_ref[...] = jnp.log2(total)
        for h in range(heads):
            part = o[h * r : (h + 1) * r]
            of_ref[:, h * width : (h + 1) * width] = part
            o_ref[:, h * width : (h + 1) * width] = part.astype(BF16)


def attend_back_kernel(
    table, lo, hi, q_ref, do_ref, of_ref, stat_ref, start_ref, kv_ref, *refs, heads, width, base, bk, last
):
    if last:
        acc_in, dq_ref, dkv, acc = refs
    else:
        acc, dkv_refs, dkv = refs[0], refs[1:-1], refs[-1]
    t = pl.program_id(0)
    r = q_ref.shape[0]

    @pl.when(t == 0)
    def _():
        dkv[...] = jnp.zeros_like(dkv)

    scale = 1.0 / math.sqrt(width)
    q = stack_heads(q_ref[...], heads, width)
    do = stack_heads(do_ref[...], heads, width)
    of = stack_heads(of_ref[...], heads, width)
    delta = jnp.sum(do.astype(F32) * of, axis=-1, keepdims=True)
    lane = lax.broadcasted_iota(jnp.int32, (heads * r, 2 * width), 1)
    rows = jnp.transpose(jnp.where(lane == 0, stat_ref[...], delta))
    stat, delta = rows[0:1, :], rows[1:2, :]
    q = jnp.concatenate([q, jnp.zeros_like(q)], axis=-1)
    q_scaled = (q.astype(F32) * scale).astype(BF16)
    do = jnp.concatenate([jnp.zeros_like(do), do], axis=-1)
    start = jnp.concatenate([start_ref[0]] * heads, axis=-1)
    pos = base + t * r + lax.broadcasted_iota(jnp.int32, (1, r), 1)
    pos = jnp.concatenate([pos] * heads, axis=-1)
    acc[...] = acc_in[...] if last else jnp.zeros_like(acc)

    def step(kb, carry):
        k0 = pl.multiple_of(kb * bk, bk)
        kv = kv_ref[pl.ds(k0, bk), :]
        s = dot_nt(kv, q_scaled)
        dp = dot_nt(kv, do)
        key = k0 + lax.broadcasted_iota(jnp.int32, (bk, 1), 0)
        p = jnp.where((key >= start) & (key <= pos), jnp.exp2(s * LOG2E - stat), 0.0)
        ds = (p * (dp - delta)).astype(BF16)
        dkv[pl.ds(k0, bk), :] += dot(ds, q_scaled) + dot(p.astype(BF16), do)
        acc[...] += dot_tn(ds, kv)
        return carry

    lax.fori_loop(lo[t], hi[t], step, 0)
    if last:
        dq = acc[...][:, :width] * scale
        for h in range(heads):
            dq_ref[:, h * width : (h + 1) * width] = dq[h * r : (h + 1) * r]
    else:

        @pl.when(t == pl.num_programs(0) - 1)
        def _():
            at = 0
            for ref in dkv_refs:
                ref[...] = dkv[at : at + ref.shape[0], :].astype(BF16)
                at += ref.shape[0]


def feed_first_kernel(*refs, hb):
    pieces, (c_ref, w_ref, hid_ref, dgu_ref, back_ref, rows_ref) = refs[:10], refs[10:]
    t = pl.program_id(0)
    r = pieces[0].shape[0]
    pick(pieces, 2 * t, rows_ref, 0)
    pick(pieces, 2 * t + 1, rows_ref, r)
    back_ref[...] = feed(rows_ref, c_ref, w_ref, hid_ref, dgu_ref, hb).astype(BF16)


def feed_last_kernel(a_ref, c_ref, w_ref, prev_ref, hid_ref, dgu_ref, near_ref, *far_refs, hb):
    t = pl.program_id(0)
    back = feed(a_ref, c_ref, w_ref, hid_ref, dgu_ref, hb) + prev_ref[...].astype(F32)
    split_store(back, t, near_ref, far_refs)


def feed(a_ref, c_ref, w_ref, hid_ref, dgu_ref, hb):
    a, c = a_ref[...], c_ref[...]
    gate, up = dot(a, w_ref[:, :hb]), dot(a, w_ref[:, hb : 2 * hb])
    d_hid = dot(c, w_ref[:, 2 * hb :])
    sig = jax.nn.sigmoid(gate)
    silu = gate * sig
    hid_ref[...] = (silu * up).astype(BF16)
    dgu_ref[:, :hb] = (d_hid * up * (sig * (1.0 + gate * (1.0 - sig)))).astype(BF16)
    dgu_ref[:, hb:] = (d_hid * silu).astype(BF16)
    return dot_nt(dgu_ref[...], w_ref[:, : 2 * hb])


def down_kernel(h0_ref, h1_ref, w0_ref, w1_ref, near_ref, *far_refs):
    t = pl.program_id(0)
    y = sum(dot_nt(h[...], w[:, 2 * h.shape[1] :]) for h, w in ((h0_ref, w0_ref), (h1_ref, w1_ref)))
    split_store(y, t, near_ref, far_refs)


def split_store(value, t, near_ref, far_refs):
    r = far_refs[0].shape[0]

    @pl.when(t < 2)
    def _():
        near_ref[...] = value.astype(BF16)

    for k, ref in enumerate(far_refs):

        @pl.when(t == 2 + k // 2)
        def _():
            ref[...] = value[k % 2 * r : (k % 2 + 1) * r].astype(BF16)


def split_outs(total, model):
    far = pl.BlockSpec((total // 8, model), lambda t: (0, 0))
    near = pl.BlockSpec((total // 4, model), lambda t: (jnp.minimum(t, 1), 0))
    return [((total // 2, model), BF16, near)] + [((total // 8, model), BF16, far)] * 4


def split_dot_kernel(a_ref, w_ref, near_ref, *far_refs):
    split_store(dot_nt(a_ref[...], w_ref[...]), pl.program_id(0), near_ref, far_refs)


def split_dot(a, w):
    total, cols = a.shape
    model = w.shape[0]
    near, *far = call(
        split_dot_kernel,
        4,
        0,
        [pl.BlockSpec((total // 4, cols), lambda t: (t, 0)), whole_block(w)],
        split_outs(total, model),
        [],
        (a, w),
        2 * total * model * cols,
        2 * total * (model + cols),
    )
    return near, far


def down_rows(h0, h1, w0, w1):
    total, hb = h0.shape[0], (h0.shape[1] + h1.shape[1]) // 2
    model = w0.shape[0]

    def row(h):
        return pl.BlockSpec((total // 4, h.shape[1]), lambda t: (t, 0))

    near, *far = call(
        down_kernel,
        4,
        0,
        [row(h0), row(h1), whole_block(w0), whole_block(w1)],
        split_outs(total, model),
        [],
        (h0, h1, w0, w1),
        4 * total * model * hb,
        2 * total * (model + 2 * hb) + 12 * model * hb,
    )
    return near, far


def whole_block(v):
    return pl.BlockSpec(v.shape, lambda t, *_: (0,) * len(v.shape), pipeline_mode=pl.Buffered(1))


def feed_forward(a, c, w, prev=None):
    total, model = c.shape
    rows = total // 4
    hb = w.shape[1] // 3

    def row(cols):
        return pl.BlockSpec((rows, cols), lambda t: (t, 0))

    outs = [((total, hb), BF16, row(hb)), ((total, 2 * hb), BF16, row(2 * hb))]
    if prev is None:
        kernel, args = feed_first_kernel, (*a, c, w)
        ins = [whole_block(piece) for piece in a] + [row(model), whole_block(w)]
        outs += [((total, model), BF16, row(model))] * 2
    else:
        kernel, args = feed_last_kernel, (a, c, w, prev)
        ins = [row(model), row(model), whole_block(w), row(model)]
        outs += split_outs(total, model)
    return call(
        functools.partial(kernel, hb=hb),
        4,
        0,
        ins,
        outs,
        [],
        args,
        12 * total * model * hb,
        2 * total * (4 * model + 3 * hb) + 6 * model * hb,
        total * hb,
    )


def pack_kernel(*refs, flip, widths, cuts):
    ins, outs = refs[: len(flip)], refs[len(flip) :]
    for quarter in range(QUAD):
        for out_ref, (low, high) in zip(outs, cuts):
            at = 0
            for ref, turned, width in zip(ins, flip, widths):
                start, end = low * width // high[1], high[0] * width // high[1]
                cut = slice(quarter * width + start, quarter * width + end)
                out_ref[quarter, :, at : at + end - start] = jnp.transpose(ref[cut, :]) if turned else ref[:, cut]
                at += end - start


def packed(weights, flip, cuts):
    rows = weights[0].shape[flip[0]]
    widths = [(w.shape[0] if f else w.shape[1]) // QUAD for w, f in zip(weights, flip)]
    shapes = [
        jax.ShapeDtypeStruct((QUAD, rows, sum((high - low) * w // of for w in widths)), BF16)
        for low, (high, of) in cuts
    ]
    return call(
        functools.partial(pack_kernel, flip=flip, widths=widths, cuts=cuts),
        1,
        0,
        [whole_block(w) for w in weights],
        [(shape.shape, BF16, whole_block(shape)) for shape in shapes],
        [],
        tuple(weights),
        1,
        sum(4 * math.prod(shape.shape) for shape in shapes),
    )


def unpack_kernel(*refs, flip, cuts):
    blocks, outs = refs[: len(cuts)], refs[len(cuts) :]
    for block, (low, high) in zip(blocks, cuts):
        at = 0
        for ref, turned in zip(outs, flip):
            width = (ref.shape[0] if turned else ref.shape[1]) // QUAD
            start, end = low * width // high[1], high[0] * width // high[1]
            for quarter in range(QUAD):
                part = block[quarter, :, at : at + end - start].astype(F32)
                cut = slice(quarter * width + start, quarter * width + end)
                if turned:
                    ref[cut, :] = jnp.transpose(part)
                else:
                    ref[:, cut] = part
            at += end - start


def unpacked(blocks, shapes, flip, cuts):
    return call(
        functools.partial(unpack_kernel, flip=flip, cuts=cuts),
        1,
        0,
        [whole_block(v) for v in blocks],
        [(shape, F32, whole_block(jax.ShapeDtypeStruct(shape, F32))) for shape in shapes],
        [],
        tuple(blocks),
        1,
        sum(6 * math.prod(v.shape) for v in blocks),
    )


def weights_kernel(a_ref, b_ref, c_ref, d_ref, *refs):
    out_ref = refs[-1]
    cols = b_ref.shape[1]
    first = dot_tn(a_ref[...], b_ref[...])
    out_ref[:, :cols] = first.astype(BF16)
    out_ref[:, cols:] = dot_tn(c_ref[...], d_ref[...]).astype(BF16)
    if len(refs) > 1:
        w_ref, sums_ref = refs[:2]
        both = first * w_ref[...].astype(F32)
        high = both.astype(BF16)
        low = (both - high.astype(F32)).astype(BF16)
        ones = jnp.ones((sums_ref.shape[0], cols), BF16)
        sums_ref[...] = dot_nt(ones, high) + dot_nt(ones, low)


def weight_grads(a, b, c, d, w=None, rows=512):
    total, model = a.shape
    cut = pl.BlockSpec((total, rows), lambda t: (0, t))

    def whole(v):
        return pl.BlockSpec(v.shape, lambda t: (0, 0), pipeline_mode=pl.Buffered(1))

    def tall(cols):
        return pl.BlockSpec((rows, cols), lambda t: (t, 0))

    cols = b.shape[1] + d.shape[1]
    more = [] if w is None else [w]
    return call(
        weights_kernel,
        model // rows,
        0,
        [cut, whole(b), cut, whole(d)] + [tall(v.shape[1]) for v in more],
        [((8, model), F32, pl.BlockSpec((8, rows), lambda t: (0, t)))] * len(more) + [((model, cols), BF16, tall(cols))],
        [],
        (a, b, c, d, *more),
        2 * total * model * cols,
        2 * (2 * total * model + (total + model) * cols),
    )


def call(kernel, blocks, prefetch, ins, outs, scratch, args, flops, nbytes, transcendentals=0):
    return pl.pallas_call(
        kernel,
        out_shape=[jax.ShapeDtypeStruct(shape, dtype) for shape, dtype, _ in outs],
        grid_spec=pltpu.PrefetchScalarGridSpec(
            num_scalar_prefetch=prefetch,
            grid=(blocks,),
            in_specs=ins,
            out_specs=[spec for _, _, spec in outs],
            scratch_shapes=scratch,
        ),
        compiler_params=pltpu.CompilerParams(
            dimension_semantics=("arbitrary",), vmem_limit_bytes=56 * 1024 * 1024
        ),
        cost_estimate=pl.CostEstimate(
            flops=int(flops), bytes_accessed=int(nbytes), transcendentals=int(transcendentals)
        ),
    )(*args)


def on_device(
    tokens,
    attn_gain,
    ffn_gain,
    query_norm_gain,
    k_gain,
    w_query,
    key_projection,
    value_projection,
    w_out,
    w_gate,
    w_up,
    w_down,
    doc_start,
    cotangent,
):
    i, x = lax.axis_index("ctx"), lax.axis_index("tp")
    n = lax.axis_size("ctx") // QUAD
    line, b, core = i // QUAD, (i // 2) % 2, i % 2
    r, model = tokens.shape
    plane = 2 * QUAD * r
    width = query_norm_gain.shape[0]
    heads = w_query.shape[1] // QUAD // width
    qw = heads * width
    hidden = w_gate.shape[1] // QUAD
    step = model // n
    reach = WB * doc_start.shape[0]

    (sent,) = packed((w_query, key_projection, value_projection, w_out), (0, 0, 0, 1), [(0, (1, 1))])
    sent, tokens = tie(spread(sent), tokens)
    w_attn = line_gather(sent.reshape(step, -1), n)
    w_qkv, w_o = w_attn[:, : qw + 2 * width], w_attn[:, qw + 2 * width :]
    x_own = tokens.astype(F32)
    scale_1 = rms_scale(x_own)

    cut = FIRST_BLOCK
    ffn_cuts = [(0, (cut, 8)), (cut, (8, 8))]
    ffn_pieces = packed((w_gate, w_up, w_down), (0, 0, 1), ffn_cuts)
    a_own = (x_own * scale_1 * attn_gain).astype(BF16)
    a_near = (swap_x(a_own), swap_b(a_own), swap_both(a_own))

    near_core, near_b = swap_core(doc_start), swap_b(doc_start)
    far = swap_core(near_b)
    rows0 = [jnp.where(core == c, doc_start, near_core) for c in range(2)]
    rows1 = [jnp.where(core == c, near_b, far) for c in range(2)]
    starts = jnp.concatenate([jnp.where(b == y, rows0[c], rows1[c]) for y in range(2) for c in range(2)])
    first = line * plane
    relative = first + jnp.arange(plane, dtype=jnp.int32) - starts
    inv_freq = jnp.power(ROPE_BASE, -2.0 * jnp.arange(width // 2, dtype=F32) / width)
    angles = relative.astype(F32)[:, None] * inv_freq[None, :]
    cos, sin = jnp.cos(angles), jnp.sin(angles)
    cos = jnp.concatenate([cos] * 4, axis=-1)
    sin = jnp.concatenate([-sin, sin] * 2, axis=-1)
    sent_0 = spread(ffn_pieces[0])
    w_ffn_0 = line_gather(sent_0.reshape(step, -1), n)
    a_near, cos, sin, pieces_1, _ = tie(a_near, cos, sin, ffn_pieces[1], sent_0)
    sent_1 = spread(pieces_1)
    a_pieces = [a_own, *a_near]
    a_pieces = a_pieces + [swap_core(piece) for piece in a_pieces]

    blocks = jnp.arange(2 * QUAD, dtype=jnp.int32)
    table = (
        ((((blocks >> 1) & 1) ^ core) << 2) | (((blocks >> 2) ^ b) << 1) | ((blocks & 1) ^ x)
    ).astype(jnp.int32)
    inverse = (
        ((((blocks >> 1) & 1) ^ b) << 2) | (((blocks >> 2) ^ core) << 1) | ((blocks & 1) ^ x)
    ).astype(jnp.int32)
    nb = 2 * QUAD

    def key_range(base, keys):
        local = starts - (first - base)
        low = jnp.clip(local[::r] // KEY_BLOCK, 0, keys // KEY_BLOCK)
        high = jnp.clip((base + (blocks + 1) * r - 1) // KEY_BLOCK + 1, low, keys // KEY_BLOCK)
        return local, low, high

    own_part, halo_part = key_range(0, plane), key_range(reach, reach)

    gain_1, gain_2 = attn_gain, ffn_gain

    def here(cols):
        return pl.BlockSpec((r, cols), lambda t, *_: (t, 0))

    def moved(cols):
        return pl.BlockSpec((r, cols), lambda t, table, *_: (table[t], 0))

    lanes = 2 * width
    two = lambda gain: jnp.concatenate([gain, gain])[None, :]
    q_gain, key_gain = two(query_norm_gain), two(k_gain)
    a_one, raw, q, kv = call(
        functools.partial(project_kernel, heads=heads, width=width),
        nb,
        1,
        [whole_block(piece) for piece in a_pieces]
        + [whole_block(w_qkv), moved(lanes), moved(lanes), whole_block(q_gain), whole_block(key_gain)],
        [
            ((plane, model), BF16, here(model)),
            ((plane, qw + lanes), F32, here(qw + lanes)),
            ((plane, qw), BF16, moved(qw)),
            ((plane, lanes), BF16, moved(lanes)),
        ],
        [],
        (inverse, *a_pieces, w_qkv, cos, sin, q_gain, key_gain),
        2 * plane * model * (qw + lanes),
        plane * (4 * model + 10 * qw),
    )
    q, kv, sent_1, cot_own = tie(q, kv, sent_1, cotangent)
    w_ffn_1 = line_gather(sent_1.reshape(step, -1), n)
    spans = []
    left, distance = reach, 1
    while left > 0:
        spans.append((distance, min(left, plane)))
        left -= plane
        distance += 1
    halo = [line_move(kv[plane - rows :], d, range(0, max(n - d, 0))) for d, rows in spans]
    attn_flops = plane * heads * (plane // 2 + 2 * KEY_BLOCK) * width
    stacked = pl.BlockSpec((heads * r, 1), lambda t, *_: (t, 0))
    sums = ((plane * heads, lanes), F32, pl.BlockSpec((heads * r, lanes), lambda t, *_: (t, 0)))

    def attend(part, base, keys, *acc):
        local, low, high = part
        outs = [((plane, qw), BF16, moved(qw)), ((plane, qw), F32, here(qw)), ((plane * heads, 1), F32, stacked)]
        return call(
            functools.partial(attend_kernel, heads=heads, width=width, base=base, bk=KEY_BLOCK, last=len(acc)),
            nb,
            3,
            [here(qw), pl.BlockSpec((r, 1), lambda t, *_: (t, 0)), whole_block(keys)] + [sums[2]] * len(acc),
            outs if acc else [sums],
            [pltpu.VMEM((heads * r, lanes), F32)] * len(acc) + [pltpu.VMEM(keys.shape, BF16)],
            (table, low, high, q, local[:, None], keys, *acc),
            8 * attn_flops,
            plane * qw * 10,
        )

    (acc,) = attend(own_part, 0, kv)
    cot = Rows(cot_own)
    acc, halo, cot.first = tie(acc, halo, cot.first)
    cot.second()
    halo_keys = jnp.concatenate(halo[::-1], axis=0)
    o, o_float, stat = attend(halo_part, reach, halo_keys, acc)

    half = plane // 2
    o, cot.last = tie(o, cot.last)

    attn_sum, cot = scatter_rows(*split_dot(o, w_o), jnp.concatenate(cot.third(), axis=0))
    resid = x_own + attn_sum
    scale_2 = rms_scale(resid)
    a_pieces = gather_rows((resid * scale_2 * gain_2).astype(BF16))

    hid_0, d_gu_0, back, a_two = feed_forward(a_pieces, cot, w_ffn_0)
    (ffn_grad_0,) = weight_grads(a_two, d_gu_0, cot, hid_0)
    w_ffn_1, _ = tie(w_ffn_1, ffn_grad_0)
    ffn_grad_0 = line_scatter(ffn_grad_0, n)
    hid_1, d_gu_1, near, *far = feed_forward(a_two, cot, w_ffn_1, back)
    d_two, ffn_grad_1 = scatter_rows(near, far, weight_grads(a_two, d_gu_1, cot, hid_1)[0])
    ffn_grad_1 = line_scatter(ffn_grad_1, n)
    d_res, d_ffn_gain = norm_back(resid, scale_2, gain_2, d_two)
    d_h = cotangent.astype(F32) + d_res

    h_pieces, down = gather_rows(d_h.astype(BF16), down_rows(hid_0, hid_1, w_ffn_0, w_ffn_1))
    ffn_sum = Sums(*down)

    def home(grad):
        return spread(grad.reshape(QUAD, step // QUAD, -1))

    d_h_rows, d_o = call(
        rows_dot_kernel,
        nb,
        0,
        [whole_block(piece) for piece in h_pieces] + [whole_block(w_o)],
        [((plane, model), BF16, here(model)), ((plane, qw), BF16, here(qw))],
        [],
        (*h_pieces, w_o),
        2 * plane * model * qw,
        4 * plane * model,
    )
    d_o, ffn_sum.parts = tie(d_o, ffn_sum.parts)
    ffn_sum.second()

    def attend_back(part, base, keys, *acc):
        local, low, high = part
        if acc:
            outs = [((plane, qw), F32, here(qw)), (keys.shape, F32, pl.BlockSpec(keys.shape, lambda t, *_: (0, 0)))]
            scratch = pltpu.VMEM((heads * r, lanes), F32)
        else:
            outs = [sums] + [
                ((rows, lanes), BF16, pl.BlockSpec((rows, lanes), lambda t, *_: (0, 0))) for _, rows in spans[::-1]
            ]
            scratch = pltpu.VMEM(keys.shape, F32)
        return call(
            functools.partial(
                attend_back_kernel, heads=heads, width=width, base=base, bk=KEY_BLOCK, last=len(acc)
            ),
            nb,
            3,
            [
                here(qw),
                moved(qw),
                here(qw),
                stacked,
                pl.BlockSpec((1, 1, r), lambda t, *_: (t, 0, 0)),
                whole_block(keys),
            ]
            + [sums[2]] * len(acc),
            outs,
            [scratch],
            (table, low, high, q, d_o, o_float, stat, local.reshape(nb, 1, r), keys, *acc),
            20 * attn_flops,
            plane * qw * 12,
        )

    acc, *halo_grads = attend_back(halo_part, reach, halo_keys)
    acc, halo_grads, ffn_sum.got, ffn_grad_0 = tie(acc, halo_grads, ffn_sum.got, ffn_grad_0)
    back_0 = home(ffn_grad_0)
    returned = [line_move(g, -d, range(d, n)) for g, (d, _) in zip(halo_grads[::-1], spans)]
    dq, dkv = attend_back(own_part, 0, kv, acc)
    out_tokens = (resid + ffn_sum.third()).astype(BF16)
    dq, back_0, returned, out_tokens = tie(dq, back_0, returned, out_tokens)
    d_raw, d_head_gains = call(
        functools.partial(prep_back_kernel, heads=heads, width=width, plane=plane),
        nb,
        1,
        [moved(qw + lanes), here(lanes), here(lanes), whole_block(q_gain), whole_block(key_gain), here(qw), here(lanes)]
        + [whole_block(g) for g in returned],
        [
            ((plane, qw + lanes), BF16, moved(qw + lanes)),
            ((8, lanes), F32, pl.BlockSpec((8, lanes), lambda t, *_: (0, 0))),
        ],
        [],
        (table, raw, cos, sin, q_gain, key_gain, dq, dkv, *returned),
        plane * (qw + width) * 20,
        plane * (qw + 2 * width) * 10,
    )
    gain_sums, attn_grad = weight_grads(a_one, d_raw, d_h_rows, o, w_qkv)
    gain_sums, d_raw = tie(gain_sums[0], d_raw)
    one = Sums(*split_dot(d_raw, w_qkv))
    attn_grad = line_scatter(attn_grad, n)
    gain_sums, ffn_grad_1 = tie(gain_sums, ffn_grad_1)
    one.parts, gain_sums = tie(one.parts, gain_sums)
    one.second_x()
    back_1 = home(ffn_grad_1)
    d_one, back_1 = one.third_x(back_1)
    ffn_outs = unpacked((back_0, back_1), [v.shape for v in (w_gate, w_up, w_down)], (0, 0, 1), ffn_cuts)
    d_one, ffn_outs, gain_sums = tie(d_one, ffn_outs, gain_sums)
    d_attn_gain = gain_sums / gain_1
    d_q_gain = d_head_gains[0, :width] + d_head_gains[0, width:]
    gains = jnp.concatenate([d_attn_gain, d_ffn_gain, d_q_gain, d_head_gains[1, :width]])
    gains = sum_over_ctx(gains + swap_x(gains), 1, QUAD)
    d_x, _ = norm_back(x_own, scale_1, gain_1, d_one)
    d_tokens = d_h + d_x

    attn_grad, back_1 = tie(attn_grad, back_1)
    attn_back = home(attn_grad)
    attn_back, gains = tie(attn_back, gains)
    gains = sum_over_ctx(gains, QUAD, QUAD * n)
    attn_outs = unpacked(
        [attn_back],
        [v.shape for v in (w_query, key_projection, value_projection, w_out)],
        (0, 0, 0, 1),
        [(0, (1, 1))],
    )
    return (
        out_tokens,
        d_tokens,
        gains[:model],
        gains[model : 2 * model],
        gains[2 * model : 2 * model + width],
        gains[2 * model + width :],
        *attn_outs,
        *ffn_outs,
    )


def solution(mesh):
    return jax.shard_map(
        on_device,
        mesh=mesh,
        in_specs=(
            P(("ctx", "tp"), None),
            P(),
            P(),
            P(),
            P(),
            P("ctx", "tp"),
            P("ctx", "tp"),
            P("ctx", "tp"),
            P("tp", "ctx"),
            P("ctx", "tp"),
            P("ctx", "tp"),
            P("tp", "ctx"),
            P("ctx"),
            P(("ctx", "tp"), None),
        ),
        out_specs=(
            P(("ctx", "tp"), None),
            P(("ctx", "tp"), None),
            P(),
            P(),
            P(),
            P(),
            P("ctx", "tp"),
            P("ctx", "tp"),
            P("ctx", "tp"),
            P("tp", "ctx"),
            P("ctx", "tp"),
            P("ctx", "tp"),
            P("tp", "ctx"),
        ),
        check_vma=False,
    )
```
